32 devices in a mesh: dp: 16 (over z, x, core), mp: 2 (over y).
Axes of the slice: x: 2, y: 2, z: 4, core: 2. Of those that a mesh axis runs over, the one named last changes fastest.
Arguments:
- inputs: bfloat16 [32768, 768], P(('dp', 'mp')), may hold values from -12 to 12
- segments: int32 [32768], P('dp'), may hold values from -1 to 9, as said below
- w_qkv: bfloat16 [3, 768, 768], P(None, 'dp', 'mp'), may hold values from -0.21875 to 0.21875
- w_out: bfloat16 [768, 768], P('mp', 'dp'), may hold values from -4 to 4
- first_gain: bfloat16 [768], P('dp'), may hold values from 0.5 to 1.5
- first_bias: bfloat16 [768], P('dp'), may hold values from -3 to 3
- w_gate: bfloat16 [768, 3072], P('dp', 'mp'), may hold values from -0.21875 to 0.21875
- w_up: bfloat16 [768, 3072], P('dp', 'mp'), may hold values from -0.21875 to 0.21875
- w_down: bfloat16 [3072, 768], P('mp', 'dp'), may hold values from -0.109375 to 0.109375
- second_gain: bfloat16 [768], P('dp'), may hold values from 0.5 to 1.5
- second_bias: bfloat16 [768], P('dp'), may hold values from -3 to 3
- d_out: bfloat16 [32768, 768], P(('dp', 'mp')), may hold values from -12 to 12
Outputs:
- outputs: bfloat16 [32768, 768], P(('dp', 'mp'))
- grad_inputs: float32 [32768, 768], P(('dp', 'mp'))
- grad_w_qkv: float32 [3, 768, 768], P(None, 'dp', 'mp')
- grad_w_out: float32 [768, 768], P('mp', 'dp')
- grad_first_gain: float32 [768], P('dp')
- grad_first_bias: float32 [768], P('dp')
- grad_w_gate: float32 [768, 3072], P('dp', 'mp')
- grad_w_up: float32 [768, 3072], P('dp', 'mp')
- grad_w_down: float32 [3072, 768], P('mp', 'dp')
- grad_second_gain: float32 [768], P('dp')
- grad_second_bias: float32 [768], P('dp')
The draws below stay inside these ranges and needn't reach their ends.
Inputs may be any that keep to these rules, and one draw needn't show every extreme that they name: `segments`: within each sequence of 2048 tokens, tokens carry the number of their document, counting from 0 in order; each document has 200 to 2000 tokens; the tokens after the last whole document are padding, marked -1, and every sequence ends with one or more of them. In the first sequence every document has exactly 200 tokens.
All inputs are finite; a program needn't handle non-finite values.
Results may differ from the reference program's by a relative error of at most 0.017.
The reference program's roundings to bfloat16 on the way count: a program that leaves them out, or rounds other values in their place, can miss the bound.
Values may be sent and summed in bfloat16 or wider, within the bound.
A program may use at most 192 MiB of HBM per device.

```python
import jax
import jax.numpy as jnp
from jax import lax

D = 768
HEADS = 12
HEAD_DIM = 64
FF = 3072
SEQ_LEN = 2048
DOC_MIN = 200
DOC_MAX = 2000
TOKENS = 32768


def draw_segments(key, part):
    seq_count = TOKENS // SEQ_LEN
    most_docs = SEQ_LEN // DOC_MIN + 1
    lengths = jax.random.randint(key, (seq_count, most_docs), DOC_MIN, DOC_MAX + 1)
    first_row = (jnp.arange(seq_count) == 0)[:, None]
    lengths = jnp.where(first_row, DOC_MIN, lengths).astype(jnp.int32)
    doc_ends = jnp.cumsum(lengths, axis=1)
    positions = jnp.arange(SEQ_LEN)
    finished = jnp.sum((doc_ends[:, None, :] <= positions[None, :, None]).astype(jnp.int32), axis=2)
    complete = jnp.sum((doc_ends <= SEQ_LEN - 1).astype(jnp.int32), axis=1)
    labels = jnp.where(finished < complete[:, None], finished, -1)
    return labels.reshape(TOKENS).astype(jnp.int32)


def raised(values, own_key, source, target, parts, factor):
    owner, partner = [(jnp.arange(values.shape[position]) // (values.shape[position] // parts)).reshape([-1 if axis == position else 1 for axis in range(values.ndim)]) for position in (source, target)]
    chosen = jax.random.permutation(own_key, parts)[partner]
    strong = (owner == chosen) | (owner == (partner + parts // 2) % parts)
    return jnp.where(strong, factor * values, values)


def shard_levels(rng, shape, pieces, low, top_value):
    def one(axis_at, blocks):
        draws = jax.random.uniform(jax.random.fold_in(jax.random.fold_in(rng, 6), axis_at), (blocks,), jnp.float32, low / len(pieces), top_value / len(pieces))
        return jnp.repeat(jnp.exp(draws), shape[axis_at] // blocks).reshape((-1,) + (1,) * (len(shape) - axis_at - 1))

    gain = one(*pieces[0])
    for cut in pieces[1:]:
        gain = gain * one(*cut)
    return gain


def bell_draw(own_key, extent, width, limit, shards=(), kind=jnp.bfloat16):
    factor_of = shard_levels(own_key, extent, shards, -0.22, 0.18) if shards else 1.0
    entries = jax.random.normal(own_key, extent, jnp.float32) * width * factor_of
    return jnp.minimum(jnp.maximum(entries, -limit), limit).astype(kind)


def heavy_noise(own_key, shape, width, bound, shards, heavy, held_as=jnp.bfloat16):
    array = width * jax.random.normal(own_key, shape, jnp.float32)
    if shards:
        array = array * shard_levels(own_key, shape, shards, -0.22, 0.18)
    return jnp.clip(raised(array, jax.random.fold_in(own_key, 3), *heavy), -bound, bound).astype(held_as)


def setup_inputs(seed: int = 0) -> dict:
    splits = jax.random.split(jax.random.key(seed), 13)
    inputs = heavy_noise(splits[0], (TOKENS, D), 1.0, 12.0, ((0, 32),), (0, 1, 32, 2.75))
    segments = draw_segments(jax.random.fold_in(splits[12], 71), 0)
    w_qkv = bell_draw(splits[2], (3, D, D), D ** -0.5, 0.21875, ((1, 16), (2, 2)))
    w_out = bell_draw(splits[3], (D, D), 0.7, 4.0, ((0, 2), (1, 16)))
    first_gain = jnp.clip(1.0 + 0.1 * jax.random.normal(splits[4], (D,), jnp.float32), 0.5, 1.5).astype(jnp.bfloat16)
    first_bias = bell_draw(splits[5], (D,), 0.5, 3.0, ((0, 16),))
    w_gate = bell_draw(splits[6], (D, FF), D ** -0.5, 0.21875, ((0, 16), (1, 2)))
    w_up = bell_draw(splits[7], (D, FF), D ** -0.5, 0.21875, ((0, 16), (1, 2)))
    w_down = bell_draw(splits[8], (FF, D), FF ** -0.5, 0.109375, ((0, 2), (1, 16)))
    second_gain = jnp.clip(1.0 + 0.1 * jax.random.normal(splits[9], (D,), jnp.float32), 0.5, 1.5).astype(jnp.bfloat16)
    second_bias = bell_draw(splits[10], (D,), 0.5, 3.0, ((0, 16),))
    d_out = heavy_noise(splits[11], (TOKENS, D), 1.0, 12.0, ((0, 32),), (0, 1, 32, 2.75))
    return {"inputs": inputs, "segments": segments, "w_qkv": w_qkv, "w_out": w_out, "first_gain": first_gain, "first_bias": first_bias, "w_gate": w_gate, "w_up": w_up, "w_down": w_down, "second_gain": second_gain, "second_bias": second_bias, "d_out": d_out}


@jax.custom_vjp
def low(v):
    return lax.optimization_barrier(v.astype(jnp.bfloat16)).astype(jnp.float32)

@jax.custom_vjp
def low_back(v):
    return v

def low_keep(v):
    return (low(v), None)

def low_pass(kept, grad):
    return (grad,)

def back_keep(v):
    return (v, None)

def back_low(kept, grad):
    return (low(grad),)
low.defvjp(low_keep, low_pass)
low_back.defvjp(back_keep, back_low)
EPSILON = 1e-12
ROPE_BASE = 1000.0
MASKED = -10000.0

def rope_tables(seq_len, head_dim):
    half_dim = head_dim // 2
    frequency = ROPE_BASE ** (-2.0 * jnp.arange(half_dim, dtype=jnp.float32) / head_dim)
    angles = jnp.arange(seq_len, dtype=jnp.float32)[:, None] * frequency[None, :]
    return (jnp.cos(angles), jnp.sin(angles))

def rotate(values, cos_table, sin_table):
    half_dim = values.shape[-1] // 2
    front_half = values[..., :half_dim]
    back_half = values[..., half_dim:]
    return jnp.concatenate([front_half * cos_table - back_half * sin_table, back_half * cos_table + front_half * sin_table], axis=-1)

def layer_norm(hidden, norm_gain, norm_bias):
    centered = hidden - lax.optimization_barrier(jnp.mean(hidden, axis=-1, keepdims=True))
    inv_std = lax.rsqrt(lax.optimization_barrier(jnp.mean(centered * centered, axis=-1, keepdims=True)) + EPSILON)
    return centered * inv_std * norm_gain + norm_bias

def attend(operands):
    queries, key_rot, values, labels = operands
    scores = jnp.einsum('qhd,khd->hqk', queries, key_rot, precision=lax.Precision.HIGHEST) * HEAD_DIM ** (-0.5)
    scores = low_back(scores)
    allowed = (labels[:, None] == labels[None, :]) & (labels[:, None] >= 0)
    masked = jnp.where(allowed[None], scores, MASKED)
    row_max = lax.optimization_barrier(jnp.max(masked, axis=2, keepdims=True))
    exponent = jnp.exp(masked - row_max) * allowed.astype(jnp.float32)[None]
    row_sum = lax.optimization_barrier(jnp.sum(exponent, axis=2, keepdims=True))
    weights = low(exponent / jnp.maximum(row_sum, 1.0))
    return jnp.einsum('hqk,khd->qhd', weights, values, precision=lax.Precision.HIGHEST)

def reference(inputs, segments, w_qkv, w_out, first_gain, first_bias, w_gate, w_up, w_down, second_gain, second_bias, d_out):
    seq_count = TOKENS // SEQ_LEN
    labels = segments.reshape(seq_count, SEQ_LEN)
    cos_table, sin_table = rope_tables(SEQ_LEN, HEAD_DIM)
    cos_wide = cos_table[:, None, :]
    sin_wide = sin_table[:, None, :]
    highest = lax.Precision.HIGHEST
    head_shape = (seq_count, SEQ_LEN, HEADS, HEAD_DIM)

    def forward(tokens_in, qkv_w, out_w, gain_one, bias_one, gate_w, up_w, down_w, gain_two, bias_two):
        projected = jnp.einsum('td,kdc->ktc', tokens_in, qkv_w, precision=highest)
        queries = low_back(projected[0])
        key_rot = low_back(projected[1])
        values = low(low_back(projected[2]))
        queries = low(rotate(queries.reshape(head_shape), cos_wide, sin_wide))
        key_rot = low(rotate(key_rot.reshape(head_shape), cos_wide, sin_wide))
        attended = lax.map(jax.checkpoint(attend), (queries, key_rot, values.reshape(head_shape), labels))
        merged = low(low_back(attended.reshape(TOKENS, D)))
        branch = low_back(jnp.dot(merged, out_w, precision=highest))
        middle = layer_norm(tokens_in + branch, gain_one, bias_one)
        middle_low = low(middle)
        gate_act = low_back(jnp.dot(middle_low, gate_w, precision=highest))
        up_act = low_back(jnp.dot(middle_low, up_w, precision=highest))
        hidden = low(jax.nn.silu(gate_act) * up_act)
        mlp_out = low_back(jnp.dot(hidden, down_w, precision=highest))
        return layer_norm(middle + mlp_out, gain_two, bias_two)
    result, pullback = jax.vjp(forward, inputs.astype(jnp.float32), w_qkv.astype(jnp.float32), w_out.astype(jnp.float32), first_gain.astype(jnp.float32), first_bias.astype(jnp.float32), w_gate.astype(jnp.float32), w_up.astype(jnp.float32), w_down.astype(jnp.float32), second_gain.astype(jnp.float32), second_bias.astype(jnp.float32))
    gradients = pullback(d_out.astype(jnp.float32))
    return (result.astype(jnp.bfloat16), gradients[0], gradients[1], gradients[2], gradients[3], gradients[4], gradients[5], gradients[6], gradients[7], gradients[8], gradients[9])
```

```python
import functools

import jax
import jax.numpy as jnp
import numpy as np
from jax import lax
from jax.experimental import pallas as pl
from jax.experimental.pallas import tpu as pltpu
from jax.sharding import Mesh
from jax.sharding import PartitionSpec as P

HEAD_DIM = 64
SEQ_LEN = 2048
LANES = 128
EPSILON = 1e-12
ROPE_BASE = 1000.0
MASKED = -10000.0
SCALE = HEAD_DIM**-0.5
F32 = jnp.float32
BF16 = jnp.bfloat16
NT = (((1,), (1,)), ((), ()))
NN = (((1,), (0,)), ((), ()))
TN = (((0,), (0,)), ((), ()))
VMEM_BYTES = 56 << 20
FWD_Q, FWD_K = 1024, 512
BWD_Q, BWD_K = 1024, 512
ROW_BLOCK = 256


def dot(left, right, dims=NN):
    return lax.dot_general(left, right, dims, preferred_element_type=F32)


def rope_tables():
    half = HEAD_DIM // 2
    frequency = ROPE_BASE ** (-2.0 * np.arange(half) / HEAD_DIM)
    angles = np.arange(SEQ_LEN)[:, None] * frequency[None, :]
    cos, sin = np.cos(angles), np.sin(angles)
    heads = LANES // HEAD_DIM
    return (
        np.tile(np.concatenate([cos, cos], 1), (1, heads)).astype(np.float32),
        np.tile(np.concatenate([-sin, sin], 1), (1, heads)).astype(np.float32),
    )


def half_swap(tile):
    lane = lax.broadcasted_iota(jnp.int32, (1, LANES), 1)
    half = HEAD_DIM // 2
    return jnp.where(
        lane % HEAD_DIM < half,
        pltpu.roll(tile, LANES - half, 1),
        pltpu.roll(tile, half, 1),
    )


def project_kernel(core_ref, x_ref, w_ref, cos_ref, sin_ref, out_ref, *, pairs):
    x = x_ref[...]
    cos, sin = cos_ref[...], sin_ref[...]
    for pair in range(pairs):
        base = pair * 3 * LANES
        tile = dot(x, w_ref[:, base : base + 3 * LANES])
        for kind in range(2):
            part = tile[:, kind * LANES : (kind + 1) * LANES]
            out_ref[:, base + kind * LANES : base + (kind + 1) * LANES] = (
                part * cos + half_swap(part) * sin
            ).astype(BF16)
        out_ref[:, base + 2 * LANES : base + 3 * LANES] = tile[:, 2 * LANES :].astype(BF16)


def project(core, rows, weights, cos, sin):
    tokens, depth = rows.shape
    wide = weights.shape[1]
    steps = tokens // ROW_BLOCK

    def turned(step, core_ref):
        return (lax.rem(step + core_ref[0] * (steps // 2), steps), 0)

    return pl.pallas_call(
        functools.partial(project_kernel, pairs=wide // (3 * LANES)),
        grid_spec=pltpu.PrefetchScalarGridSpec(
            num_scalar_prefetch=1,
            grid=(steps,),
            in_specs=[
                pl.BlockSpec((ROW_BLOCK, depth), lambda i, c: (i, 0)),
                pl.BlockSpec((depth, wide), lambda i, c: (0, 0)),
                pl.BlockSpec((ROW_BLOCK, LANES), turned),
                pl.BlockSpec((ROW_BLOCK, LANES), turned),
            ],
            out_specs=pl.BlockSpec((ROW_BLOCK, wide), lambda i, c: (i, 0)),
        ),
        out_shape=jax.ShapeDtypeStruct((tokens, wide), BF16),
        compiler_params=pltpu.CompilerParams(vmem_limit_bytes=VMEM_BYTES),
        cost_estimate=pl.CostEstimate(
            flops=2 * tokens * depth * wide,
            bytes_accessed=2 * tokens * (depth + wide) + 2 * depth * wide,
            transcendentals=0,
        ),
        name="project",
    )(core, rows, weights, cos, sin)


def block_range(labels, block, other, turn):
    blocks = labels.shape[0] // block
    valid = labels >= 0
    tiles = labels.reshape(blocks, block)
    first, last = tiles[:, 0], jnp.max(tiles, axis=1)
    low = jnp.sum((valid[None] & (labels[None] < first[:, None])).astype(jnp.int32), 1)
    high = jnp.sum((valid[None] & (labels[None] <= last[:, None])).astype(jnp.int32), 1)
    offset = (labels.shape[0] - turn) // other
    return low // other + offset, jnp.where(high > low, (high + other - 1) // other, low // other) + offset


def attend_kernel(low_ref, high_ref, q_ref, k_ref, v_ref, key_ref, query_ref, o_ref, lse_ref, v_turned):
    tokens = q_ref.shape[0]
    key_blocks = tokens // FWD_K
    lane = lax.broadcasted_iota(jnp.int32, (1, LANES), 1)
    zero = jnp.zeros((), BF16)
    v_turned[...] = v_ref[...].T

    @pl.loop(0, tokens // FWD_Q)
    def _(i):
        q0 = pl.multiple_of(i * FWD_Q, FWD_Q)
        scaled = q_ref[pl.ds(q0, FWD_Q), :] * jnp.asarray(SCALE, BF16)
        halves = (
            jnp.where(lane < HEAD_DIM, scaled, zero),
            jnp.where(lane >= HEAD_DIM, scaled, zero),
        )
        query_label = query_ref[:, pl.ds(q0, FWD_Q)]

        def body(j, carry):
            k0 = pl.multiple_of(lax.rem(j, key_blocks) * FWD_K, FWD_K)
            k = k_ref[pl.ds(k0, FWD_K), :]
            same = key_ref[pl.ds(k0, FWD_K), :] == query_label
            scores = [dot(k, half, NT) for half in halves]
            out = []
            for h in range(2):
                top, total, acc = carry[h]
                s = jnp.where(same, scores[h], -1e30)
                new_top = jnp.maximum(top, jnp.max(s, axis=0, keepdims=True))
                fade = jnp.exp(top - new_top)
                e = jnp.exp(s - new_top)
                total = fade * total + jnp.sum(e, axis=0, keepdims=True)
                part = dot(v_turned[h * HEAD_DIM : (h + 1) * HEAD_DIM, pl.ds(k0, FWD_K)], e.astype(BF16))
                out.append((new_top, total, acc * fade + part))
            return tuple(out)

        start = (
            jnp.full((1, FWD_Q), MASKED, F32),
            jnp.zeros((1, FWD_Q), F32),
            jnp.zeros((HEAD_DIM, FWD_Q), F32),
        )
        ended = lax.fori_loop(low_ref[i], high_ref[i], body, (start, start))
        out = []
        for h in range(2):
            top, total, acc = ended[h]
            norm = jnp.maximum(total, 1.0)
            out.append(acc / norm)
            lse_ref[0, pl.ds(h, 1), pl.ds(q0, FWD_Q)] = top + jnp.log(norm)
        o_ref[pl.ds(q0, FWD_Q), :] = jnp.concatenate(out, 0).T.astype(BF16)


def attend(qkv, labels, turn):
    tokens = qkv.shape[0]
    pairs = qkv.shape[1] // (3 * LANES)
    low, high = block_range(labels, FWD_Q, FWD_K, turn)
    queries = jnp.where(labels < 0, -2, labels)
    whole = lambda shape: pl.BlockSpec(shape, lambda p, *_: (0,) * len(shape))
    part = lambda kind: pl.BlockSpec((tokens, LANES), lambda p, *_: (0, 3 * p + kind))
    return pl.pallas_call(
        attend_kernel,
        grid_spec=pltpu.PrefetchScalarGridSpec(
            num_scalar_prefetch=2,
            grid=(pairs,),
            in_specs=[part(0), part(1), part(2), whole((tokens, 1)), whole((1, tokens))],
            out_specs=[
                pl.BlockSpec((tokens, LANES), lambda p, *_: (0, p)),
                pl.BlockSpec((1, 2, tokens), lambda p, *_: (p, 0, 0)),
            ],
            scratch_shapes=[pltpu.VMEM((LANES, tokens), BF16)],
        ),
        out_shape=[
            jax.ShapeDtypeStruct((tokens, pairs * LANES), BF16),
            jax.ShapeDtypeStruct((pairs, 2, tokens), F32),
        ],
        compiler_params=pltpu.CompilerParams(vmem_limit_bytes=VMEM_BYTES),
        cost_estimate=pl.CostEstimate(
            flops=pairs * 8 * tokens * tokens * LANES,
            bytes_accessed=pairs * 4 * tokens * LANES * 2,
            transcendentals=pairs * 2 * tokens * tokens,
        ),
        name="attend",
    )(low, high, qkv, qkv, qkv, labels[:, None], queries[None])


def attend_back_kernel(
    low_ref,
    high_ref,
    q_ref,
    k_ref,
    v_ref,
    o_ref,
    do_ref,
    lse_ref,
    key_ref,
    query_ref,
    cos_ref,
    sin_ref,
    out_ref,
    dq_turned,
    inner,
    k_turned,
    *,
    turn_steps,
):
    tokens = q_ref.shape[0]
    query_blocks = tokens // BWD_Q
    lane = lax.broadcasted_iota(jnp.int32, (1, LANES), 1)
    zero = jnp.zeros((), BF16)
    picks = (lane < HEAD_DIM, lane >= HEAD_DIM)
    k_turned[...] = k_ref[...].T
    product = (o_ref[...].astype(F32) * do_ref[...].astype(F32)).T
    inner[0:1, :] = jnp.sum(product[:HEAD_DIM], axis=0, keepdims=True)
    inner[1:2, :] = jnp.sum(product[HEAD_DIM:], axis=0, keepdims=True)
    dq_turned[...] = jnp.zeros_like(dq_turned)

    def unrope(tile, row0, rows):
        cos, sin = cos_ref[pl.ds(row0, rows), :], sin_ref[pl.ds(row0, rows), :]
        return (tile * cos - half_swap(tile) * sin).astype(BF16)

    @pl.loop(0, tokens // BWD_K)
    def _(j):
        k0 = pl.multiple_of(j * BWD_K, BWD_K)
        key_label = key_ref[pl.ds(k0, BWD_K), :]
        dks, dvs = [], []
        for h in range(2):
            k = jnp.where(picks[h], k_ref[pl.ds(k0, BWD_K), :], zero)
            v = jnp.where(picks[h], v_ref[pl.ds(k0, BWD_K), :], zero)
            kt = k_turned[pl.ds(h * HEAD_DIM, HEAD_DIM), pl.ds(k0, BWD_K)]

            def body(i, carry):
                dk, dv = carry
                q0 = pl.multiple_of(lax.rem(i, query_blocks) * BWD_Q, BWD_Q)
                q = q_ref[pl.ds(q0, BWD_Q), :]
                do = do_ref[pl.ds(q0, BWD_Q), :]
                s = dot(k, q, NT)
                p = jnp.exp(s * SCALE - lse_ref[0, pl.ds(h, 1), pl.ds(q0, BWD_Q)])
                p = jnp.where(key_label == query_ref[:, pl.ds(q0, BWD_Q)], p, 0.0)
                dp = dot(v, do, NT)
                ds = (p * (dp - inner[pl.ds(h, 1), pl.ds(q0, BWD_Q)])).astype(BF16)
                dv = dv + dot(p.astype(BF16), do)
                dk = dk + dot(ds, q)
                dq_turned[pl.ds(h * HEAD_DIM, HEAD_DIM), pl.ds(q0, BWD_Q)] += dot(kt, ds)
                return dk, dv

            empty = jnp.zeros((BWD_K, LANES), F32)
            dk, dv = lax.fori_loop(low_ref[j], high_ref[j], body, (empty, empty))
            dks.append(dk)
            dvs.append(dv)
        dk = jnp.where(picks[0], dks[0], dks[1]) * SCALE
        out_ref[pl.ds(k0, BWD_K), LANES : 2 * LANES] = unrope(dk, k0, BWD_K)
        out_ref[pl.ds(k0, BWD_K), 2 * LANES :] = jnp.where(picks[0], dvs[0], dvs[1]).astype(BF16)

    out_ref[:, :LANES] = unrope(dq_turned[...].T * SCALE, 0, tokens)


def attend_back(pair, qkv, o, do, lse, labels, turn, cos, sin):
    tokens = qkv.shape[0]
    low, high = block_range(labels, BWD_K, BWD_Q, turn)
    queries = jnp.where(labels < 0, -2, labels)
    whole = lambda shape: pl.BlockSpec(shape, lambda g, *_: (0,) * len(shape))
    part = lambda kind: pl.BlockSpec((tokens, LANES), lambda g, *_: (0, 3 * pair + kind))
    own = pl.BlockSpec((tokens, LANES), lambda g, *_: (0, pair))
    return pl.pallas_call(
        functools.partial(attend_back_kernel, turn_steps=0),
        grid_spec=pltpu.PrefetchScalarGridSpec(
            num_scalar_prefetch=2,
            grid=(1,),
            in_specs=[
                part(0),
                part(1),
                part(2),
                own,
                own,
                pl.BlockSpec((1, 2, tokens), lambda g, *_: (pair, 0, 0)),
                whole((tokens, 1)),
                whole((1, tokens)),
                whole((tokens, LANES)),
                whole((tokens, LANES)),
            ],
            out_specs=whole((tokens, 3 * LANES)),
            scratch_shapes=[
                pltpu.VMEM((LANES, tokens), F32),
                pltpu.VMEM((8, tokens), F32),
                pltpu.VMEM((LANES, tokens), BF16),
            ],
        ),
        out_shape=jax.ShapeDtypeStruct((tokens, 3 * LANES), BF16),
        compiler_params=pltpu.CompilerParams(vmem_limit_bytes=VMEM_BYTES),
        cost_estimate=pl.CostEstimate(
            flops=20 * tokens * tokens * LANES,
            bytes_accessed=8 * tokens * LANES * 2,
            transcendentals=2 * tokens * tokens,
        ),
        name="attend_back",
    )(low, high, qkv, qkv, qkv, o, do, lse, labels[:, None], queries[None], cos, sin)


def norm_forward(hidden, gain, bias):
    centered = hidden - jnp.mean(hidden, axis=-1, keepdims=True)
    inv_std = lax.rsqrt(jnp.mean(centered * centered, axis=-1, keepdims=True) + EPSILON)
    normed = centered * inv_std
    return normed * gain + bias, normed, inv_std


def norm_back(grad_y, normed, inv_std, gain):
    grad_gain = jnp.sum(grad_y * normed, axis=0)
    grad_bias = jnp.sum(grad_y, axis=0)
    scaled = grad_y * gain
    grad_h = inv_std * (
        scaled
        - jnp.mean(scaled, axis=-1, keepdims=True)
        - normed * jnp.mean(scaled * normed, axis=-1, keepdims=True)
    )
    return grad_h, grad_gain, grad_bias


def on_device(
    mp,
    inputs,
    segments,
    w_qkv,
    w_out,
    first_gain,
    first_bias,
    w_gate,
    w_up,
    w_down,
    second_gain,
    second_bias,
    d_out,
):
    group = ("chip", "mp")
    crossing = [(a * mp + b, b * mp + a) for a in range(2) for b in range(mp)]

    def cross(tensor):
        return lax.ppermute(tensor, ("core", "mp"), crossing)

    def mate(tensor):
        return lax.ppermute(tensor, "core", [(0, 1), (1, 0)])

    core = lax.axis_index("core")
    shard, half_cols = w_qkv.shape[1], w_qkv.shape[2]
    pairs = half_cols // LANES
    width = inputs.shape[1]
    half_ff = w_gate.shape[1]
    half_len = inputs.shape[0]
    turn = core * half_len

    vectors = jnp.stack([first_gain, first_bias, second_gain, second_bias], axis=1)
    pad = jnp.zeros((shard, LANES - 4), BF16)
    attn_shard = jnp.concatenate(
        [
            w_qkv.reshape(3, shard, pairs, LANES).transpose(1, 2, 0, 3).reshape(shard, 3 * half_cols),
            w_out.T,
            vectors,
            pad,
        ],
        axis=1,
    )
    ff_shard = jnp.concatenate([w_gate, w_up, w_down.T], axis=1)
    attn_w = lax.all_gather(cross(attn_shard), group, axis=0, tiled=True)
    rows_own = cross(inputs)
    labels = cross(segments)
    ff_own = lax.all_gather(cross(ff_shard), group, axis=0, tiled=True)
    ff_mate = mate(ff_own)
    d_own = cross(d_out)

    rows_all = jnp.concatenate([rows_own, mate(rows_own)], axis=0)
    labels = jnp.where(core == 0, labels, jnp.roll(labels, half_len))
    qkv_w = attn_w[:, : 3 * half_cols]
    out_own = attn_w[:, 3 * half_cols : 4 * half_cols]
    out_mate = mate(out_own)
    gains = attn_w[:, 4 * half_cols : 4 * half_cols + 4].astype(F32).T
    gain_one, bias_one, gain_two, bias_two = gains[0], gains[1], gains[2], gains[3]
    cos, sin = (jnp.asarray(t) for t in rope_tables())

    qkv = project(core.reshape(1), rows_all, qkv_w, cos, sin)
    o, lse = attend(qkv, labels, turn)
    o_in = mate(o[half_len:])
    attn = dot(o[:half_len], out_own, NT) + dot(o_in, out_mate, NT)
    middle, first_hat, first_inv = norm_forward(rows_own.astype(F32) + attn, gain_one, bias_one)
    middle_low = middle.astype(BF16)

    saved = []
    mlp = None
    for block in (ff_own, ff_mate):
        gate_w, up_w, down_t = (block[:, k * half_ff : (k + 1) * half_ff] for k in range(3))
        gate = dot(middle_low, gate_w)
        up = dot(middle_low, up_w)
        sig = jax.nn.sigmoid(gate)
        silu = gate * sig
        hidden = (silu * up).astype(BF16)
        part = dot(hidden, down_t, NT)
        mlp = part if mlp is None else mlp + part
        saved.append((gate_w, up_w, down_t, gate, up, sig, silu, hidden))
    result, second_hat, second_inv = norm_forward(middle + mlp, gain_two, bias_two)
    outputs = cross(result.astype(BF16))
    grad_two, second_gain_part, second_bias_part = norm_back(
        d_own.astype(F32), second_hat, second_inv, gain_two
    )
    grad_two_low = grad_two.astype(BF16)
    grad_middle = grad_two
    grads = []
    for gate_w, up_w, down_t, gate, up, sig, silu, hidden in saved:
        grad_down_t = dot(grad_two_low, hidden, TN)
        grad_hidden = dot(grad_two_low, down_t)
        grad_gate = (grad_hidden * up * sig * (1.0 + gate * (1.0 - sig))).astype(BF16)
        grad_up = (grad_hidden * silu).astype(BF16)
        grads.append((dot(middle_low, grad_gate, TN), dot(middle_low, grad_up, TN), grad_down_t))
        grad_middle = grad_middle + dot(grad_gate, gate_w, NT) + dot(grad_up, up_w, NT)
    grad_one, first_gain_part, first_bias_part = norm_back(grad_middle, first_hat, first_inv, gain_one)
    sums = jnp.stack([first_gain_part, first_bias_part, second_gain_part, second_bias_part], axis=1)
    sums = jnp.concatenate([sums, jnp.zeros((width, LANES - 4), F32)], axis=1)
    ff_grad = jnp.concatenate([*grads[0], sums], axis=1)
    ff_sent = mate(jnp.concatenate([*grads[1], sums], axis=1).astype(BF16))
    ff_grad = (ff_grad + ff_sent.astype(F32)).astype(BF16)
    ff_grad = cross(lax.psum_scatter(ff_grad, group, scatter_dimension=0, tiled=True)).astype(F32)

    grad_one_low = grad_one.astype(BF16)
    grad_one_all = jnp.concatenate([grad_one_low, mate(grad_one_low)], axis=0)
    grad_one_home = cross(grad_one)
    do = dot(grad_one_all, out_own).astype(BF16)
    grad_out_t = dot(grad_one_all, o, TN).astype(BF16)
    cos_turned, sin_turned = (
        jnp.where(core == 0, t, jnp.roll(t, half_len, axis=0)) for t in (cos, sin)
    )
    grad_rows = None
    weight_grads = []
    for pair in range(pairs):
        back = attend_back(pair, qkv, o, do, lse, labels, turn, cos_turned, sin_turned)
        weight_grads.append(dot(rows_all, back, TN).astype(BF16))
        part = dot(back, qkv_w[:, pair * 3 * LANES : (pair + 1) * 3 * LANES], NT)
        grad_rows = part if grad_rows is None else grad_rows + part
    grad_rows = grad_rows[:half_len] + mate(grad_rows[half_len:].astype(BF16)).astype(F32)
    grad_inputs = grad_one_home + cross(grad_rows.astype(BF16)).astype(F32)
    attn_grad = jnp.concatenate([*weight_grads, grad_out_t], axis=1)
    attn_grad = cross(lax.psum_scatter(attn_grad, group, scatter_dimension=0, tiled=True)).astype(F32)

    grad_qkv = (
        attn_grad[:, : 3 * half_cols]
        .reshape(shard, pairs, 3, LANES)
        .transpose(2, 0, 1, 3)
        .reshape(3, shard, half_cols)
    )
    grad_out = attn_grad[:, 3 * half_cols :].T
    grad_gate, grad_up, grad_down_t = (ff_grad[:, k * half_ff : (k + 1) * half_ff] for k in range(3))
    grad_vectors = ff_grad[:, 3 * half_ff : 3 * half_ff + 4]
    return (
        outputs,
        grad_inputs,
        grad_qkv,
        grad_out,
        grad_vectors[:, 0],
        grad_vectors[:, 1],
        grad_gate,
        grad_up,
        grad_down_t.T,
        grad_vectors[:, 2],
        grad_vectors[:, 3],
    )


def solution(mesh):
    dp, mp = mesh.shape["dp"], mesh.shape["mp"]
    split = Mesh(mesh.devices.reshape(dp // 2, 2, mp), ("chip", "core", "mp"))
    rows = P(("chip", "core", "mp"), None)
    vector = P(("chip", "core"))
    columns = P(("chip", "core"), "mp")
    turned = P("mp", ("chip", "core"))
    stacked = P(None, ("chip", "core"), "mp")
    return jax.shard_map(
        functools.partial(on_device, mp),
        mesh=split,
        in_specs=(
            rows,
            vector,
            stacked,
            turned,
            vector,
            vector,
            columns,
            columns,
            turned,
            vector,
            vector,
            rows,
        ),
        out_specs=(
            rows,
            rows,
            stacked,
            turned,
            vector,
            vector,
            columns,
            columns,
            turned,
            vector,
            vector,
        ),
        check_vma=False,
    )
```

```python
import functools

import jax
import jax.numpy as jnp
import numpy as np
from jax import lax
from jax.experimental import pallas as pl
from jax.experimental.pallas import tpu as pltpu
from jax.sharding import Mesh
from jax.sharding import PartitionSpec as P

HEAD_DIM = 64
SEQ_LEN = 2048
LANES = 128
EPSILON = 1e-12
ROPE_BASE = 1000.0
MASKED = -10000.0
SCALE = HEAD_DIM**-0.5
F32 = jnp.float32
BF16 = jnp.bfloat16
NT = (((1,), (1,)), ((), ()))
NN = (((1,), (0,)), ((), ()))
TN = (((0,), (0,)), ((), ()))
VMEM_BYTES = 60 << 20
FWD_Q, FWD_K = 1024, 512
BWD_Q, BWD_K = 1024, 512
ROW_BLOCK = 256
MESH_ID = pl.DeviceIdType.MESH
LINE = 4


def dot(left, right, dims=NN):
    return lax.dot_general(left, right, dims, preferred_element_type=F32)


def rope_tables():
    half = HEAD_DIM // 2
    frequency = ROPE_BASE ** (-2.0 * np.arange(half) / HEAD_DIM)
    angles = np.arange(SEQ_LEN)[:, None] * frequency[None, :]
    cos, sin = np.cos(angles), np.sin(angles)
    heads = LANES // HEAD_DIM
    return (
        np.tile(np.concatenate([cos, cos], 1), (1, heads)).astype(np.float32),
        np.tile(np.concatenate([-sin, sin], 1), (1, heads)).astype(np.float32),
    )


def half_swap(tile):
    lane = lax.broadcasted_iota(jnp.int32, (1, LANES), 1)
    half = HEAD_DIM // 2
    return jnp.where(
        lane % HEAD_DIM < half,
        pltpu.roll(tile, LANES - half, 1),
        pltpu.roll(tile, half, 1),
    )


def project_kernel(core_ref, x_ref, w_ref, cos_ref, sin_ref, out_ref, *, pairs):
    x = x_ref[...]
    cos, sin = cos_ref[...], sin_ref[...]
    for pair in range(pairs):
        base = pair * 3 * LANES
        tile = dot(x, w_ref[0, :, base : base + 3 * LANES])
        for kind in range(2):
            part = tile[:, kind * LANES : (kind + 1) * LANES]
            out_ref[:, base + kind * LANES : base + (kind + 1) * LANES] = (
                part * cos + half_swap(part) * sin
            ).astype(BF16)
        out_ref[:, base + 2 * LANES : base + 3 * LANES] = tile[:, 2 * LANES :].astype(BF16)


def project(core, rows, weights, cos, sin):
    tokens, depth = rows.shape
    wide = weights.shape[2] // (4 * LANES) * 3 * LANES
    steps = tokens // ROW_BLOCK

    def turned(step, core_ref):
        return (lax.rem(step + core_ref[0] * (steps // 2), steps), 0)

    return pl.pallas_call(
        functools.partial(project_kernel, pairs=wide // (3 * LANES)),
        grid_spec=pltpu.PrefetchScalarGridSpec(
            num_scalar_prefetch=1,
            grid=(steps,),
            in_specs=[
                pl.BlockSpec((ROW_BLOCK, depth), lambda i, c: (i, 0)),
                pl.BlockSpec((1, depth, wide), lambda i, c: (c[0], 0, 0)),
                pl.BlockSpec((ROW_BLOCK, LANES), turned),
                pl.BlockSpec((ROW_BLOCK, LANES), turned),
            ],
            out_specs=pl.BlockSpec((ROW_BLOCK, wide), lambda i, c: (i, 0)),
        ),
        out_shape=jax.ShapeDtypeStruct((tokens, wide), BF16),
        compiler_params=pltpu.CompilerParams(vmem_limit_bytes=VMEM_BYTES),
        cost_estimate=pl.CostEstimate(
            flops=2 * tokens * depth * wide,
            bytes_accessed=2 * tokens * (depth + wide) + 2 * depth * wide,
            transcendentals=0,
        ),
        name="project",
    )(core, rows, weights, cos, sin)


def block_range(labels, block, other, turn):
    blocks = labels.shape[0] // block
    valid = labels >= 0
    tiles = labels.reshape(blocks, block)
    first, last = tiles[:, 0], jnp.max(tiles, axis=1)
    low = jnp.sum((valid[None] & (labels[None] < first[:, None])).astype(jnp.int32), 1)
    high = jnp.sum((valid[None] & (labels[None] <= last[:, None])).astype(jnp.int32), 1)
    offset = (labels.shape[0] - turn) // other
    return low // other + offset, jnp.where(high > low, (high + other - 1) // other, low // other) + offset


def attend_kernel(low_ref, high_ref, q_ref, k_ref, v_ref, key_ref, query_ref, o_ref, lse_ref, v_turned):
    tokens = q_ref.shape[0]
    key_blocks = tokens // FWD_K
    lane = lax.broadcasted_iota(jnp.int32, (1, LANES), 1)
    zero = jnp.zeros((), BF16)
    v_turned[...] = v_ref[...].T

    @pl.loop(0, tokens // FWD_Q)
    def _(i):
        q0 = pl.multiple_of(i * FWD_Q, FWD_Q)
        scaled = q_ref[pl.ds(q0, FWD_Q), :] * jnp.asarray(SCALE, BF16)
        halves = (
            jnp.where(lane < HEAD_DIM, scaled, zero),
            jnp.where(lane >= HEAD_DIM, scaled, zero),
        )
        query_label = query_ref[:, pl.ds(q0, FWD_Q)]

        def body(j, carry):
            k0 = pl.multiple_of(lax.rem(j, key_blocks) * FWD_K, FWD_K)
            k = k_ref[pl.ds(k0, FWD_K), :]
            same = key_ref[pl.ds(k0, FWD_K), :] == query_label
            scores = [dot(k, half, NT) for half in halves]
            out = []
            for h in range(2):
                top, total, acc = carry[h]
                s = jnp.where(same, scores[h], -1e30)
                new_top = jnp.maximum(top, jnp.max(s, axis=0, keepdims=True))
                fade = jnp.exp(top - new_top)
                e = jnp.exp(s - new_top)
                total = fade * total + jnp.sum(e, axis=0, keepdims=True)
                part = dot(v_turned[h * HEAD_DIM : (h + 1) * HEAD_DIM, pl.ds(k0, FWD_K)], e.astype(BF16))
                out.append((new_top, total, acc * fade + part))
            return tuple(out)

        start = (
            jnp.full((1, FWD_Q), MASKED, F32),
            jnp.zeros((1, FWD_Q), F32),
            jnp.zeros((HEAD_DIM, FWD_Q), F32),
        )
        ended = lax.fori_loop(low_ref[i], high_ref[i], body, (start, start))
        out = []
        for h in range(2):
            top, total, acc = ended[h]
            norm = jnp.maximum(total, 1.0)
            out.append(acc / norm)
            lse_ref[0, pl.ds(h, 1), pl.ds(q0, FWD_Q)] = top + jnp.log(norm)
        o_ref[pl.ds(q0, FWD_Q), :] = jnp.concatenate(out, 0).T.astype(BF16)


def attend(qkv, labels, turn):
    tokens = qkv.shape[0]
    pairs = qkv.shape[1] // (3 * LANES)
    low, high = block_range(labels, FWD_Q, FWD_K, turn)
    queries = jnp.where(labels < 0, -2, labels)
    whole = lambda shape: pl.BlockSpec(shape, lambda p, *_: (0,) * len(shape))
    part = lambda kind: pl.BlockSpec((tokens, LANES), lambda p, *_: (0, 3 * p + kind))
    return pl.pallas_call(
        attend_kernel,
        grid_spec=pltpu.PrefetchScalarGridSpec(
            num_scalar_prefetch=2,
            grid=(pairs,),
            in_specs=[part(0), part(1), part(2), whole((tokens, 1)), whole((1, tokens))],
            out_specs=[
                pl.BlockSpec((tokens, LANES), lambda p, *_: (0, p)),
                pl.BlockSpec((1, 2, tokens), lambda p, *_: (p, 0, 0)),
            ],
            scratch_shapes=[pltpu.VMEM((LANES, tokens), BF16)],
        ),
        out_shape=[
            jax.ShapeDtypeStruct((tokens, pairs * LANES), BF16),
            jax.ShapeDtypeStruct((pairs, 2, tokens), F32),
        ],
        compiler_params=pltpu.CompilerParams(vmem_limit_bytes=VMEM_BYTES),
        cost_estimate=pl.CostEstimate(
            flops=pairs * 8 * tokens * tokens * LANES,
            bytes_accessed=pairs * 4 * tokens * LANES * 2,
            transcendentals=pairs * 2 * tokens * tokens,
        ),
        name="attend",
    )(low, high, qkv, qkv, qkv, labels[:, None], queries[None])


def attend_back_step(t, refs, scratch):
    q_all, o_all, do_all, lse_ref, key_ref, query_ref, cos_ref, sin_ref, out_ref = refs
    dq_turned, inner, k_turned = scratch
    tokens = q_all.shape[0]
    blocks = tokens // BWD_K
    pair, j = t // blocks, lax.rem(t, blocks)
    lane = lax.broadcasted_iota(jnp.int32, (1, LANES), 1)
    zero = jnp.zeros((), BF16)
    picks = (lane < HEAD_DIM, lane >= HEAD_DIM)

    def lanes(kind):
        return pl.ds(pl.multiple_of((pair * 3 + kind) * LANES, LANES), LANES)

    own = pl.ds(pl.multiple_of(pair * LANES, LANES), LANES)

    def unrope(tile, rows):
        return (tile * cos_ref[rows, :] - half_swap(tile) * sin_ref[rows, :]).astype(BF16)

    @pl.when(j == 0)
    def _():
        k_turned[...] = q_all[:, lanes(1)].T
        product = (o_all[:, own].astype(F32) * do_all[:, own].astype(F32)).T
        inner[0:1, :] = jnp.sum(product[:HEAD_DIM], axis=0, keepdims=True)
        inner[1:2, :] = jnp.sum(product[HEAD_DIM:], axis=0, keepdims=True)
        dq_turned[...] = jnp.zeros_like(dq_turned)

    key_rows = pl.ds(pl.multiple_of(j * BWD_K, BWD_K), BWD_K)
    key_label = key_ref[key_rows, :]
    dks, dvs = [], []
    for h in range(2):
        k = jnp.where(picks[h], q_all[key_rows, lanes(1)], zero)
        v = jnp.where(picks[h], q_all[key_rows, lanes(2)], zero)
        kt = k_turned[pl.ds(h * HEAD_DIM, HEAD_DIM), key_rows]

        def body(i, carry):
            dk, dv = carry
            query_rows = pl.ds(pl.multiple_of(i * BWD_Q, BWD_Q), BWD_Q)
            q = q_all[query_rows, lanes(0)]
            do = do_all[query_rows, own]
            s = dot(k, q, NT)
            p = jnp.exp(s * SCALE - lse_ref[pair, pl.ds(h, 1), query_rows])
            p = jnp.where(key_label == query_ref[:, query_rows], p, 0.0)
            dp = dot(v, do, NT)
            ds = (p * (dp - inner[pl.ds(h, 1), query_rows])).astype(BF16)
            dv = dv + dot(p.astype(BF16), do)
            dk = dk + dot(ds, q)
            dq_turned[pl.ds(h * HEAD_DIM, HEAD_DIM), query_rows] += dot(kt, ds)
            return dk, dv

        empty = jnp.zeros((BWD_K, LANES), F32)
        dk, dv = lax.fori_loop(0, tokens // BWD_Q, body, (empty, empty))
        dks.append(dk)
        dvs.append(dv)
    out_ref[key_rows, lanes(1)] = unrope(jnp.where(picks[0], dks[0], dks[1]) * SCALE, key_rows)
    out_ref[key_rows, lanes(2)] = jnp.where(picks[0], dvs[0], dvs[1]).astype(BF16)

    @pl.when(j == blocks - 1)
    def _():
        out_ref[:, lanes(0)] = unrope(dq_turned[...].T * SCALE, pl.ds(0, tokens))


def attend_back_kernel(*refs, remote):
    refs, steps = list(refs), refs[0].shape[0] // BWD_K * (refs[0].shape[1] // (3 * LANES))
    inputs, refs = refs[:8], refs[8:]
    if not remote:
        out_ref, scratch = refs[0], refs[1:]

        @pl.loop(0, steps)
        def _(t):
            attend_back_step(t, (*inputs, out_ref), scratch)

        return
    grads, out_ref, sums, scratch = refs[0], refs[1], refs[2], refs[3:]
    greet(False)
    reduce = Reduce(grads, sums, scratch[3:])
    reduce.begin()

    @pl.loop(0, max(steps, reduce.STEPS))
    def _(t):
        reduce.step(t)

        @pl.when(t < steps)
        def _():
            attend_back_step(t, (*inputs, out_ref), scratch[:3])

    reduce.end()


def attend_back(qkv, o, do, lse, labels, cos, sin, grads, devices, collective_id):
    tokens, wide = qkv.shape
    remote = devices == 8 * LINE
    queries = jnp.where(labels < 0, -2, labels)
    vmem = pl.BlockSpec(memory_space=pltpu.VMEM)
    operands = [qkv, o, do, lse, labels[:, None], queries[None], cos, sin]
    out_shape = [jax.ShapeDtypeStruct((tokens, wide), BF16)]
    scratch = [
        pltpu.VMEM((LANES, tokens), F32),
        pltpu.VMEM((8, tokens), F32),
        pltpu.VMEM((LANES, tokens), BF16),
    ]
    in_specs = [vmem] * 8
    params = dict(vmem_limit_bytes=VMEM_BYTES)
    if remote:
        rows, width = 2 * grads.shape[1] // devices, grads.shape[2]
        operands.append(grads)
        in_specs.append(pl.BlockSpec(memory_space=pl.ANY))
        out_shape.append(jax.ShapeDtypeStruct((rows, width), F32))
        scratch += Reduce.scratch(rows, width)
        params.update(collective_id=collective_id, has_side_effects=True)
    out = pl.pallas_call(
        functools.partial(attend_back_kernel, remote=remote),
        in_specs=in_specs,
        out_specs=[vmem] * len(out_shape),
        out_shape=out_shape,
        scratch_shapes=scratch,
        compiler_params=pltpu.CompilerParams(**params),
        cost_estimate=pl.CostEstimate(
            flops=wide // (3 * LANES) * 20 * tokens * tokens * LANES,
            bytes_accessed=8 * tokens * wide,
            transcendentals=wide // (3 * LANES) * 2 * tokens * tokens,
        ),
        name="attend_back",
    )(*operands)
    return (out[0], out[1]) if remote else (out[0], scatter_sum(grads))


def scatter_sum(grads):
    flat = grads.reshape(-1, grads.shape[2])
    return lax.psum_scatter(flat, ("mp", "chip", "core"), scatter_dimension=0, tiled=True).astype(F32)


def place():
    chip = lax.axis_index("chip")
    return chip // 2, lax.rem(chip, 2), lax.axis_index("core"), lax.axis_index("mp")


def target(a, b, core, y):
    return {"chip": a * 2 + b, "core": core, "mp": y}


def greet(moves):
    a, b, core, y = place()
    barrier = pltpu.get_barrier_semaphore()

    def signal(device):
        pl.semaphore_signal(barrier, inc=1, device_id=device, device_id_type=MESH_ID)

    signal(target(a, 1 - b, core, y))
    signal(target(a, b, core, 1 - y))
    signal(target(a, b, 1 - core, y))

    @pl.when(a > 0)
    def _():
        signal(target(a - 1, b, core, y))

    @pl.when(a < LINE - 1)
    def _():
        signal(target(a + 1, b, core, y))

    @pl.when(moves)
    def _():
        signal(target(a, b, y, core))

    edges = jnp.where(a > 0, 1, 0) + jnp.where(a < LINE - 1, 1, 0) + jnp.where(moves, 1, 0)
    pl.semaphore_wait(barrier, 3 + edges)


class Gather:
    def __init__(self, src, dst, send, recv, local):
        self.src, self.dst, self.send, self.recv, self.local = src, dst, send, recv, local
        self.rows, self.width = src.shape
        tiles = self.width // LANES
        first = (tiles + 1) // 2 * LANES
        self.columns = [(0, first), (first, self.width - first)]
        self.a, self.b, self.core, self.y = place()

    def span(self, half):
        start, size = (0, self.width) if half is None else self.columns[half]
        return pl.ds(start, size)

    def at(self, piece, core=None):
        pa, pb, py, half = piece
        core = self.core if core is None else core
        row = pl.multiple_of(((pa * 2 + pb) * 2 + core) * self.rows, self.rows)
        return self.dst.at[py, pl.ds(row, self.rows), self.span(half)]

    def own_copy(self):
        return pltpu.make_async_copy(self.src, self.at((self.a, self.b, self.y, None)), self.local)

    def start(self, piece, slot, device, mine=False):
        source = self.src.at[:, self.span(piece[3])] if mine else self.at(piece)
        pltpu.make_async_remote_copy(
            source, self.at(piece), self.send.at[slot], self.recv.at[slot], device_id=device, device_id_type=MESH_ID
        ).start()

    def handle(self, piece, slot, core=None):
        ref = self.at(piece, core)
        return pltpu.make_async_remote_copy(
            ref,
            ref,
            self.send.at[slot],
            self.recv.at[slot],
            device_id=target(self.a, self.b, 1 - self.core, self.y),
            device_id_type=MESH_ID,
        )

    def arrived(self, piece, slot, core=None):
        self.handle(piece, slot, core).wait_recv()

    def sent(self, piece, slot):
        self.handle(piece, slot).wait_send()

    def to_x(self, piece, slot, mine=False):
        self.start(piece, slot, target(self.a, 1 - self.b, self.core, self.y), mine)

    def to_y(self, piece, slot, mine=False):
        self.start(piece, slot, target(self.a, self.b, self.core, 1 - self.y), mine)

    def to_mate(self, piece, slot, mine=False):
        self.start(piece, slot, target(self.a, self.b, 1 - self.core, self.y), mine)

    def to_line(self, piece, slot, step, mine=False):
        self.start(piece, slot, target(self.a + step, self.b, self.core, self.y), mine)

    def spread(self, pa, rank, mine=False):
        b, y = self.b, self.y
        self.to_x((pa, b, y, 0), 6 + rank, mine)
        self.to_y((pa, b, y, 1), 18 + rank, mine)
        for half in range(2):
            self.to_mate((pa, b, y, half), 30 + 2 * rank + half, mine)
        self.to_y((pa, b, y, 0), 22 + rank, mine)
        self.to_x((pa, b, y, 1), 10 + rank, mine)

    def begin(self):
        a, b, y = self.a, self.b, self.y
        piece = (a, b, y, None)

        @pl.when(a < LINE - 1)
        def _():
            self.to_line(piece, 0, 1, True)

        @pl.when(a > 0)
        def _():
            self.to_line(piece, 3, -1, True)

        self.spread(a, 0, True)
        self.own_copy().start()

    def hop(self, h):
        a, b, y = self.a, self.b, self.y

        @pl.when(a - h >= 0)
        def _():
            self.arrived((a - h, b, y, None), h - 1)
            if h < LINE - 1:

                @pl.when(a < LINE - 1)
                def _():
                    self.to_line((a - h, b, y, None), h, 1)

            self.spread(a - h, LINE - h)

        @pl.when(a + h < LINE)
        def _():
            self.arrived((a + h, b, y, None), 2 + h)
            if h < LINE - 1:

                @pl.when(a > 0)
                def _():
                    self.to_line((a + h, b, y, None), 3 + h, -1)

            self.spread(a + h, h)

    def ranks(self):
        return [(rank, lax.rem(self.a + rank, LINE)) for rank in range(LINE)]

    def turn(self):
        b, y = self.b, self.y
        for rank, pa in self.ranks():
            self.arrived((pa, 1 - b, y, 0), 6 + rank)
            self.to_y((pa, 1 - b, y, 0), 26 + rank)
            self.to_mate((pa, 1 - b, y, 0), 38 + rank)
            self.arrived((pa, b, 1 - y, 1), 18 + rank)
            self.to_x((pa, b, 1 - y, 1), 14 + rank)
            self.to_mate((pa, b, 1 - y, 1), 42 + rank)

    def last(self):
        b, y = self.b, self.y
        for rank, pa in self.ranks():
            for far in range(2):
                pb, py = (b, 1 - b)[far], (y, 1 - y)[far]
                self.arrived((pa, pb, 1 - y, 0), 22 + 4 * far + rank)
                self.to_mate((pa, pb, 1 - y, 0), 46 + 4 * far + rank)
                self.arrived((pa, 1 - b, py, 1), 10 + 4 * far + rank)
                self.to_mate((pa, 1 - b, py, 1), 54 + 4 * far + rank)

    def end(self):
        a, b, y = self.a, self.b, self.y
        other = 1 - self.core
        for rank, pa in self.ranks():
            pieces = [((pa, b, y, 0), 30 + 2 * rank), ((pa, b, y, 1), 31 + 2 * rank)]
            pieces += [((pa, 1 - b, y, 0), 38 + rank), ((pa, b, 1 - y, 1), 42 + rank)]
            for far in range(2):
                pb, py = (b, 1 - b)[far], (y, 1 - y)[far]
                pieces += [((pa, pb, 1 - y, 0), 46 + 4 * far + rank), ((pa, 1 - b, py, 1), 54 + 4 * far + rank)]
            for piece, slot in pieces:
                self.arrived(piece, slot, other)
                self.sent(piece, slot)
            self.sent((pa, b, y, 0), 6 + rank)
            self.sent((pa, b, y, 1), 18 + rank)
            self.sent((pa, b, y, 1), 10 + rank)
            self.sent((pa, b, 1 - y, 1), 14 + rank)
            self.sent((pa, b, y, 0), 22 + rank)
            self.sent((pa, 1 - b, y, 0), 26 + rank)

        @pl.when(a < LINE - 1)
        def _():
            self.sent((a, b, y, None), 0)

        @pl.when(a > 0)
        def _():
            self.sent((a, b, y, None), 3)

        for h in range(1, LINE - 1):

            @pl.when((a - h >= 0) & (a < LINE - 1))
            def _():
                self.sent((a - h, b, y, None), h)

            @pl.when((a + h < LINE) & (a > 0))
            def _():
                self.sent((a + h, b, y, None), 3 + h)

        self.own_copy().wait()


def enter_kernel(src, rows, dst, rows_all, send, recv, local, row_send, row_recv):
    a, b, core, y = place()
    half = rows.shape[0]
    moves = core != y
    greet(moves)
    crossing = pltpu.make_async_remote_copy(
        rows,
        rows_all.at[pl.ds(0, half)],
        row_send.at[0],
        row_recv.at[0],
        device_id=target(a, b, y, core),
        device_id_type=MESH_ID,
    )

    def to_mate(source):
        return pltpu.make_async_remote_copy(
            source,
            rows_all.at[pl.ds(half, half)],
            row_send.at[1],
            row_recv.at[1],
            device_id=target(a, b, 1 - core, y),
            device_id_type=MESH_ID,
        )

    stay = pltpu.make_async_copy(rows, rows_all.at[pl.ds(0, half)], row_recv.at[2])

    @pl.when(moves)
    def _():
        crossing.start()

    @pl.when(jnp.logical_not(moves))
    def _():
        stay.start()
        to_mate(rows).start()

    gather = Gather(src, dst, send, recv, local)
    gather.begin()
    for h in range(1, LINE):
        gather.hop(h)

    @pl.when(moves)
    def _():
        crossing.wait()
        to_mate(rows_all.at[pl.ds(0, half)]).start()

    gather.turn()
    gather.last()

    @pl.when(jnp.logical_not(moves))
    def _():
        stay.wait()

    to_mate(rows_all.at[pl.ds(0, half)]).wait()
    gather.end()


def enter(shard, rows, devices, cross, mate, collective_id):
    shard_rows, width = shard.shape
    if devices != 2 * 2 * 2 * LINE:
        weights = lax.all_gather(shard, ("mp", "chip", "core"), axis=0, tiled=True)
        own = cross(rows)
        return weights.reshape(2, -1, width), jnp.concatenate([own, mate(own)], axis=0)
    anywhere = pl.BlockSpec(memory_space=pl.ANY)
    return pl.pallas_call(
        enter_kernel,
        out_shape=[
            jax.ShapeDtypeStruct((2, devices // 2 * shard_rows, width), shard.dtype),
            jax.ShapeDtypeStruct((2 * rows.shape[0], rows.shape[1]), rows.dtype),
        ],
        in_specs=[anywhere, anywhere],
        out_specs=[anywhere, anywhere],
        scratch_shapes=[
            pltpu.SemaphoreType.DMA((62,)),
            pltpu.SemaphoreType.DMA((62,)),
            pltpu.SemaphoreType.DMA,
            pltpu.SemaphoreType.DMA((2,)),
            pltpu.SemaphoreType.DMA((3,)),
        ],
        compiler_params=pltpu.CompilerParams(collective_id=collective_id, has_side_effects=True),
        name="enter",
    )(shard, rows)


class Reduce:
    STEPS = 14

    def __init__(self, src, out, scratch):
        self.src, self.out = src, out
        (
            self.acc,
            self.mates,
            self.y_two,
            self.x_two,
            self.x_one,
            self.y_one,
            self.up,
            self.down,
            self.load_sem,
            self.mate_send,
            self.mate_recv,
            self.y_send,
            self.y_recv,
            self.x_send,
            self.x_recv,
            self.up_send,
            self.up_recv,
            self.down_send,
            self.down_recv,
        ) = scratch
        self.rows, self.width = self.acc.shape[3:]
        self.first = self.y_two.shape[3]
        self.a, self.b, self.core, self.y = place()

    @staticmethod
    def scratch(rows, width):
        first = (width // LANES + 1) // 2 * LANES
        dma = pltpu.SemaphoreType.DMA
        return [
            pltpu.VMEM((LINE, 2, 2, rows, width), BF16),
            pltpu.VMEM((LINE, 2, 2, rows, width), BF16),
            pltpu.VMEM((LINE, 2, rows, first), BF16),
            pltpu.VMEM((LINE, 2, rows, width - first), BF16),
            pltpu.VMEM((LINE, rows, first), BF16),
            pltpu.VMEM((LINE, rows, width - first), BF16),
            pltpu.VMEM((LINE, rows, width), BF16),
            pltpu.VMEM((LINE, rows, width), BF16),
            dma((LINE, 2, 2)),
            dma((LINE, 2, 2)),
            dma((LINE, 2, 2)),
            dma((LINE, 3)),
            dma((LINE, 3)),
            dma((LINE, 3)),
            dma((LINE, 3)),
            dma((LINE,)),
            dma((LINE,)),
            dma((LINE,)),
            dma((LINE,)),
        ]

    def owner(self, group):
        near = jnp.where(self.a < LINE // 2, LINE - 1 - group, group)
        inner = [[3, 0, 2, 1], [0, 3, 1, 2]]
        pick = lambda order: sum(jnp.where(group == g, order[g], 0) for g in range(LINE))
        return jnp.where(self.a == 1, pick(inner[0]), jnp.where(self.a == 2, pick(inner[1]), near))

    def remote(self, src, dst, send, recv, device):
        return pltpu.make_async_remote_copy(src, dst, send, recv, device_id=device, device_id_type=MESH_ID)

    def source(self, group, pb, py, core):
        row = pl.multiple_of(((self.owner(group) * 2 + pb) * 2 + core) * self.rows, self.rows)
        return self.src.at[py, pl.ds(row, self.rows), :]

    def load(self, group, pb, py):
        return pltpu.make_async_copy(
            self.source(group, pb, py, self.core), self.acc.at[group, pb, py], self.load_sem.at[group, pb, py]
        )

    def to_mate(self, group, pb, py):
        return self.remote(
            self.source(group, pb, py, 1 - self.core),
            self.mates.at[group, pb, py],
            self.mate_send.at[group, pb, py],
            self.mate_recv.at[group, pb, py],
            target(self.a, self.b, 1 - self.core, self.y),
        )

    def low(self):
        return pl.ds(0, self.first)

    def high(self):
        return pl.ds(self.first, self.width - self.first)

    def over_y(self, group, k):
        device = target(self.a, self.b, self.core, 1 - self.y)
        if k < 2:
            src, dst = self.acc.at[group, k, 1 - self.y, :, self.low()], self.y_two.at[group, k]
        else:
            src, dst = self.acc.at[group, self.b, 1 - self.y, :, self.high()], self.y_one.at[group]
        return self.remote(src, dst, self.y_send.at[group, k], self.y_recv.at[group, k], device)

    def over_x(self, group, k):
        device = target(self.a, 1 - self.b, self.core, self.y)
        if k < 2:
            src, dst = self.acc.at[group, 1 - self.b, k, :, self.high()], self.x_two.at[group, k]
        else:
            src, dst = self.acc.at[group, 1 - self.b, self.y, :, self.low()], self.x_one.at[group]
        return self.remote(src, dst, self.x_send.at[group, k], self.x_recv.at[group, k], device)

    def along(self, group, step):
        pa = self.owner(group)
        src = self.acc.at[group, self.b, self.y]
        device = target(self.a + step, self.b, self.core, self.y)
        buffer, send, recv = (
            (self.up, self.up_send, self.up_recv) if step > 0 else (self.down, self.down_send, self.down_recv)
        )
        return self.remote(src, buffer.at[pa], send.at[pa], recv.at[pa], device)

    def add(self, ref, other):
        tile = 16

        @pl.loop(0, self.rows // tile)
        def _(i):
            span = pl.ds(pl.multiple_of(i * tile, tile), tile)
            ref[span, :] = (ref[span, :].astype(F32) + other[span, :].astype(F32)).astype(BF16)

    def begin(self):
        for group in range(LINE):
            for pb in range(2):
                for py in range(2):
                    self.to_mate(group, pb, py).start()
                    self.load(group, pb, py).start()

    def first_stage(self, group):
        for pb in range(2):
            for py in range(2):
                self.load(group, pb, py).wait()
                self.to_mate(group, pb, py).wait_recv()
                self.add(self.acc.at[group, pb, py], self.mates.at[group, pb, py])
        for k in range(2):
            self.over_y(group, k).start()
            self.over_x(group, k).start()

    def second_stage(self, group):
        for k in range(2):
            self.over_y(group, k).wait_recv()
            self.add(self.acc.at[group, k, self.y, :, self.low()], self.y_two.at[group, k])
            self.over_x(group, k).wait_recv()
            self.add(self.acc.at[group, self.b, k, :, self.high()], self.x_two.at[group, k])
        self.over_x(group, 2).start()
        self.over_y(group, 2).start()

    def third_stage(self, group):
        mine = self.acc.at[group, self.b, self.y]
        self.over_x(group, 2).wait_recv()
        self.add(mine.at[:, self.low()], self.x_one.at[group])
        self.over_y(group, 2).wait_recv()
        self.add(mine.at[:, self.high()], self.y_one.at[group])
        pa = self.owner(group)

        @pl.when((self.a == 0) & (pa > 0))
        def _():
            self.along(group, 1).start()

        @pl.when((self.a == LINE - 1) & (pa < LINE - 1))
        def _():
            self.along(group, -1).start()

    def line_stage(self, group):
        mine = self.acc.at[group, self.b, self.y]
        pa = self.owner(group)

        @pl.when((self.a > 0) & (pa > self.a))
        def _():
            self.along(group, 1).wait_recv()
            self.add(mine, self.up.at[pa])
            self.along(group, 1).start()

        @pl.when((self.a < LINE - 1) & (pa < self.a))
        def _():
            self.along(group, -1).wait_recv()
            self.add(mine, self.down.at[pa])
            self.along(group, -1).start()

    def step(self, t):
        for stage, start in ((self.first_stage, 1), (self.second_stage, 3), (self.third_stage, 5), (self.line_stage, 7)):

            @pl.when((lax.rem(t, 2) == 1) & (t >= start) & (t < start + 2 * LINE))
            def _():
                stage((t - start) // 2)

    def end(self):
        last = LINE - 1
        mine = self.acc.at[last, self.b, self.y]

        @pl.when(self.a > 0)
        def _():
            self.along(last, 1).wait_recv()
            self.add(mine, self.up.at[self.a])

        @pl.when(self.a < LINE - 1)
        def _():
            self.along(last, -1).wait_recv()
            self.add(mine, self.down.at[self.a])

        self.out[...] = mine[...].astype(F32)
        for group in range(LINE):
            for pb in range(2):
                for py in range(2):
                    self.to_mate(group, pb, py).wait_send()
            for k in range(3):
                self.over_y(group, k).wait_send()
                self.over_x(group, k).wait_send()
            pa = self.owner(group)

            @pl.when(pa > self.a)
            def _():
                self.along(group, 1).wait_send()

            @pl.when(pa < self.a)
            def _():
                self.along(group, -1).wait_send()


def reduce_kernel(src, out, *scratch):
    greet(False)
    reduce = Reduce(src, out, scratch)
    reduce.begin()

    @pl.loop(0, reduce.STEPS)
    def _(t):
        reduce.step(t)

    reduce.end()


def reduce_all(grads, devices, collective_id):
    if devices != 8 * LINE:
        return scatter_sum(grads)
    rows, width = 2 * grads.shape[1] // devices, grads.shape[2]
    return pl.pallas_call(
        reduce_kernel,
        in_specs=[pl.BlockSpec(memory_space=pl.ANY)],
        out_specs=pl.BlockSpec(memory_space=pltpu.VMEM),
        out_shape=jax.ShapeDtypeStruct((rows, width), F32),
        scratch_shapes=Reduce.scratch(rows, width),
        compiler_params=pltpu.CompilerParams(
            collective_id=collective_id, has_side_effects=True, vmem_limit_bytes=VMEM_BYTES
        ),
        name="reduce_pieces",
    )(grads)


def norm_forward(hidden, gain, bias):
    centered = hidden - jnp.mean(hidden, axis=-1, keepdims=True)
    inv_std = lax.rsqrt(jnp.mean(centered * centered, axis=-1, keepdims=True) + EPSILON)
    normed = centered * inv_std
    return normed * gain + bias, normed, inv_std


def norm_back(grad_y, normed, inv_std, gain):
    grad_gain = jnp.sum(grad_y * normed, axis=0)
    grad_bias = jnp.sum(grad_y, axis=0)
    scaled = grad_y * gain
    grad_h = inv_std * (
        scaled
        - jnp.mean(scaled, axis=-1, keepdims=True)
        - normed * jnp.mean(scaled * normed, axis=-1, keepdims=True)
    )
    return grad_h, grad_gain, grad_bias


def on_device(
    mp,
    devices,
    inputs,
    segments,
    w_qkv,
    w_out,
    first_gain,
    first_bias,
    w_gate,
    w_up,
    w_down,
    second_gain,
    second_bias,
    d_out,
):
    group = ("chip", "mp")
    crossing = [(a * mp + b, b * mp + a) for a in range(2) for b in range(mp)]

    def cross(tensor):
        return lax.ppermute(tensor, ("core", "mp"), crossing)

    def mate(tensor):
        return lax.ppermute(tensor, "core", [(0, 1), (1, 0)])

    core = lax.axis_index("core")
    shard, half_cols = w_qkv.shape[1], w_qkv.shape[2]
    pairs = half_cols // LANES
    width = inputs.shape[1]
    half_ff = w_gate.shape[1]
    half_len = inputs.shape[0]
    turn = core * half_len

    vectors = jnp.stack([first_gain, first_bias, second_gain, second_bias], axis=1)
    pad = jnp.zeros((shard, LANES - 4), BF16)
    attn_shard = jnp.concatenate(
        [
            w_qkv.reshape(3, shard, pairs, LANES).transpose(1, 2, 0, 3).reshape(shard, 3 * half_cols),
            w_out.T,
            vectors,
            pad,
        ],
        axis=1,
    )
    ff_shard = jnp.concatenate([w_gate, w_up, w_down.T], axis=1)
    labels = cross(segments)
    attn_w, rows_all = enter(attn_shard, inputs, devices, cross, mate, 1)
    rows_own = rows_all[:half_len]
    d_own = cross(d_out)
    after = attn_w[0, :shard, :1] * 0
    ff_w = lax.all_gather(ff_shard + after, ("mp", "chip", "core"), axis=0, tiled=True)
    ff_w = ff_w.reshape(2, width, 3 * half_ff)

    labels = jnp.where(core == 0, labels, jnp.roll(labels, half_len))
    attn_own = lax.dynamic_index_in_dim(attn_w, core, 0, False)
    qkv_w = attn_own[:, : 3 * half_cols]
    out_own = attn_own[:, 3 * half_cols : 4 * half_cols]
    out_mate = lax.dynamic_index_in_dim(attn_w, 1 - core, 0, False)[:, 3 * half_cols : 4 * half_cols]
    gains = attn_w[0, :, 4 * half_cols : 4 * half_cols + 4].astype(F32).T
    gain_one, bias_one, gain_two, bias_two = gains[0], gains[1], gains[2], gains[3]
    cos, sin = (jnp.asarray(t) for t in rope_tables())

    qkv = project(core.reshape(1), rows_all, attn_w, cos, sin)
    o, lse = attend(qkv, labels, turn)
    o_in = mate(o[half_len:])
    attn = dot(o[:half_len], out_own, NT) + dot(o_in, out_mate, NT)
    middle, first_hat, first_inv = norm_forward(rows_own.astype(F32) + attn, gain_one, bias_one)
    middle_low = middle.astype(BF16)

    saved = []
    mlp = None
    for block in (ff_w[0], ff_w[1]):
        gate_w, up_w, down_t = (block[:, k * half_ff : (k + 1) * half_ff] for k in range(3))
        gate = dot(middle_low, gate_w)
        up = dot(middle_low, up_w)
        sig = jax.nn.sigmoid(gate)
        silu = gate * sig
        hidden = (silu * up).astype(BF16)
        part = dot(hidden, down_t, NT)
        mlp = part if mlp is None else mlp + part
        saved.append((gate_w, up_w, down_t, gate, up, sig, silu, hidden))
    result, second_hat, second_inv = norm_forward(middle + mlp, gain_two, bias_two)
    outputs = cross(result.astype(BF16))
    grad_two, second_gain_part, second_bias_part = norm_back(
        d_own.astype(F32), second_hat, second_inv, gain_two
    )
    grad_two_low = grad_two.astype(BF16)
    grad_middle = grad_two
    grads = []
    for gate_w, up_w, down_t, gate, up, sig, silu, hidden in saved:
        grad_down_t = dot(grad_two_low, hidden, TN)
        grad_hidden = dot(grad_two_low, down_t)
        grad_gate = (grad_hidden * up * sig * (1.0 + gate * (1.0 - sig))).astype(BF16)
        grad_up = (grad_hidden * silu).astype(BF16)
        grads.append((dot(middle_low, grad_gate, TN), dot(middle_low, grad_up, TN), grad_down_t))
        grad_middle = grad_middle + dot(grad_gate, gate_w, NT) + dot(grad_up, up_w, NT)
    grad_one, first_gain_part, first_bias_part = norm_back(grad_middle, first_hat, first_inv, gain_one)
    sums = jnp.stack([first_gain_part, first_bias_part, second_gain_part, second_bias_part], axis=1)
    sums = jnp.concatenate([sums, jnp.zeros((width, LANES - 4), F32)], axis=1)
    ff_sum = jnp.stack([jnp.concatenate([*part, sums], axis=1).astype(BF16) for part in grads])
    grad_one_low = grad_one.astype(BF16)
    grad_one_all = jnp.concatenate([grad_one_low, mate(grad_one_low)], axis=0)
    grad_one_home = cross(grad_one)
    do = dot(grad_one_all, out_own).astype(BF16)
    grad_out_t = dot(grad_one_all, o, TN).astype(BF16)
    cos_turned, sin_turned = (
        jnp.where(core == 0, t, jnp.roll(t, half_len, axis=0)) for t in (cos, sin)
    )
    back, ff_grad = attend_back(qkv, o, do, lse, labels, cos_turned, sin_turned, ff_sum, devices, 2)
    weight_grad = dot(rows_all, back, TN).astype(BF16)
    attn_sum = jnp.concatenate([weight_grad, grad_out_t], axis=1)
    attn_sum = jnp.where(jnp.arange(2)[:, None, None] == core, attn_sum[None], 0)
    attn_grad = reduce_all(attn_sum, devices, 3)
    grad_rows = dot(back, qkv_w, NT)
    grad_rows = grad_rows[:half_len] + mate(grad_rows[half_len:].astype(BF16)).astype(F32)
    grad_inputs = grad_one_home + cross(grad_rows.astype(BF16)).astype(F32)
    grad_qkv = (
        attn_grad[:, : 3 * half_cols]
        .reshape(shard, pairs, 3, LANES)
        .transpose(2, 0, 1, 3)
        .reshape(3, shard, half_cols)
    )
    grad_out = attn_grad[:, 3 * half_cols :].T
    grad_gate, grad_up, grad_down_t = (ff_grad[:, k * half_ff : (k + 1) * half_ff] for k in range(3))
    grad_vectors = ff_grad[:, 3 * half_ff : 3 * half_ff + 4]
    return (
        outputs,
        grad_inputs,
        grad_qkv,
        grad_out,
        grad_vectors[:, 0],
        grad_vectors[:, 1],
        grad_gate,
        grad_up,
        grad_down_t.T,
        grad_vectors[:, 2],
        grad_vectors[:, 3],
    )


def solution(mesh):
    dp, mp = mesh.shape["dp"], mesh.shape["mp"]
    split = Mesh(mesh.devices.reshape(dp // 2, 2, mp), ("chip", "core", "mp"))
    rows = P(("chip", "core", "mp"), None)
    vector = P(("chip", "core"))
    columns = P(("chip", "core"), "mp")
    turned = P("mp", ("chip", "core"))
    stacked = P(None, ("chip", "core"), "mp")
    return jax.shard_map(
        functools.partial(on_device, mp, dp * mp),
        mesh=split,
        in_specs=(
            rows,
            vector,
            stacked,
            turned,
            vector,
            vector,
            columns,
            columns,
            turned,
            vector,
            vector,
            rows,
        ),
        out_specs=(
            rows,
            rows,
            stacked,
            turned,
            vector,
            vector,
            columns,
            columns,
            turned,
            vector,
            vector,
        ),
        check_vma=False,
    )
```

```python
import functools

import jax
import jax.numpy as jnp
import numpy as np
from jax import lax
from jax.experimental import pallas as pl
from jax.experimental.pallas import tpu as pltpu
from jax.sharding import Mesh
from jax.sharding import PartitionSpec as P

HEAD_DIM = 64
SEQ_LEN = 2048
LANES = 128
EPSILON = 1e-12
ROPE_BASE = 1000.0
MASKED = -10000.0
SCALE = HEAD_DIM**-0.5
F32 = jnp.float32
BF16 = jnp.bfloat16
NT = (((1,), (1,)), ((), ()))
NN = (((1,), (0,)), ((), ()))
TN = (((0,), (0,)), ((), ()))
VMEM_BYTES = 60 << 20
FEED_VMEM = 62 << 20
FWD_Q, FWD_K = 1024, 512
BWD_Q, BWD_K = 1024, 512
ROW_BLOCK = 256
MESH_ID = pl.DeviceIdType.MESH
LINE = 4
FIRST_TILES = 2
ROW_PARTS = LINE


def dot(left, right, dims=NN):
    return lax.dot_general(left, right, dims, preferred_element_type=F32)


def rope_tables():
    half = HEAD_DIM // 2
    frequency = ROPE_BASE ** (-2.0 * np.arange(half) / HEAD_DIM)
    angles = np.arange(SEQ_LEN)[:, None] * frequency[None, :]
    cos, sin = np.cos(angles), np.sin(angles)
    heads = LANES // HEAD_DIM
    return (
        np.tile(np.concatenate([cos, cos], 1), (1, heads)).astype(np.float32),
        np.tile(np.concatenate([-sin, sin], 1), (1, heads)).astype(np.float32),
    )


def half_swap(tile):
    lane = lax.broadcasted_iota(jnp.int32, (1, LANES), 1)
    half = HEAD_DIM // 2
    return jnp.where(
        lane % HEAD_DIM < half,
        pltpu.roll(tile, LANES - half, 1),
        pltpu.roll(tile, half, 1),
    )


def project_kernel(core_ref, x_ref, w_ref, cos_ref, sin_ref, out_ref, *, pairs):
    x = x_ref[...]
    cos, sin = cos_ref[...], sin_ref[...]
    for pair in range(pairs):
        base = pair * 3 * LANES
        tile = dot(x, w_ref[0, :, base : base + 3 * LANES])
        for kind in range(2):
            part = tile[:, kind * LANES : (kind + 1) * LANES]
            out_ref[:, base + kind * LANES : base + (kind + 1) * LANES] = (
                part * cos + half_swap(part) * sin
            ).astype(BF16)
        out_ref[:, base + 2 * LANES : base + 3 * LANES] = tile[:, 2 * LANES :].astype(BF16)


def project(core, rows, weights, cos, sin):
    tokens, depth = rows.shape
    wide = weights.shape[2]
    steps = tokens // ROW_BLOCK

    def turned(step, core_ref):
        return (lax.rem(step + core_ref[0] * (steps // 2), steps), 0)

    return pl.pallas_call(
        functools.partial(project_kernel, pairs=wide // (3 * LANES)),
        grid_spec=pltpu.PrefetchScalarGridSpec(
            num_scalar_prefetch=1,
            grid=(steps,),
            in_specs=[
                pl.BlockSpec((ROW_BLOCK, depth), lambda i, c: (i, 0)),
                pl.BlockSpec((1, depth, wide), lambda i, c: (c[0], 0, 0)),
                pl.BlockSpec((ROW_BLOCK, LANES), turned),
                pl.BlockSpec((ROW_BLOCK, LANES), turned),
            ],
            out_specs=pl.BlockSpec((ROW_BLOCK, wide), lambda i, c: (i, 0)),
        ),
        out_shape=jax.ShapeDtypeStruct((tokens, wide), BF16),
        compiler_params=pltpu.CompilerParams(vmem_limit_bytes=VMEM_BYTES),
        cost_estimate=pl.CostEstimate(
            flops=2 * tokens * depth * wide,
            bytes_accessed=2 * tokens * (depth + wide) + 2 * depth * wide,
            transcendentals=0,
        ),
        name="project",
    )(core, rows, weights, cos, sin)


def block_range(labels, block, other, turn):
    blocks = labels.shape[0] // block
    valid = labels >= 0
    tiles = labels.reshape(blocks, block)
    first, last = tiles[:, 0], jnp.max(tiles, axis=1)
    low = jnp.sum((valid[None] & (labels[None] < first[:, None])).astype(jnp.int32), 1)
    high = jnp.sum((valid[None] & (labels[None] <= last[:, None])).astype(jnp.int32), 1)
    offset = (labels.shape[0] - turn) // other
    return low // other + offset, jnp.where(high > low, (high + other - 1) // other, low // other) + offset


def attend_kernel(low_ref, high_ref, q_ref, k_ref, v_ref, key_ref, query_ref, o_ref, lse_ref, v_turned):
    tokens = q_ref.shape[0]
    key_blocks = tokens // FWD_K
    lane = lax.broadcasted_iota(jnp.int32, (1, LANES), 1)
    zero = jnp.zeros((), BF16)
    v_turned[...] = v_ref[...].T

    @pl.loop(0, tokens // FWD_Q)
    def _(i):
        q0 = pl.multiple_of(i * FWD_Q, FWD_Q)
        scaled = q_ref[pl.ds(q0, FWD_Q), :] * jnp.asarray(SCALE, BF16)
        halves = (
            jnp.where(lane < HEAD_DIM, scaled, zero),
            jnp.where(lane >= HEAD_DIM, scaled, zero),
        )
        query_label = query_ref[:, pl.ds(q0, FWD_Q)]

        def body(j, carry):
            k0 = pl.multiple_of(lax.rem(j, key_blocks) * FWD_K, FWD_K)
            k = k_ref[pl.ds(k0, FWD_K), :]
            same = key_ref[pl.ds(k0, FWD_K), :] == query_label
            scores = [dot(k, half, NT) for half in halves]
            out = []
            for h in range(2):
                top, total, acc = carry[h]
                s = jnp.where(same, scores[h], -1e30)
                new_top = jnp.maximum(top, jnp.max(s, axis=0, keepdims=True))
                fade = jnp.exp(top - new_top)
                e = jnp.exp(s - new_top)
                total = fade * total + jnp.sum(e, axis=0, keepdims=True)
                part = dot(v_turned[h * HEAD_DIM : (h + 1) * HEAD_DIM, pl.ds(k0, FWD_K)], e.astype(BF16))
                out.append((new_top, total, acc * fade + part))
            return tuple(out)

        start = (
            jnp.full((1, FWD_Q), MASKED, F32),
            jnp.zeros((1, FWD_Q), F32),
            jnp.zeros((HEAD_DIM, FWD_Q), F32),
        )
        ended = lax.fori_loop(low_ref[i], high_ref[i], body, (start, start))
        out = []
        for h in range(2):
            top, total, acc = ended[h]
            norm = jnp.maximum(total, 1.0)
            out.append(acc / norm)
            lse_ref[0, pl.ds(h, 1), pl.ds(q0, FWD_Q)] = top + jnp.log(norm)
        o_ref[pl.ds(q0, FWD_Q), :] = jnp.concatenate(out, 0).T.astype(BF16)


def attend(qkv, labels, turn):
    tokens = qkv.shape[0]
    pairs = qkv.shape[1] // (3 * LANES)
    low, high = block_range(labels, FWD_Q, FWD_K, turn)
    queries = jnp.where(labels < 0, -2, labels)
    whole = lambda shape: pl.BlockSpec(shape, lambda p, *_: (0,) * len(shape))
    part = lambda kind: pl.BlockSpec((tokens, LANES), lambda p, *_: (0, 3 * p + kind))
    return pl.pallas_call(
        attend_kernel,
        grid_spec=pltpu.PrefetchScalarGridSpec(
            num_scalar_prefetch=2,
            grid=(pairs,),
            in_specs=[part(0), part(1), part(2), whole((tokens, 1)), whole((1, tokens))],
            out_specs=[
                pl.BlockSpec((tokens, LANES), lambda p, *_: (0, p)),
                pl.BlockSpec((1, 2, tokens), lambda p, *_: (p, 0, 0)),
            ],
            scratch_shapes=[pltpu.VMEM((LANES, tokens), BF16)],
        ),
        out_shape=[
            jax.ShapeDtypeStruct((tokens, pairs * LANES), BF16),
            jax.ShapeDtypeStruct((pairs, 2, tokens), F32),
        ],
        compiler_params=pltpu.CompilerParams(vmem_limit_bytes=VMEM_BYTES),
        cost_estimate=pl.CostEstimate(
            flops=pairs * 8 * tokens * tokens * LANES,
            bytes_accessed=pairs * 4 * tokens * LANES * 2,
            transcendentals=pairs * 2 * tokens * tokens,
        ),
        name="attend",
    )(low, high, qkv, qkv, qkv, labels[:, None], queries[None])


def attend_back_step(t, refs, scratch):
    q_all, o_all, do_all, lse_ref, key_ref, query_ref, cos_ref, sin_ref, out_ref = refs
    dq_turned, inner, k_turned = scratch
    tokens = q_all.shape[0]
    blocks = tokens // BWD_K
    pair, j = t // blocks, lax.rem(t, blocks)
    lane = lax.broadcasted_iota(jnp.int32, (1, LANES), 1)
    zero = jnp.zeros((), BF16)
    picks = (lane < HEAD_DIM, lane >= HEAD_DIM)

    def lanes(kind):
        return pl.ds(pl.multiple_of((pair * 3 + kind) * LANES, LANES), LANES)

    own = pl.ds(pl.multiple_of(pair * LANES, LANES), LANES)

    def unrope(tile, rows):
        return (tile * cos_ref[rows, :] - half_swap(tile) * sin_ref[rows, :]).astype(BF16)

    @pl.when(j == 0)
    def _():
        k_turned[...] = q_all[:, lanes(1)].T
        product = (o_all[:, own].astype(F32) * do_all[:, own].astype(F32)).T
        inner[0:1, :] = jnp.sum(product[:HEAD_DIM], axis=0, keepdims=True)
        inner[1:2, :] = jnp.sum(product[HEAD_DIM:], axis=0, keepdims=True)
        dq_turned[...] = jnp.zeros_like(dq_turned)

    key_rows = pl.ds(pl.multiple_of(j * BWD_K, BWD_K), BWD_K)
    key_label = key_ref[key_rows, :]
    dks, dvs = [], []
    for h in range(2):
        k = jnp.where(picks[h], q_all[key_rows, lanes(1)], zero)
        v = jnp.where(picks[h], q_all[key_rows, lanes(2)], zero)
        kt = k_turned[pl.ds(h * HEAD_DIM, HEAD_DIM), key_rows]

        def body(i, carry):
            dk, dv = carry
            query_rows = pl.ds(pl.multiple_of(i * BWD_Q, BWD_Q), BWD_Q)
            q = q_all[query_rows, lanes(0)]
            do = do_all[query_rows, own]
            s = dot(k, q, NT)
            p = jnp.exp(s * SCALE - lse_ref[pair, pl.ds(h, 1), query_rows])
            p = jnp.where(key_label == query_ref[:, query_rows], p, 0.0)
            dp = dot(v, do, NT)
            ds = (p * (dp - inner[pl.ds(h, 1), query_rows])).astype(BF16)
            dv = dv + dot(p.astype(BF16), do)
            dk = dk + dot(ds, q)
            dq_turned[pl.ds(h * HEAD_DIM, HEAD_DIM), query_rows] += dot(kt, ds)
            return dk, dv

        empty = jnp.zeros((BWD_K, LANES), F32)
        dk, dv = lax.fori_loop(0, tokens // BWD_Q, body, (empty, empty))
        dks.append(dk)
        dvs.append(dv)
    out_ref[key_rows, lanes(1)] = unrope(jnp.where(picks[0], dks[0], dks[1]) * SCALE, key_rows)
    out_ref[key_rows, lanes(2)] = jnp.where(picks[0], dvs[0], dvs[1]).astype(BF16)

    @pl.when(j == blocks - 1)
    def _():
        out_ref[:, lanes(0)] = unrope(dq_turned[...].T * SCALE, pl.ds(0, tokens))


def attend_back_kernel(*refs, remote):
    refs, steps = list(refs), refs[0].shape[0] // BWD_K * (refs[0].shape[1] // (3 * LANES))
    inputs, refs = refs[:9], refs[9:]
    do_all, do_sem, scratch = refs[-2], refs[-1], None
    refs = refs[:-2]
    half = inputs[2].shape[0]
    takes = [
        pltpu.make_async_copy(inputs[2 + k], do_all.at[pl.ds(k * half, half)], do_sem.at[k]) for k in range(2)
    ]
    inputs = [*inputs[:2], do_all, *inputs[4:]]
    for take in takes:
        take.start()
    if not remote:
        out_ref, scratch = refs[0], refs[1:]
        for take in takes:
            take.wait()

        @pl.loop(0, steps)
        def _(t):
            attend_back_step(t, (*inputs, out_ref), scratch)

        return
    grads, out_ref, sums, scratch = refs[0], refs[1], refs[2], refs[3:]
    greet(False)
    reduce = Reduce(grads, sums, scratch[3:])
    reduce.begin()
    for take in takes:
        take.wait()

    @pl.loop(0, max(steps, reduce.STEPS))
    def _(t):
        reduce.step(t)

        @pl.when(t < steps)
        def _():
            attend_back_step(t, (*inputs, out_ref), scratch[:3])

    reduce.end()


def attend_back(qkv, o, do, do_in, lse, labels, cos, sin, grads, devices, collective_id):
    tokens, wide = qkv.shape
    remote = devices == 8 * LINE
    queries = jnp.where(labels < 0, -2, labels)
    vmem = pl.BlockSpec(memory_space=pltpu.VMEM)
    operands = [qkv, o, do, do_in, lse, labels[:, None], queries[None], cos, sin]
    out_shape = [jax.ShapeDtypeStruct((tokens, wide), BF16)]
    scratch = [
        pltpu.VMEM((LANES, tokens), F32),
        pltpu.VMEM((8, tokens), F32),
        pltpu.VMEM((LANES, tokens), BF16),
    ]
    anywhere = pl.BlockSpec(memory_space=pl.ANY)
    in_specs = [vmem, vmem, anywhere, anywhere] + [vmem] * 5
    params = dict(vmem_limit_bytes=VMEM_BYTES)
    if remote:
        rows, width = 2 * grads.shape[1] // devices, grads.shape[2]
        operands.append(grads)
        in_specs.append(pl.BlockSpec(memory_space=pl.ANY))
        out_shape.append(jax.ShapeDtypeStruct((rows, width), F32))
        scratch += Reduce.scratch(rows, width, (width // LANES + 1) // 2 * LANES)
        params.update(collective_id=collective_id, has_side_effects=True)
    scratch += [pltpu.VMEM((tokens, wide // 3), BF16), pltpu.SemaphoreType.DMA((2,))]
    out = pl.pallas_call(
        functools.partial(attend_back_kernel, remote=remote),
        in_specs=in_specs,
        out_specs=[vmem] * len(out_shape),
        out_shape=out_shape,
        scratch_shapes=scratch,
        compiler_params=pltpu.CompilerParams(**params),
        cost_estimate=pl.CostEstimate(
            flops=wide // (3 * LANES) * 20 * tokens * tokens * LANES,
            bytes_accessed=8 * tokens * wide,
            transcendentals=wide // (3 * LANES) * 2 * tokens * tokens,
        ),
        name="attend_back",
    )(*operands)
    return (out[0], out[1]) if remote else (out[0], scatter_sum(grads))


def scatter_sum(grads):
    flat = grads.reshape(-1, grads.shape[2])
    return lax.psum_scatter(flat, ("mp", "chip", "core"), scatter_dimension=0, tiled=True).astype(F32)


def place():
    chip = lax.axis_index("chip")
    return chip // 2, lax.rem(chip, 2), lax.axis_index("core"), lax.axis_index("mp")


def target(a, b, core, y):
    return {"chip": a * 2 + b, "core": core, "mp": y}


def greet(moves):
    a, b, core, y = place()
    barrier = pltpu.get_barrier_semaphore()

    def signal(device):
        pl.semaphore_signal(barrier, inc=1, device_id=device, device_id_type=MESH_ID)

    signal(target(a, 1 - b, core, y))
    signal(target(a, b, core, 1 - y))
    signal(target(a, b, 1 - core, y))

    @pl.when(a > 0)
    def _():
        signal(target(a - 1, b, core, y))

    @pl.when(a < LINE - 1)
    def _():
        signal(target(a + 1, b, core, y))

    @pl.when(moves)
    def _():
        signal(target(a, b, y, core))

    edges = jnp.where(a > 0, 1, 0) + jnp.where(a < LINE - 1, 1, 0) + jnp.where(moves, 1, 0)
    pl.semaphore_wait(barrier, 3 + edges)


class Gather:
    def __init__(self, src, dst, send, recv, local):
        self.src, self.dst, self.send, self.recv, self.local = src, dst, send, recv, local
        self.rows, self.width = src.shape
        tiles = self.width // LANES
        first = FIRST_TILES * LANES if FIRST_TILES < tiles else tiles // 2 * LANES
        self.columns = [(0, first), (first, self.width - first)]
        self.a, self.b, self.core, self.y = place()

    def span(self, half):
        start, size = (0, self.width) if half is None else self.columns[half]
        return pl.ds(start, size)

    def at(self, piece, core=None):
        pa, pb, py, half = piece
        core = self.core if core is None else core
        row = pl.multiple_of(((pa * 2 + pb) * 2 + core) * self.rows, self.rows)
        return self.dst.at[py, pl.ds(row, self.rows), self.span(half)]

    def own_copy(self):
        return pltpu.make_async_copy(self.src, self.at((self.a, self.b, self.y, None)), self.local)

    def start(self, piece, slot, device, mine=False):
        source = self.src.at[:, self.span(piece[3])] if mine else self.at(piece)
        pltpu.make_async_remote_copy(
            source, self.at(piece), self.send.at[slot], self.recv.at[slot], device_id=device, device_id_type=MESH_ID
        ).start()

    def handle(self, piece, slot, core=None):
        ref = self.at(piece, core)
        return pltpu.make_async_remote_copy(
            ref,
            ref,
            self.send.at[slot],
            self.recv.at[slot],
            device_id=target(self.a, self.b, 1 - self.core, self.y),
            device_id_type=MESH_ID,
        )

    def arrived(self, piece, slot, core=None):
        self.handle(piece, slot, core).wait_recv()

    def sent(self, piece, slot):
        self.handle(piece, slot).wait_send()

    def to_x(self, piece, slot, mine=False):
        self.start(piece, slot, target(self.a, 1 - self.b, self.core, self.y), mine)

    def to_y(self, piece, slot, mine=False):
        self.start(piece, slot, target(self.a, self.b, self.core, 1 - self.y), mine)

    def to_mate(self, piece, slot, mine=False):
        self.start(piece, slot, target(self.a, self.b, 1 - self.core, self.y), mine)

    def to_line(self, piece, slot, step, mine=False):
        self.start(piece, slot, target(self.a + step, self.b, self.core, self.y), mine)

    def spread(self, pa, rank, mine=False):
        b, y = self.b, self.y
        self.to_x((pa, b, y, 0), 6 + rank, mine)
        self.to_y((pa, b, y, 1), 18 + rank, mine)
        for half in range(2):
            self.to_mate((pa, b, y, half), 30 + 2 * rank + half, mine)
        self.to_y((pa, b, y, 0), 22 + rank, mine)
        self.to_x((pa, b, y, 1), 10 + rank, mine)

    def begin(self):
        a, b, y = self.a, self.b, self.y
        piece = (a, b, y, None)

        @pl.when(a < LINE - 1)
        def _():
            self.to_line(piece, 0, 1, True)

        @pl.when(a > 0)
        def _():
            self.to_line(piece, 3, -1, True)

        self.spread(a, 0, True)
        self.own_copy().start()

    def hop(self, h):
        a, b, y = self.a, self.b, self.y

        @pl.when(a - h >= 0)
        def _():
            self.arrived((a - h, b, y, None), h - 1)
            if h < LINE - 1:

                @pl.when(a < LINE - 1)
                def _():
                    self.to_line((a - h, b, y, None), h, 1)

            self.spread(a - h, LINE - h)

        @pl.when(a + h < LINE)
        def _():
            self.arrived((a + h, b, y, None), 2 + h)
            if h < LINE - 1:

                @pl.when(a > 0)
                def _():
                    self.to_line((a + h, b, y, None), 3 + h, -1)

            self.spread(a + h, h)

    def ranks(self):
        return [(rank, lax.rem(self.a + rank, LINE)) for rank in range(LINE)]

    def turn(self):
        b, y = self.b, self.y
        for rank, pa in self.ranks():
            self.arrived((pa, 1 - b, y, 0), 6 + rank)
            self.to_y((pa, 1 - b, y, 0), 26 + rank)
            self.to_mate((pa, 1 - b, y, 0), 38 + rank)
            self.arrived((pa, b, 1 - y, 1), 18 + rank)
            self.to_x((pa, b, 1 - y, 1), 14 + rank)
            self.to_mate((pa, b, 1 - y, 1), 42 + rank)

    def last(self):
        b, y = self.b, self.y
        for rank, pa in self.ranks():
            for far in range(2):
                pb, py = (b, 1 - b)[far], (y, 1 - y)[far]
                self.arrived((pa, pb, 1 - y, 0), 22 + 4 * far + rank)
                self.to_mate((pa, pb, 1 - y, 0), 46 + 4 * far + rank)
                self.arrived((pa, 1 - b, py, 1), 10 + 4 * far + rank)
                self.to_mate((pa, 1 - b, py, 1), 54 + 4 * far + rank)

    def end(self):
        a, b, y = self.a, self.b, self.y
        other = 1 - self.core
        for rank, pa in self.ranks():
            pieces = [((pa, b, y, 0), 30 + 2 * rank), ((pa, b, y, 1), 31 + 2 * rank)]
            pieces += [((pa, 1 - b, y, 0), 38 + rank), ((pa, b, 1 - y, 1), 42 + rank)]
            for far in range(2):
                pb, py = (b, 1 - b)[far], (y, 1 - y)[far]
                pieces += [((pa, pb, 1 - y, 0), 46 + 4 * far + rank), ((pa, 1 - b, py, 1), 54 + 4 * far + rank)]
            for piece, slot in pieces:
                self.arrived(piece, slot, other)
                self.sent(piece, slot)
            self.sent((pa, b, y, 0), 6 + rank)
            self.sent((pa, b, y, 1), 18 + rank)
            self.sent((pa, b, y, 1), 10 + rank)
            self.sent((pa, b, 1 - y, 1), 14 + rank)
            self.sent((pa, b, y, 0), 22 + rank)
            self.sent((pa, 1 - b, y, 0), 26 + rank)

        @pl.when(a < LINE - 1)
        def _():
            self.sent((a, b, y, None), 0)

        @pl.when(a > 0)
        def _():
            self.sent((a, b, y, None), 3)

        for h in range(1, LINE - 1):

            @pl.when((a - h >= 0) & (a < LINE - 1))
            def _():
                self.sent((a - h, b, y, None), h)

            @pl.when((a + h < LINE) & (a > 0))
            def _():
                self.sent((a + h, b, y, None), 3 + h)

        self.own_copy().wait()


def enter_kernel(src, rows, dst, rows_all, copy_send, copy_recv, local, row_send, row_recv, held):
    a, b, core, y = place()
    half = rows.shape[0]
    part = half // ROW_PARTS
    moves = core != y
    greet(moves)

    def crossing(k):
        span = pl.ds(k * part, part)
        return pltpu.make_async_remote_copy(
            rows.at[span],
            rows_all.at[span],
            row_send.at[0, k],
            row_recv.at[0, k],
            device_id=target(a, b, y, core),
            device_id_type=MESH_ID,
        )

    def to_mate(source, k):
        return pltpu.make_async_remote_copy(
            source.at[pl.ds(k * part, part)],
            rows_all.at[pl.ds(half + k * part, part)],
            row_send.at[1, k],
            row_recv.at[1, k],
            device_id=target(a, b, 1 - core, y),
            device_id_type=MESH_ID,
        )

    take = pltpu.make_async_copy(rows, held, row_recv.at[2, 0])
    stay = pltpu.make_async_copy(held, rows_all.at[pl.ds(0, half)], row_recv.at[2, 1])

    def send(k):
        @pl.when(moves)
        def _():
            crossing(k).start()

        @pl.when(jnp.logical_not(moves))
        def _():
            to_mate(rows, k).start()

    @pl.when(jnp.logical_not(moves))
    def _():
        take.start()

    def hand_on(k):
        @pl.when(moves)
        def _():
            crossing(k).wait()
            to_mate(rows_all, k).start()

    gather = Gather(src, dst, copy_send, copy_recv, local)
    gather.begin()
    send(0)

    @pl.when(jnp.logical_not(moves))
    def _():
        take.wait()
        stay.start()

    for h in range(1, LINE):
        gather.hop(h)
        send(h)
    hand_on(0)
    hand_on(1)
    gather.turn()
    hand_on(2)
    hand_on(3)
    gather.last()

    @pl.when(jnp.logical_not(moves))
    def _():
        stay.wait()

    for k in range(ROW_PARTS):
        to_mate(rows_all, k).wait()
    gather.end()


def enter(shard, rows, devices, cross, mate, collective_id):
    shard_rows, width = shard.shape
    if devices != 2 * 2 * 2 * LINE:
        weights = lax.all_gather(shard, ("mp", "chip", "core"), axis=0, tiled=True)
        own = cross(rows)
        return weights.reshape(2, -1, width), jnp.concatenate([own, mate(own)], axis=0)
    anywhere = pl.BlockSpec(memory_space=pl.ANY)
    return pl.pallas_call(
        enter_kernel,
        out_shape=[
            jax.ShapeDtypeStruct((2, devices // 2 * shard_rows, width), shard.dtype),
            jax.ShapeDtypeStruct((2 * rows.shape[0], rows.shape[1]), rows.dtype),
        ],
        in_specs=[anywhere, anywhere],
        out_specs=[anywhere, anywhere],
        scratch_shapes=[
            pltpu.SemaphoreType.DMA((62,)),
            pltpu.SemaphoreType.DMA((62,)),
            pltpu.SemaphoreType.DMA,
            pltpu.SemaphoreType.DMA((2, ROW_PARTS)),
            pltpu.SemaphoreType.DMA((3, ROW_PARTS)),
            pltpu.VMEM(rows.shape, rows.dtype),
        ],
        compiler_params=pltpu.CompilerParams(collective_id=collective_id, has_side_effects=True),
        name="enter",
    )(shard, rows)


class Reduce:
    STEPS = 14

    def __init__(self, src, out, scratch):
        self.src, self.out = src, out
        (
            self.acc,
            self.mates,
            self.y_two,
            self.x_two,
            self.x_one,
            self.y_one,
            self.up,
            self.down,
            self.load_sem,
            self.mate_send,
            self.mate_recv,
            self.y_send,
            self.y_recv,
            self.x_send,
            self.x_recv,
            self.up_send,
            self.up_recv,
            self.down_send,
            self.down_recv,
        ) = scratch
        self.rows, self.width = self.acc.shape[3:]
        self.first = self.y_two.shape[3]
        self.a, self.b, self.core, self.y = place()

    @staticmethod
    def scratch(rows, width, first):
        dma = pltpu.SemaphoreType.DMA
        return [
            pltpu.VMEM((LINE, 2, 2, rows, width), BF16),
            pltpu.VMEM((LINE, 2, 2, rows, width), BF16),
            pltpu.VMEM((LINE, 2, rows, first), BF16),
            pltpu.VMEM((LINE, 2, rows, width - first), BF16),
            pltpu.VMEM((LINE, rows, first), BF16),
            pltpu.VMEM((LINE, rows, width - first), BF16),
            pltpu.VMEM((LINE, rows, width), BF16),
            pltpu.VMEM((LINE, rows, width), BF16),
            dma((LINE, 2, 2)),
            dma((LINE, 2, 2)),
            dma((LINE, 2, 2)),
            dma((LINE, 3)),
            dma((LINE, 3)),
            dma((LINE, 3)),
            dma((LINE, 3)),
            dma((LINE,)),
            dma((LINE,)),
            dma((LINE,)),
            dma((LINE,)),
        ]

    def owner(self, group):
        near = jnp.where(self.a < LINE // 2, LINE - 1 - group, group)
        inner = [[3, 0, 2, 1], [0, 3, 1, 2]]
        pick = lambda order: sum(jnp.where(group == g, order[g], 0) for g in range(LINE))
        return jnp.where(self.a == 1, pick(inner[0]), jnp.where(self.a == 2, pick(inner[1]), near))

    def remote(self, src, dst, send, recv, device):
        return pltpu.make_async_remote_copy(src, dst, send, recv, device_id=device, device_id_type=MESH_ID)

    def source(self, group, pb, py, core):
        row = pl.multiple_of(((self.owner(group) * 2 + pb) * 2 + core) * self.rows, self.rows)
        return self.src.at[py, pl.ds(row, self.rows), :]

    def load(self, group, pb, py):
        return pltpu.make_async_copy(
            self.source(group, pb, py, self.core), self.acc.at[group, pb, py], self.load_sem.at[group, pb, py]
        )

    def to_mate(self, group, pb, py):
        return self.remote(
            self.source(group, pb, py, 1 - self.core),
            self.mates.at[group, pb, py],
            self.mate_send.at[group, pb, py],
            self.mate_recv.at[group, pb, py],
            target(self.a, self.b, 1 - self.core, self.y),
        )

    def low(self):
        return pl.ds(0, self.first)

    def high(self):
        return pl.ds(self.first, self.width - self.first)

    def over_y(self, group, k):
        device = target(self.a, self.b, self.core, 1 - self.y)
        if k < 2:
            src, dst = self.acc.at[group, k, 1 - self.y, :, self.low()], self.y_two.at[group, k]
        else:
            src, dst = self.acc.at[group, self.b, 1 - self.y, :, self.high()], self.y_one.at[group]
        return self.remote(src, dst, self.y_send.at[group, k], self.y_recv.at[group, k], device)

    def over_x(self, group, k):
        device = target(self.a, 1 - self.b, self.core, self.y)
        if k < 2:
            src, dst = self.acc.at[group, 1 - self.b, k, :, self.high()], self.x_two.at[group, k]
        else:
            src, dst = self.acc.at[group, 1 - self.b, self.y, :, self.low()], self.x_one.at[group]
        return self.remote(src, dst, self.x_send.at[group, k], self.x_recv.at[group, k], device)

    def along(self, group, step):
        pa = self.owner(group)
        src = self.acc.at[group, self.b, self.y]
        device = target(self.a + step, self.b, self.core, self.y)
        buffer, send, recv = (
            (self.up, self.up_send, self.up_recv) if step > 0 else (self.down, self.down_send, self.down_recv)
        )
        return self.remote(src, buffer.at[pa], send.at[pa], recv.at[pa], device)

    def add(self, ref, other):
        tile = 16

        @pl.loop(0, self.rows // tile)
        def _(i):
            span = pl.ds(pl.multiple_of(i * tile, tile), tile)
            ref[span, :] += other[span, :]

    def begin(self):
        for group in range(LINE):
            for pb in range(2):
                for py in range(2):
                    self.to_mate(group, pb, py).start()
                    self.load(group, pb, py).start()

    def first_stage(self, group):
        for pb in range(2):
            for py in range(2):
                self.load(group, pb, py).wait()
                self.to_mate(group, pb, py).wait_recv()
                self.add(self.acc.at[group, pb, py], self.mates.at[group, pb, py])
        for k in range(2):
            self.over_y(group, k).start()
            self.over_x(group, k).start()

    def second_stage(self, group):
        for k in range(2):
            self.over_y(group, k).wait_recv()
            self.add(self.acc.at[group, k, self.y, :, self.low()], self.y_two.at[group, k])
            self.over_x(group, k).wait_recv()
            self.add(self.acc.at[group, self.b, k, :, self.high()], self.x_two.at[group, k])
        self.over_x(group, 2).start()
        self.over_y(group, 2).start()

    def third_stage(self, group):
        mine = self.acc.at[group, self.b, self.y]
        self.over_x(group, 2).wait_recv()
        self.add(mine.at[:, self.low()], self.x_one.at[group])
        self.over_y(group, 2).wait_recv()
        self.add(mine.at[:, self.high()], self.y_one.at[group])
        pa = self.owner(group)

        @pl.when((self.a == 0) & (pa > 0))
        def _():
            self.along(group, 1).start()

        @pl.when((self.a == LINE - 1) & (pa < LINE - 1))
        def _():
            self.along(group, -1).start()

    def line_stage(self, group):
        mine = self.acc.at[group, self.b, self.y]
        pa = self.owner(group)

        @pl.when((self.a > 0) & (pa > self.a))
        def _():
            self.along(group, 1).wait_recv()
            self.add(mine, self.up.at[pa])
            self.along(group, 1).start()

        @pl.when((self.a < LINE - 1) & (pa < self.a))
        def _():
            self.along(group, -1).wait_recv()
            self.add(mine, self.down.at[pa])
            self.along(group, -1).start()

    def step(self, t):
        for stage, start in ((self.first_stage, 1), (self.second_stage, 3), (self.third_stage, 5), (self.line_stage, 7)):

            @pl.when((lax.rem(t, 2) == 1) & (t >= start) & (t < start + 2 * LINE))
            def _():
                stage((t - start) // 2)

    def end(self):
        last = LINE - 1
        mine = self.acc.at[last, self.b, self.y]

        @pl.when(self.a > 0)
        def _():
            self.along(last, 1).wait_recv()
            self.add(mine, self.up.at[self.a])

        @pl.when(self.a < LINE - 1)
        def _():
            self.along(last, -1).wait_recv()
            self.add(mine, self.down.at[self.a])

        self.out[...] = mine[...].astype(F32)
        for group in range(LINE):
            self.mates_sent(group)
            for k in range(3):
                self.over_y(group, k).wait_send()
                self.over_x(group, k).wait_send()
            pa = self.owner(group)

            @pl.when(pa > self.a)
            def _():
                self.along(group, 1).wait_send()

            @pl.when(pa < self.a)
            def _():
                self.along(group, -1).wait_send()


    def mates_sent(self, group):
        for pb in range(2):
            for py in range(2):
                self.to_mate(group, pb, py).wait_send()


class Place(Reduce):
    def load(self, group, pb):
        return pltpu.make_async_copy(
            self.source(group, pb, self.core), self.acc.at[group, pb, self.core], self.load_sem.at[group, pb, 0]
        )

    def source(self, group, pb, core):
        row = pl.multiple_of(((self.owner(group) * 2 + pb) * 2 + core) * self.rows, self.rows)
        return self.src.at[pl.ds(row, self.rows), :]

    def to_mate(self, group, pb, py):
        return self.remote(
            self.source(group, pb, 1 - self.core),
            self.acc.at[group, pb, py],
            self.mate_send.at[group, pb, 0],
            self.mate_recv.at[group, pb, 0],
            target(self.a, self.b, 1 - self.core, self.y),
        )

    def begin(self):
        for group in range(LINE):
            for pb in range(2):
                self.to_mate(group, pb, self.core).start()
                self.load(group, pb).start()

    def first_stage(self, group):
        for pb in range(2):
            self.load(group, pb).wait()
            self.to_mate(group, pb, 1 - self.core).wait_recv()
        for k in range(2):
            self.over_y(group, k).start()
            self.over_x(group, k).start()

    def mates_sent(self, group):
        for pb in range(2):
            self.to_mate(group, pb, self.core).wait_send()


def leave_kernel(
    back_ref,
    rows_ref,
    o_hbm,
    low_hbm,
    low_in_hbm,
    weights_hbm,
    grad_hbm,
    y_hbm,
    y_in_hbm,
    sums_ref,
    grad_ref,
    y_ref,
    o_ref,
    low_ref,
    weights_ref,
    total,
    grads,
    mate_out,
    mate_in,
    cross_out,
    cross_in,
    load_sem,
    mate_send,
    mate_recv,
    cross_send,
    cross_recv,
    *scratch,
):
    a, b, core, y = place()
    moves = core != y
    half = total.shape[0]
    wide = back_ref.shape[1]
    loads = [
        pltpu.make_async_copy(low_hbm, low_ref.at[pl.ds(0, half)], load_sem.at[0]),
        pltpu.make_async_copy(low_in_hbm, low_ref.at[pl.ds(half, half)], load_sem.at[1]),
        pltpu.make_async_copy(o_hbm, o_ref, load_sem.at[2]),
        pltpu.make_async_copy(weights_hbm.at[core], weights_ref, load_sem.at[3]),
        pltpu.make_async_copy(grad_hbm, total, load_sem.at[4]),
    ]
    for load in loads:
        load.start()
    moved = pltpu.make_async_copy(y_in_hbm, y_ref, load_sem.at[5])
    stayed = pltpu.make_async_copy(y_hbm, y_ref, load_sem.at[5])

    @pl.when(moves)
    def _():
        moved.start()

    @pl.when(jnp.logical_not(moves))
    def _():
        stayed.start()

    greet(moves)
    reduce = Place(grads, sums_ref, scratch)
    loads[3].wait()
    mate_out[...] = dot(back_ref[half:, :], weights_ref[...], NT).astype(BF16)
    exchange = reduce.remote(mate_out, mate_in, mate_send, mate_recv, target(a, b, 1 - core, y))
    exchange.start()
    loads[4].wait()
    total[...] += dot(back_ref[:half, :], weights_ref[...], NT)
    exchange.wait()
    total[...] += mate_in[...].astype(F32)
    crossing = reduce.remote(cross_out, cross_in, cross_send, cross_recv, target(a, b, y, core))

    @pl.when(moves)
    def _():
        cross_out[...] = total[...].astype(BF16)
        crossing.start()

    rows = rows_ref[...]
    for start in range(0, wide, 3 * LANES):
        span = slice(start, start + 3 * LANES)
        grads[:, span] = dot(rows, back_ref[:, span], TN).astype(BF16)
    for load in loads[:3]:
        load.wait()
    grads[:, wide:] = dot(low_ref[...], o_ref[...], TN).astype(BF16)
    reduce.begin()

    @pl.loop(1, reduce.STEPS)
    def _(t):
        reduce.step(t)

    @pl.when(moves)
    def _():
        crossing.wait()
        grad_ref[...] = cross_in[...].astype(F32)
        moved.wait()

    @pl.when(jnp.logical_not(moves))
    def _():
        grad_ref[...] = total[...]
        stayed.wait()

    reduce.end()


def leave(back, rows_all, o, low, low_in, weights, grad_one, y_own, y_in, collective_id):
    tokens, width = rows_all.shape
    half = tokens // 2
    wide, out_wide = back.shape[1], o.shape[1]
    rows = width // (4 * LINE)
    vmem, anywhere = pl.BlockSpec(memory_space=pltpu.VMEM), pl.BlockSpec(memory_space=pl.ANY)
    dma = pltpu.SemaphoreType.DMA
    return pl.pallas_call(
        leave_kernel,
        in_specs=[vmem, vmem] + [anywhere] * 7,
        out_specs=[vmem] * 3,
        out_shape=[
            jax.ShapeDtypeStruct((rows, wide + out_wide), F32),
            jax.ShapeDtypeStruct((half, width), F32),
            jax.ShapeDtypeStruct((half, width), BF16),
        ],
        scratch_shapes=[
            pltpu.VMEM((tokens, out_wide), BF16),
            pltpu.VMEM((tokens, width), BF16),
            pltpu.VMEM((width, wide), BF16),
            pltpu.VMEM((half, width), F32),
            pltpu.VMEM((width, wide + out_wide), BF16),
            pltpu.VMEM((half, width), BF16),
            pltpu.VMEM((half, width), BF16),
            pltpu.VMEM((half, width), BF16),
            pltpu.VMEM((half, width), BF16),
            dma((6,)),
            dma,
            dma,
            dma,
            dma,
            *Reduce.scratch(rows, wide + out_wide, FIRST_TILES * LANES),
        ],
        compiler_params=pltpu.CompilerParams(
            collective_id=collective_id, has_side_effects=True, vmem_limit_bytes=VMEM_BYTES
        ),
        cost_estimate=pl.CostEstimate(
            flops=4 * tokens * width * (wide + out_wide), bytes_accessed=40 * half * width, transcendentals=0
        ),
        name="leave",
    )(back, rows_all, o, low, low_in, weights, grad_one, y_own, y_in)


FF_ROWS = 256


def normalize(hidden):
    centered = hidden - jnp.mean(hidden, axis=-1, keepdims=True)
    inv_std = lax.rsqrt(jnp.mean(centered * centered, axis=-1, keepdims=True) + EPSILON)
    return centered * inv_std, inv_std


def normalize_back(grad_y, normed, inv_std, gain):
    scaled = grad_y * gain
    return inv_std * (
        scaled
        - jnp.mean(scaled, axis=-1, keepdims=True)
        - normed * jnp.mean(scaled * normed, axis=-1, keepdims=True)
    )


def feed_kernel(
    core_ref,
    x_ref,
    o_ref,
    o_in_ref,
    out_own_ref,
    out_mate_ref,
    vectors_ref,
    d_ref,
    d_in_ref,
    weights_ref,
    y_ref,
    grad_ref,
    grad_low_ref,
    do_ref,
    do_mate_ref,
    sums_ref,
    weights,
    acts,
    turned,
    factor,
    silus,
    vectors,
    totals,
    sems,
    *,
    blocks,
):
    step = pl.program_id(0)
    half_ff = weights.shape[2] // 3

    def fetch(half, kind):
        columns = pl.ds(kind * half_ff, half_ff)
        return pltpu.make_async_copy(
            weights_ref.at[half, :, columns], weights.at[half, :, columns], sems.at[half, kind]
        )

    @pl.when(step == 0)
    def _():
        for half in range(2):
            for kind in range(3):
                fetch(half, kind).start()
        vectors[...] = vectors_ref[0].astype(F32).T[:8]
        totals[...] = jnp.zeros_like(totals)

    @pl.when(step < blocks)
    def _():
        def weight(half, kind):
            return weights[half, :, kind * half_ff : (kind + 1) * half_ff]

        def ready(half, kinds):
            @pl.when(step == 0)
            def _():
                for kind in kinds:
                    fetch(half, kind).wait()

        rows = pl.ds(pl.multiple_of(step * FF_ROWS, FF_ROWS), FF_ROWS)
        gain_one, bias_one, gain_two, bias_two = (vectors[k : k + 1, :] for k in range(4))
        attn = dot(o_ref[...], out_own_ref[0], NT) + dot(o_in_ref[...], out_mate_ref[0], NT)
        first_hat, first_inv = normalize(x_ref[...].astype(F32) + attn)
        middle = first_hat * gain_one + bias_one
        middle_low = middle.astype(BF16)
        turned[0, :, rows] = middle_low.T
        mlp = middle
        for half in range(2):
            columns = slice(half * half_ff, (half + 1) * half_ff)
            ready(half, (0, 1))
            gate = dot(middle_low, weight(half, 0))
            up = dot(middle_low, weight(half, 1))
            sig = jax.nn.sigmoid(gate)
            silu = gate * sig
            hidden = (silu * up).astype(BF16)
            acts[2, rows, columns] = hidden
            silus[:, columns] = silu
            factor[:, columns] = up * sig * (1.0 + gate * (1.0 - sig))
            ready(half, (2,))
            mlp = mlp + dot(hidden, weight(half, 2), NT)
        second_hat, second_inv = normalize(mlp)
        y_ref[...] = (second_hat * gain_two + bias_two).astype(BF16)
        d = jnp.where(core_ref[1] == 1, d_in_ref[...], d_ref[...]).astype(F32)
        grad_two = normalize_back(d, second_hat, second_inv, gain_two)
        totals[2:3, :] += jnp.sum(d * second_hat, axis=0, keepdims=True)
        totals[3:4, :] += jnp.sum(d, axis=0, keepdims=True)
        grad_low = grad_two.astype(BF16)
        turned[1, :, rows] = grad_low.T
        grad_middle = grad_two
        for half in range(2):
            columns = slice(half * half_ff, (half + 1) * half_ff)
            grad_hidden = dot(grad_low, weight(half, 2))
            grad_gate = (grad_hidden * factor[:, columns]).astype(BF16)
            grad_up = (grad_hidden * silus[:, columns]).astype(BF16)
            acts[0, rows, columns] = grad_gate
            acts[1, rows, columns] = grad_up
            grad_middle = grad_middle + dot(grad_gate, weight(half, 0), NT) + dot(grad_up, weight(half, 1), NT)
        totals[0:1, :] += jnp.sum(grad_middle * first_hat, axis=0, keepdims=True)
        totals[1:2, :] += jnp.sum(grad_middle, axis=0, keepdims=True)
        grad_one = normalize_back(grad_middle, first_hat, first_inv, gain_one)
        grad_ref[...] = grad_one
        first_low = grad_one.astype(BF16)
        grad_low_ref[...] = first_low
        do_ref[...] = dot(first_low, out_own_ref[0]).astype(BF16)
        do_mate_ref[...] = dot(first_low, out_mate_ref[0]).astype(BF16)

    cut = half_ff // 2
    index = jnp.maximum(step - blocks, 0)
    half, place_in = index // 7, lax.rem(index, 7)

    @pl.when((step >= blocks) & (place_in < 6))
    def _():
        kind = place_in // 2
        start = pl.multiple_of(half * half_ff + lax.rem(place_in, 2) * cut, cut)
        sums_ref[0] = dot(turned[kind // 2], acts[kind, :, pl.ds(start, cut)]).astype(BF16)

    @pl.when((step >= blocks) & (place_in == 6))
    def _():
        sums_ref[0, :, :LANES] = totals[...].T.astype(BF16)


def feed(place_id, rows_all, o, o_in, ff_w, d_out, d_in):
    half_len, width = d_out.shape
    half_cols = o.shape[1]
    half_ff = 4 * half_cols
    blocks = half_len // FF_ROWS
    token = lambda columns: pl.BlockSpec((FF_ROWS, columns), lambda i, c: (jnp.minimum(i, blocks - 1), 0))

    def place_sums(i, c):
        k = jnp.maximum(i - blocks, 0)
        return (k // 7, 0, lax.rem(k, 7))

    return pl.pallas_call(
        functools.partial(feed_kernel, blocks=blocks),
        grid_spec=pltpu.PrefetchScalarGridSpec(
            num_scalar_prefetch=1,
            grid=(blocks + 14,),
            in_specs=[
                token(width),
                token(half_cols),
                token(half_cols),
                pl.BlockSpec((1, width, half_cols), lambda i, c: (c[0], 0, 12)),
                pl.BlockSpec((1, width, half_cols), lambda i, c: (1 - c[0], 0, 12)),
                pl.BlockSpec((1, width, LANES), lambda i, c: (0, 0, 13 * half_cols // LANES)),
                token(width),
                token(width),
                pl.BlockSpec(memory_space=pl.ANY),
            ],
            out_specs=[
                token(width),
                token(width),
                token(width),
                token(half_cols),
                token(half_cols),
                pl.BlockSpec((1, width, half_ff // 2), place_sums),
            ],
            scratch_shapes=[
                pltpu.VMEM((2, width, 3 * half_ff), BF16),
                pltpu.VMEM((3, half_len, 2 * half_ff), BF16),
                pltpu.VMEM((2, width, half_len), BF16),
                pltpu.VMEM((FF_ROWS, 2 * half_ff), F32),
                pltpu.VMEM((FF_ROWS, 2 * half_ff), F32),
                pltpu.VMEM((8, width), F32),
                pltpu.VMEM((LANES, width), F32),
                pltpu.SemaphoreType.DMA((2, 3)),
            ],
        ),
        out_shape=[
            jax.ShapeDtypeStruct((half_len, width), BF16),
            jax.ShapeDtypeStruct((half_len, width), F32),
            jax.ShapeDtypeStruct((half_len, width), BF16),
            jax.ShapeDtypeStruct((half_len, half_cols), BF16),
            jax.ShapeDtypeStruct((half_len, half_cols), BF16),
            jax.ShapeDtypeStruct((2, width, 3 * half_ff + LANES), BF16),
        ],
        compiler_params=pltpu.CompilerParams(vmem_limit_bytes=FEED_VMEM),
        cost_estimate=pl.CostEstimate(
            flops=half_len * width * (2 * 2 * width + 6 * 6 * half_ff),
            bytes_accessed=4 * ff_w.size + 20 * half_len * width,
            transcendentals=2 * half_len * half_ff,
        ),
        name="feed",
    )(place_id, rows_all, o, o_in, ff_w, ff_w, ff_w, d_out, d_in, ff_w)


def on_device(
    mp,
    devices,
    inputs,
    segments,
    w_qkv,
    w_out,
    first_gain,
    first_bias,
    w_gate,
    w_up,
    w_down,
    second_gain,
    second_bias,
    d_out,
):
    group = ("chip", "mp")
    swaps = [(a * mp + b, b * mp + a) for a in range(2) for b in range(mp) if a != b]

    core, y = lax.axis_index("core"), lax.axis_index("mp")
    moves = core != y

    def cross_in(tensor):
        return lax.ppermute(tensor, ("core", "mp"), swaps)

    def cross(tensor):
        return jnp.where(moves, cross_in(tensor), tensor)

    def mate(tensor):
        return lax.ppermute(tensor, "core", [(0, 1), (1, 0)])

    shard, half_cols = w_qkv.shape[1], w_qkv.shape[2]
    pairs = half_cols // LANES
    half_ff = w_gate.shape[1]
    half_len, width = inputs.shape
    turn = core * half_len

    attn_shard = w_qkv.reshape(3, shard, pairs, LANES).transpose(1, 2, 0, 3).reshape(shard, 3 * half_cols)
    vectors = jnp.stack([first_gain, first_bias, second_gain, second_bias], axis=1)
    pad = jnp.zeros((shard, LANES - 4), BF16)
    ff_shard = jnp.concatenate([w_gate, w_up, w_down.T, w_out.T, vectors, pad], axis=1)
    labels = cross(segments)
    attn_w, rows_all = enter(attn_shard, inputs, devices, cross, mate, 1)
    d_in = cross_in(d_out)
    after = jnp.zeros((), BF16)
    ff_w = lax.all_gather(ff_shard + after, ("mp", "chip", "core"), axis=0, tiled=True)
    ff_w = ff_w.reshape(2, width, -1)

    labels = jnp.where(core == 0, labels, jnp.roll(labels, half_len))
    cos, sin = (jnp.asarray(t) for t in rope_tables())
    place_id = jnp.stack([core, moves.astype(jnp.int32)])

    qkv = project(place_id, rows_all, attn_w, cos, sin)
    o, lse = attend(qkv, labels, turn)
    o_in = mate(o[half_len:])
    y_own, grad_one, grad_one_low, do, do_mate, ff_sum = feed(place_id, rows_all, o, o_in, ff_w, d_out, d_in)
    y_in = cross_in(y_own)
    do_in = mate(do_mate)
    grad_low_in = mate(grad_one_low)
    cos_turned, sin_turned = (
        jnp.where(core == 0, t, jnp.roll(t, half_len, axis=0)) for t in (cos, sin)
    )
    back, ff_grad = attend_back(qkv, o, do, do_in, lse, labels, cos_turned, sin_turned, ff_sum, devices, 2)
    if devices == 8 * LINE:
        attn_grad, grad_inputs, outputs = leave(
            back, rows_all, o, grad_one_low, grad_low_in, attn_w, grad_one, y_own, y_in, 3
        )
    else:
        weight_grad = dot(rows_all, back, TN).astype(BF16)
        grad_out_t = dot(jnp.concatenate([grad_one_low, grad_low_in]), o, TN).astype(BF16)
        attn_sum = jnp.concatenate([weight_grad, grad_out_t], axis=1)
        attn_sum = jnp.where(jnp.arange(2)[:, None, None] == core, attn_sum[None], 0)
        attn_grad = scatter_sum(attn_sum)
        grad_rows = dot(back, lax.dynamic_index_in_dim(attn_w, core, 0, False), NT)
        grad_rows = grad_rows[:half_len] + mate(grad_rows[half_len:].astype(BF16)).astype(F32)
        grad_inputs = grad_one + grad_rows
        grad_inputs = jnp.where(moves, cross_in(grad_inputs.astype(BF16)).astype(F32), grad_inputs)
        outputs = jnp.where(moves, y_in, y_own)

    grad_qkv = (
        attn_grad[:, : 3 * half_cols]
        .reshape(shard, pairs, 3, LANES)
        .transpose(2, 0, 1, 3)
        .reshape(3, shard, half_cols)
    )
    grad_out = attn_grad[:, 3 * half_cols :].T
    grad_gate, grad_up, grad_down_t = (ff_grad[:, k * half_ff : (k + 1) * half_ff] for k in range(3))
    grad_vectors = ff_grad[:, 3 * half_ff : 3 * half_ff + 4]
    return (
        outputs,
        grad_inputs,
        grad_qkv,
        grad_out,
        grad_vectors[:, 0],
        grad_vectors[:, 1],
        grad_gate,
        grad_up,
        grad_down_t.T,
        grad_vectors[:, 2],
        grad_vectors[:, 3],
    )


def solution(mesh):
    dp, mp = mesh.shape["dp"], mesh.shape["mp"]
    split = Mesh(mesh.devices.reshape(dp // 2, 2, mp), ("chip", "core", "mp"))
    rows = P(("chip", "core", "mp"), None)
    vector = P(("chip", "core"))
    columns = P(("chip", "core"), "mp")
    turned = P("mp", ("chip", "core"))
    stacked = P(None, ("chip", "core"), "mp")
    return jax.shard_map(
        functools.partial(on_device, mp, dp * mp),
        mesh=split,
        in_specs=(
            rows,
            vector,
            stacked,
            turned,
            vector,
            vector,
            columns,
            columns,
            turned,
            vector,
            vector,
            rows,
        ),
        out_specs=(
            rows,
            rows,
            stacked,
            turned,
            vector,
            vector,
            columns,
            columns,
            turned,
            vector,
            vector,
        ),
        check_vma=False,
    )
```

```python
import functools

import jax
import jax.numpy as jnp
import numpy as np
from jax import lax
from jax.experimental import pallas as pl
from jax.experimental.pallas import tpu as pltpu
from jax.sharding import Mesh
from jax.sharding import PartitionSpec as P

HEAD_DIM = 64
SEQ_LEN = 2048
LANES = 128
EPSILON = 1e-12
ROPE_BASE = 1000.0
MASKED = -10000.0
SCALE = HEAD_DIM**-0.5
F32 = jnp.float32
BF16 = jnp.bfloat16
NT = (((1,), (1,)), ((), ()))
NN = (((1,), (0,)), ((), ()))
TN = (((0,), (0,)), ((), ()))
VMEM_BYTES = 60 << 20
FEED_VMEM = 62 << 20
FWD_Q, FWD_K = 1024, 512
BWD_K = 512
ROW_BLOCK = 256
MESH_ID = pl.DeviceIdType.MESH
LINE = 4
FIRST_TILES = 2
ROW_PARTS = LINE


def dot(left, right, dims=NN):
    return lax.dot_general(left, right, dims, preferred_element_type=F32)


def rope_tables():
    half = HEAD_DIM // 2
    frequency = ROPE_BASE ** (-2.0 * np.arange(half) / HEAD_DIM)
    angles = np.arange(SEQ_LEN)[:, None] * frequency[None, :]
    cos, sin = np.cos(angles), np.sin(angles)
    heads = LANES // HEAD_DIM
    return (
        np.tile(np.concatenate([cos, cos], 1), (1, heads)).astype(np.float32),
        np.tile(np.concatenate([-sin, sin], 1), (1, heads)).astype(np.float32),
    )


def half_swap(tile):
    lane = lax.broadcasted_iota(jnp.int32, (1, LANES), 1)
    half = HEAD_DIM // 2
    return jnp.where(
        lane % HEAD_DIM < half,
        pltpu.roll(tile, LANES - half, 1),
        pltpu.roll(tile, half, 1),
    )


def project_kernel(core_ref, x_ref, w_ref, cos_ref, sin_ref, out_ref, *, pairs):
    x = x_ref[...]
    cos, sin = cos_ref[...], sin_ref[...]
    for pair in range(pairs):
        base = pair * 3 * LANES
        tile = dot(x, w_ref[0, :, base : base + 3 * LANES])
        for kind in range(2):
            part = tile[:, kind * LANES : (kind + 1) * LANES]
            out_ref[:, base + kind * LANES : base + (kind + 1) * LANES] = (
                part * cos + half_swap(part) * sin
            ).astype(BF16)
        out_ref[:, base + 2 * LANES : base + 3 * LANES] = tile[:, 2 * LANES :].astype(BF16)


def project(core, rows, weights, cos, sin):
    tokens, depth = rows.shape
    wide = weights.shape[2]
    steps = tokens // ROW_BLOCK

    def turned(step, core_ref):
        return (lax.rem(step + core_ref[0] * (steps // 2), steps), 0)

    return pl.pallas_call(
        functools.partial(project_kernel, pairs=wide // (3 * LANES)),
        grid_spec=pltpu.PrefetchScalarGridSpec(
            num_scalar_prefetch=1,
            grid=(steps,),
            in_specs=[
                pl.BlockSpec((ROW_BLOCK, depth), lambda i, c: (i, 0)),
                pl.BlockSpec((1, depth, wide), lambda i, c: (c[0], 0, 0)),
                pl.BlockSpec((ROW_BLOCK, LANES), turned),
                pl.BlockSpec((ROW_BLOCK, LANES), turned),
            ],
            out_specs=pl.BlockSpec((ROW_BLOCK, wide), lambda i, c: (i, 0)),
        ),
        out_shape=jax.ShapeDtypeStruct((tokens, wide), BF16),
        compiler_params=pltpu.CompilerParams(vmem_limit_bytes=VMEM_BYTES),
        cost_estimate=pl.CostEstimate(
            flops=2 * tokens * depth * wide,
            bytes_accessed=2 * tokens * (depth + wide) + 2 * depth * wide,
            transcendentals=0,
        ),
        name="project",
    )(core, rows, weights, cos, sin)


def block_range(labels, block, other, turn):
    blocks = labels.shape[0] // block
    valid = labels >= 0
    tiles = labels.reshape(blocks, block)
    first, last = tiles[:, 0], jnp.max(tiles, axis=1)
    low = jnp.sum((valid[None] & (labels[None] < first[:, None])).astype(jnp.int32), 1)
    high = jnp.sum((valid[None] & (labels[None] <= last[:, None])).astype(jnp.int32), 1)
    offset = (labels.shape[0] - turn) // other
    return low // other + offset, jnp.where(high > low, (high + other - 1) // other, low // other) + offset


def attend_kernel(low_ref, high_ref, q_ref, k_ref, v_ref, key_ref, query_ref, o_ref, lse_ref, v_turned):
    tokens = q_ref.shape[0]
    key_blocks = tokens // FWD_K
    lane = lax.broadcasted_iota(jnp.int32, (1, LANES), 1)
    zero = jnp.zeros((), BF16)
    v_turned[...] = v_ref[...].T

    @pl.loop(0, tokens // FWD_Q)
    def _(i):
        q0 = pl.multiple_of(i * FWD_Q, FWD_Q)
        scaled = q_ref[pl.ds(q0, FWD_Q), :] * jnp.asarray(SCALE, BF16)
        halves = (
            jnp.where(lane < HEAD_DIM, scaled, zero),
            jnp.where(lane >= HEAD_DIM, scaled, zero),
        )
        query_label = query_ref[:, pl.ds(q0, FWD_Q)]

        def body(j, carry):
            k0 = pl.multiple_of(lax.rem(j, key_blocks) * FWD_K, FWD_K)
            k = k_ref[pl.ds(k0, FWD_K), :]
            same = key_ref[pl.ds(k0, FWD_K), :] == query_label
            scores = [dot(k, half, NT) for half in halves]
            out = []
            for h in range(2):
                top, total, acc = carry[h]
                s = jnp.where(same, scores[h], -1e30)
                new_top = jnp.maximum(top, jnp.max(s, axis=0, keepdims=True))
                fade = jnp.exp(top - new_top)
                e = jnp.exp(s - new_top)
                total = fade * total + jnp.sum(e, axis=0, keepdims=True)
                part = dot(v_turned[h * HEAD_DIM : (h + 1) * HEAD_DIM, pl.ds(k0, FWD_K)], e.astype(BF16))
                out.append((new_top, total, acc * fade + part))
            return tuple(out)

        start = (
            jnp.full((1, FWD_Q), MASKED, F32),
            jnp.zeros((1, FWD_Q), F32),
            jnp.zeros((HEAD_DIM, FWD_Q), F32),
        )
        ended = lax.fori_loop(low_ref[i], high_ref[i], body, (start, start))
        out = []
        for h in range(2):
            top, total, acc = ended[h]
            norm = jnp.maximum(total, 1.0)
            out.append(acc / norm)
            lse_ref[0, pl.ds(h, 1), pl.ds(q0, FWD_Q)] = top + jnp.log(norm)
        o_ref[pl.ds(q0, FWD_Q), :] = jnp.concatenate(out, 0).T.astype(BF16)


def attend(qkv, labels, turn):
    tokens = qkv.shape[0]
    pairs = qkv.shape[1] // (3 * LANES)
    low, high = block_range(labels, FWD_Q, FWD_K, turn)
    queries = jnp.where(labels < 0, -2, labels)
    whole = lambda shape: pl.BlockSpec(shape, lambda p, *_: (0,) * len(shape))
    part = lambda kind: pl.BlockSpec((tokens, LANES), lambda p, *_: (0, 3 * p + kind))
    return pl.pallas_call(
        attend_kernel,
        grid_spec=pltpu.PrefetchScalarGridSpec(
            num_scalar_prefetch=2,
            grid=(pairs,),
            in_specs=[part(0), part(1), part(2), whole((tokens, 1)), whole((1, tokens))],
            out_specs=[
                pl.BlockSpec((tokens, LANES), lambda p, *_: (0, p)),
                pl.BlockSpec((1, 2, tokens), lambda p, *_: (p, 0, 0)),
            ],
            scratch_shapes=[pltpu.VMEM((LANES, tokens), BF16)],
        ),
        out_shape=[
            jax.ShapeDtypeStruct((tokens, pairs * LANES), BF16),
            jax.ShapeDtypeStruct((pairs, 2, tokens), F32),
        ],
        compiler_params=pltpu.CompilerParams(vmem_limit_bytes=VMEM_BYTES),
        cost_estimate=pl.CostEstimate(
            flops=pairs * 8 * tokens * tokens * LANES,
            bytes_accessed=pairs * 4 * tokens * LANES * 2,
            transcendentals=pairs * 2 * tokens * tokens,
        ),
        name="attend",
    )(low, high, qkv, qkv, qkv, labels[:, None], queries[None])


def attend_back_step(t, refs, scratch):
    o_all, do_all, lse_ref, key_ref, query_ref, cos_ref, sin_ref, rows_ref, q_all, grads_ref = refs
    dq_turned, inner, k_turned, held = scratch
    tokens = q_all.shape[0]
    steps = 2 * tokens // BWD_K
    pair, place_in = t // steps, lax.rem(t, steps)
    j, h = place_in // 2, lax.rem(place_in, 2)
    half = tokens // 2
    turn = lax.axis_index("core") * half
    lane = lax.broadcasted_iota(jnp.int32, (1, LANES), 1)
    zero = jnp.zeros((), BF16)
    mine = lane // HEAD_DIM == h

    def lanes(kind):
        return pl.ds(pl.multiple_of((pair * 3 + kind) * LANES, LANES), LANES)

    own = pl.ds(pl.multiple_of(pair * LANES, LANES), LANES)
    feats = pl.ds(pl.multiple_of(h * HEAD_DIM, HEAD_DIM), HEAD_DIM)

    def unrope(tile, start, rows):
        at = pl.ds(pl.multiple_of(lax.rem(start + turn, tokens), rows), rows)
        return (tile * cos_ref[at, :] - half_swap(tile) * sin_ref[at, :]).astype(BF16)

    @pl.when(place_in == 0)
    def _():
        k_turned[...] = q_all[:, lanes(1)].T
        product = (o_all[:, own].astype(F32) * do_all[:, own].astype(F32)).T
        inner[0:1, :] = jnp.sum(product[:HEAD_DIM], axis=0, keepdims=True)
        inner[1:2, :] = jnp.sum(product[HEAD_DIM:], axis=0, keepdims=True)
        dq_turned[...] = jnp.zeros_like(dq_turned)

    start = pl.multiple_of(j * BWD_K, BWD_K)
    key_rows = pl.ds(start, BWD_K)
    k = jnp.where(mine, q_all[key_rows, lanes(1)], zero)
    v = jnp.where(mine, q_all[key_rows, lanes(2)], zero)
    q, do = q_all[:, lanes(0)], do_all[:, own]
    s = dot(k, q, NT)
    p = jnp.exp(s * SCALE - lse_ref[pair, pl.ds(h, 1), :])
    p = jnp.where(key_ref[key_rows, :] == query_ref[...], p, 0.0)
    dp = dot(v, do, NT)
    ds = (p * (dp - inner[pl.ds(h, 1), :])).astype(BF16)
    dv = dot(p.astype(BF16), do)
    dk = dot(ds, q)
    dq_turned[feats, :] += dot(k_turned[feats, key_rows], ds)
    results = (unrope(dk * SCALE, start, BWD_K), dv.astype(BF16))

    @pl.when(h == 0)
    def _():
        for kind in range(2):
            held[kind] = results[kind]

    @pl.when(h == 1)
    def _():
        for kind in range(2):
            q_all[key_rows, lanes(1 + kind)] = jnp.where(lane < HEAD_DIM, held[kind], results[kind])

    @pl.when(place_in == steps - 1)
    def _():
        for at in (0, half):
            rows = pl.ds(at, half)
            q_all[rows, lanes(0)] = unrope(dq_turned[:, rows].T * SCALE, at, half)
        span = pl.ds(pl.multiple_of(pair * 3 * LANES, LANES), 3 * LANES)
        grads_ref[:, span] = dot(rows_ref[...], q_all[:, span], TN).astype(BF16)


def attend_back_kernel(*refs, remote):
    refs, steps = list(refs), 2 * refs[0].shape[0] // BWD_K * (refs[0].shape[1] // (3 * LANES))
    inputs, refs = refs[:10], refs[10:]
    do_all, do_sem, scratch = refs[-2], refs[-1], None
    refs = refs[:-2]
    half = inputs[2].shape[0]
    takes = [
        pltpu.make_async_copy(inputs[2 + k], do_all.at[pl.ds(k * half, half)], do_sem.at[k]) for k in range(2)
    ]
    takes.append(pltpu.make_async_copy(inputs[0], refs[1 if remote else 0], do_sem.at[2]))
    inputs = [inputs[1], do_all, *inputs[4:]]
    for take in takes:
        take.start()
    if not remote:
        out_ref, grads_ref, scratch = refs[0], refs[1], refs[2:]
        for take in takes:
            take.wait()

        @pl.loop(0, steps)
        def _(t):
            attend_back_step(t, (*inputs, out_ref, grads_ref), scratch)

        return
    grads, out_ref, grads_ref, sums, scratch = refs[0], refs[1], refs[2], refs[3], refs[4:]
    greet(False)
    reduce = Reduce(grads, sums, scratch[4:])
    reduce.begin()
    for take in takes:
        take.wait()

    @pl.loop(0, max(steps, reduce.STEPS))
    def _(t):
        reduce.step(t)

        @pl.when(t < steps)
        def _():
            attend_back_step(t, (*inputs, out_ref, grads_ref), scratch[:4])

    reduce.end()


def attend_back(qkv, o, do, do_in, lse, labels, cos, sin, rows_all, grads, devices, collective_id):
    tokens, wide = qkv.shape
    remote = devices == 8 * LINE
    queries = jnp.where(labels < 0, -2, labels)
    vmem = pl.BlockSpec(memory_space=pltpu.VMEM)
    operands = [qkv, o, do, do_in, lse, labels[:, None], queries[None], cos, sin, rows_all]
    out_shape = [
        jax.ShapeDtypeStruct((tokens, wide), BF16),
        jax.ShapeDtypeStruct((rows_all.shape[1], wide), BF16),
    ]
    scratch = [
        pltpu.VMEM((LANES, tokens), F32),
        pltpu.VMEM((8, tokens), F32),
        pltpu.VMEM((LANES, tokens), BF16),
        pltpu.VMEM((2, BWD_K, LANES), BF16),
    ]
    anywhere = pl.BlockSpec(memory_space=pl.ANY)
    in_specs = [anywhere, vmem, anywhere, anywhere] + [vmem] * 6
    params = dict(vmem_limit_bytes=VMEM_BYTES)
    if remote:
        rows, width = 2 * grads.shape[1] // devices, grads.shape[2]
        operands.append(grads)
        in_specs.append(pl.BlockSpec(memory_space=pl.ANY))
        out_shape.append(jax.ShapeDtypeStruct((rows, width), F32))
        scratch += Reduce.scratch(rows, width, (width // LANES + 1) // 2 * LANES)
        params.update(collective_id=collective_id, has_side_effects=True)
    scratch += [pltpu.VMEM((tokens, wide // 3), BF16), pltpu.SemaphoreType.DMA((3,))]
    out = pl.pallas_call(
        functools.partial(attend_back_kernel, remote=remote),
        in_specs=in_specs,
        out_specs=[vmem] * len(out_shape),
        out_shape=out_shape,
        scratch_shapes=scratch,
        compiler_params=pltpu.CompilerParams(**params),
        cost_estimate=pl.CostEstimate(
            flops=wide // (3 * LANES) * 20 * tokens * tokens * LANES,
            bytes_accessed=8 * tokens * wide,
            transcendentals=wide // (3 * LANES) * 2 * tokens * tokens,
        ),
        name="attend_back",
    )(*operands)
    return tuple(out) if remote else (*out, scatter_sum(grads))


def scatter_sum(grads):
    flat = grads.reshape(-1, grads.shape[2])
    return lax.psum_scatter(flat, ("mp", "chip", "core"), scatter_dimension=0, tiled=True).astype(F32)


def place():
    chip = lax.axis_index("chip")
    return chip // 2, lax.rem(chip, 2), lax.axis_index("core"), lax.axis_index("mp")


def target(a, b, core, y):
    return {"chip": a * 2 + b, "core": core, "mp": y}


def greet(moves):
    a, b, core, y = place()
    barrier = pltpu.get_barrier_semaphore()

    def signal(device):
        pl.semaphore_signal(barrier, inc=1, device_id=device, device_id_type=MESH_ID)

    signal(target(a, 1 - b, core, y))
    signal(target(a, b, core, 1 - y))
    signal(target(a, b, 1 - core, y))

    @pl.when(a > 0)
    def _():
        signal(target(a - 1, b, core, y))

    @pl.when(a < LINE - 1)
    def _():
        signal(target(a + 1, b, core, y))

    @pl.when(moves)
    def _():
        signal(target(a, b, y, core))

    edges = jnp.where(a > 0, 1, 0) + jnp.where(a < LINE - 1, 1, 0) + jnp.where(moves, 1, 0)
    pl.semaphore_wait(barrier, 3 + edges)


class Gather:
    def __init__(self, src, dst, send, recv, local, first_tiles):
        self.src, self.dst, self.send, self.recv, self.local = src, dst, send, recv, local
        self.rows, self.width = src.shape
        tiles = self.width // LANES
        first = (first_tiles or tiles // 2) * LANES
        self.columns = [(0, first), (first, self.width - first)]
        self.a, self.b, self.core, self.y = place()

    def span(self, half):
        start, size = (0, self.width) if half is None else self.columns[half]
        return pl.ds(start, size)

    def at(self, piece, core=None):
        pa, pb, py, half = piece
        core = self.core if core is None else core
        row = pl.multiple_of(((pa * 2 + pb) * 2 + core) * self.rows, self.rows)
        return self.dst.at[py, pl.ds(row, self.rows), self.span(half)]

    def own_copy(self):
        return pltpu.make_async_copy(self.src, self.at((self.a, self.b, self.y, None)), self.local)

    def start(self, piece, slot, device, mine=False):
        source = self.src.at[:, self.span(piece[3])] if mine else self.at(piece)
        pltpu.make_async_remote_copy(
            source, self.at(piece), self.send.at[slot], self.recv.at[slot], device_id=device, device_id_type=MESH_ID
        ).start()

    def handle(self, piece, slot, core=None):
        ref = self.at(piece, core)
        return pltpu.make_async_remote_copy(
            ref,
            ref,
            self.send.at[slot],
            self.recv.at[slot],
            device_id=target(self.a, self.b, 1 - self.core, self.y),
            device_id_type=MESH_ID,
        )

    def arrived(self, piece, slot, core=None):
        self.handle(piece, slot, core).wait_recv()

    def sent(self, piece, slot):
        self.handle(piece, slot).wait_send()

    def to_x(self, piece, slot, mine=False):
        self.start(piece, slot, target(self.a, 1 - self.b, self.core, self.y), mine)

    def to_y(self, piece, slot, mine=False):
        self.start(piece, slot, target(self.a, self.b, self.core, 1 - self.y), mine)

    def to_mate(self, piece, slot, mine=False):
        self.start(piece, slot, target(self.a, self.b, 1 - self.core, self.y), mine)

    def to_line(self, piece, slot, step, mine=False):
        self.start(piece, slot, target(self.a + step, self.b, self.core, self.y), mine)

    def spread(self, pa, rank, mine=False):
        b, y = self.b, self.y
        self.to_x((pa, b, y, 0), 6 + rank, mine)
        self.to_y((pa, b, y, 1), 18 + rank, mine)
        for half in range(2):
            self.to_mate((pa, b, y, half), 30 + 2 * rank + half, mine)
        self.to_y((pa, b, y, 0), 22 + rank, mine)
        self.to_x((pa, b, y, 1), 10 + rank, mine)

    def begin(self):
        a, b, y = self.a, self.b, self.y
        piece = (a, b, y, None)

        @pl.when(a < LINE - 1)
        def _():
            self.to_line(piece, 0, 1, True)

        @pl.when(a > 0)
        def _():
            self.to_line(piece, 3, -1, True)

        self.spread(a, 0, True)
        self.own_copy().start()

    def hop(self, h):
        a, b, y = self.a, self.b, self.y

        @pl.when(a - h >= 0)
        def _():
            self.arrived((a - h, b, y, None), h - 1)
            if h < LINE - 1:

                @pl.when(a < LINE - 1)
                def _():
                    self.to_line((a - h, b, y, None), h, 1)

            self.spread(a - h, LINE - h)

        @pl.when(a + h < LINE)
        def _():
            self.arrived((a + h, b, y, None), 2 + h)
            if h < LINE - 1:

                @pl.when(a > 0)
                def _():
                    self.to_line((a + h, b, y, None), 3 + h, -1)

            self.spread(a + h, h)

    def ranks(self):
        return [(rank, lax.rem(self.a + rank, LINE)) for rank in range(LINE)]

    def turn(self):
        b, y = self.b, self.y
        for rank, pa in self.ranks():
            self.arrived((pa, 1 - b, y, 0), 6 + rank)
            self.to_y((pa, 1 - b, y, 0), 26 + rank)
            self.to_mate((pa, 1 - b, y, 0), 38 + rank)
            self.arrived((pa, b, 1 - y, 1), 18 + rank)
            self.to_x((pa, b, 1 - y, 1), 14 + rank)
            self.to_mate((pa, b, 1 - y, 1), 42 + rank)

    def last(self):
        b, y = self.b, self.y
        for rank, pa in self.ranks():
            for far in range(2):
                pb, py = (b, 1 - b)[far], (y, 1 - y)[far]
                self.arrived((pa, pb, 1 - y, 0), 22 + 4 * far + rank)
                self.to_mate((pa, pb, 1 - y, 0), 46 + 4 * far + rank)
                self.arrived((pa, 1 - b, py, 1), 10 + 4 * far + rank)
                self.to_mate((pa, 1 - b, py, 1), 54 + 4 * far + rank)

    def end(self):
        a, b, y = self.a, self.b, self.y
        other = 1 - self.core
        for rank, pa in self.ranks():
            pieces = [((pa, b, y, 0), 30 + 2 * rank), ((pa, b, y, 1), 31 + 2 * rank)]
            pieces += [((pa, 1 - b, y, 0), 38 + rank), ((pa, b, 1 - y, 1), 42 + rank)]
            for far in range(2):
                pb, py = (b, 1 - b)[far], (y, 1 - y)[far]
                pieces += [((pa, pb, 1 - y, 0), 46 + 4 * far + rank), ((pa, 1 - b, py, 1), 54 + 4 * far + rank)]
            for piece, slot in pieces:
                self.arrived(piece, slot, other)
                self.sent(piece, slot)
            self.sent((pa, b, y, 0), 6 + rank)
            self.sent((pa, b, y, 1), 18 + rank)
            self.sent((pa, b, y, 1), 10 + rank)
            self.sent((pa, b, 1 - y, 1), 14 + rank)
            self.sent((pa, b, y, 0), 22 + rank)
            self.sent((pa, 1 - b, y, 0), 26 + rank)

        @pl.when(a < LINE - 1)
        def _():
            self.sent((a, b, y, None), 0)

        @pl.when(a > 0)
        def _():
            self.sent((a, b, y, None), 3)

        for h in range(1, LINE - 1):

            @pl.when((a - h >= 0) & (a < LINE - 1))
            def _():
                self.sent((a - h, b, y, None), h)

            @pl.when((a + h < LINE) & (a > 0))
            def _():
                self.sent((a + h, b, y, None), 3 + h)

        self.own_copy().wait()


def front_kernel(
    attn_src,
    rows,
    ff_src,
    labels_ref,
    cos_ref,
    sin_ref,
    attn_w,
    rows_all,
    ff_w,
    qkv_ref,
    o_ref,
    o_in,
    lse_ref,
    attn_send,
    attn_recv,
    attn_local,
    ff_send,
    ff_recv,
    ff_local,
    row_send,
    row_recv,
    label_sems,
    o_send,
    o_recv,
    load_sems,
    held,
    labels_in,
    query_labels,
    key_labels,
    weights,
    x_ref,
    v_turned,
    state,
    acc,
):
    a, b, core, y = place()
    half = rows.shape[0]
    tokens = 2 * half
    part = half // ROW_PARTS
    moves = core != y
    turn = core * half
    greet(moves)
    labels_across = pltpu.make_async_remote_copy(
        labels_ref,
        labels_in,
        label_sems.at[0],
        label_sems.at[1],
        device_id=target(a, b, y, core),
        device_id_type=MESH_ID,
    )

    def crossing(k):
        span = pl.ds(k * part, part)
        return pltpu.make_async_remote_copy(
            rows.at[span],
            rows_all.at[span],
            row_send.at[0, k],
            row_recv.at[0, k],
            device_id=target(a, b, y, core),
            device_id_type=MESH_ID,
        )

    def to_mate(source, k):
        return pltpu.make_async_remote_copy(
            source.at[pl.ds(k * part, part)],
            rows_all.at[pl.ds(half + k * part, part)],
            row_send.at[1, k],
            row_recv.at[1, k],
            device_id=target(a, b, 1 - core, y),
            device_id_type=MESH_ID,
        )

    take = pltpu.make_async_copy(rows, held, row_recv.at[2, 0])
    stay = pltpu.make_async_copy(held, rows_all.at[pl.ds(0, half)], row_recv.at[2, 1])

    def send(k):
        @pl.when(moves)
        def _():
            crossing(k).start()

        @pl.when(jnp.logical_not(moves))
        def _():
            to_mate(rows, k).start()

    def hand_on(k):
        @pl.when(moves)
        def _():
            crossing(k).wait()
            to_mate(rows_all, k).start()

    @pl.when(moves)
    def _():
        labels_across.start()

    @pl.when(jnp.logical_not(moves))
    def _():
        take.start()

    gather = Gather(attn_src, attn_w, attn_send, attn_recv, attn_local, FIRST_TILES)
    later = Gather(ff_src, ff_w, ff_send, ff_recv, ff_local, None)
    gather.begin()
    send(0)

    @pl.when(jnp.logical_not(moves))
    def _():
        take.wait()
        stay.start()

    for h in range(1, LINE):
        gather.hop(h)
        send(h)
    later.begin()
    hand_on(0)
    hand_on(1)
    gather.turn()
    hand_on(2)
    hand_on(3)
    gather.last()

    @pl.when(jnp.logical_not(moves))
    def _():
        stay.wait()

    for k in range(ROW_PARTS):
        to_mate(rows_all, k).wait()
    gather.end()
    later.hop(1)
    load_w = pltpu.make_async_copy(attn_w.at[core], weights, load_sems.at[0])
    load_x = pltpu.make_async_copy(rows_all, x_ref, load_sems.at[1])
    load_w.start()
    load_x.start()

    @pl.when(moves)
    def _():
        labels_across.wait()

    labels = jnp.where(moves, labels_in[...], labels_ref[...])
    labels = jnp.where(core == 1, jnp.concatenate([labels[:, half:], labels[:, :half]], axis=1), labels)
    query_labels[...] = jnp.where(labels < 0, -2, labels)
    key_labels[...] = jnp.broadcast_to(labels, (LANES, tokens)).T
    load_w.wait()
    load_x.wait()
    pairs = weights.shape[1] // (3 * LANES)

    @pl.loop(0, tokens // ROW_BLOCK)
    def _(i):
        at = pl.ds(pl.multiple_of(i * ROW_BLOCK, ROW_BLOCK), ROW_BLOCK)
        table = pl.ds(pl.multiple_of(lax.rem(i * ROW_BLOCK + turn, tokens), ROW_BLOCK), ROW_BLOCK)
        x = x_ref[at, :]
        cos, sin = cos_ref[table, :], sin_ref[table, :]
        for pair in range(pairs):
            base = pair * 3 * LANES
            tile = dot(x, weights[:, base : base + 3 * LANES])
            for kind in range(2):
                span = slice(base + kind * LANES, base + (kind + 1) * LANES)
                flat = tile[:, kind * LANES : (kind + 1) * LANES]
                qkv_ref[at, span] = (flat * cos + half_swap(flat) * sin).astype(BF16)
            qkv_ref[at, base + 2 * LANES : base + 3 * LANES] = tile[:, 2 * LANES :].astype(BF16)

    later.hop(2)
    lane = lax.broadcasted_iota(jnp.int32, (1, LANES), 1)
    zero = jnp.zeros((), BF16)
    blocks = tokens // FWD_K

    def o_to_mate(pair):
        span = pl.ds(pl.multiple_of(pair * LANES, LANES), LANES)
        return pltpu.make_async_remote_copy(
            o_ref.at[pl.ds(half, half), span],
            o_in.at[:, span],
            o_send.at[pair],
            o_recv.at[pair],
            device_id=target(a, b, 1 - core, y),
            device_id_type=MESH_ID,
        )

    @pl.loop(0, pairs * blocks)
    def _(t):
        pair, j = t // blocks, lax.rem(t, blocks)

        def lanes(kind):
            return pl.ds(pl.multiple_of((pair * 3 + kind) * LANES, LANES), LANES)

        @pl.when(t == blocks)
        def _():
            later.hop(3)

        @pl.when(t == 2 * blocks)
        def _():
            later.turn()

        @pl.when(j == 0)
        def _():
            v_turned[...] = qkv_ref[:, lanes(2)].T
            for h in range(2):
                state[2 * h : 2 * h + 1, :] = jnp.full((1, tokens), MASKED, F32)
                state[2 * h + 1 : 2 * h + 2, :] = jnp.zeros((1, tokens), F32)
            acc[...] = jnp.zeros_like(acc)

        keys = pl.ds(pl.multiple_of(j * FWD_K, FWD_K), FWD_K)
        k = qkv_ref[keys, lanes(1)]
        q = qkv_ref[:, lanes(0)] * jnp.asarray(SCALE, BF16)
        same = key_labels[keys, :1] == query_labels[...]
        for h in range(2):
            feats = slice(h * HEAD_DIM, (h + 1) * HEAD_DIM)
            s = dot(k, jnp.where(lane // HEAD_DIM == h, q, zero), NT)
            s = jnp.where(same, s, -1e30)
            top, total = state[2 * h : 2 * h + 1, :], state[2 * h + 1 : 2 * h + 2, :]
            new_top = jnp.maximum(top, jnp.max(s, axis=0, keepdims=True))
            fade = jnp.exp(top - new_top)
            e = jnp.exp(s - new_top)
            state[2 * h : 2 * h + 1, :] = new_top
            state[2 * h + 1 : 2 * h + 2, :] = fade * total + jnp.sum(e, axis=0, keepdims=True)
            acc[feats, :] = acc[feats, :] * fade + dot(v_turned[feats, keys], e.astype(BF16))

        @pl.when(j == blocks - 1)
        def _():
            for h in range(2):
                feats = slice(h * HEAD_DIM, (h + 1) * HEAD_DIM)
                norm = jnp.maximum(state[2 * h + 1 : 2 * h + 2, :], 1.0)
                acc[feats, :] = acc[feats, :] / norm
                lse_ref[pair, pl.ds(h, 1), :] = state[2 * h : 2 * h + 1, :] + jnp.log(norm)
            o_ref[:, pl.ds(pl.multiple_of(pair * LANES, LANES), LANES)] = acc[...].T.astype(BF16)
            o_to_mate(pair).start()

    later.last()
    later.end()
    for pair in range(pairs):
        o_to_mate(pair).wait()


def front(attn_shard, rows, ff_shard, segments, cos, sin, devices, collective_id):
    shard, wide = attn_shard.shape
    half, width = rows.shape
    tokens, out_wide = 2 * half, wide // 3
    vmem, anywhere = pl.BlockSpec(memory_space=pltpu.VMEM), pl.BlockSpec(memory_space=pl.ANY)
    dma = pltpu.SemaphoreType.DMA
    return pl.pallas_call(
        front_kernel,
        in_specs=[anywhere, anywhere, anywhere, vmem, vmem, vmem],
        out_specs=[anywhere, anywhere, anywhere, vmem, vmem, anywhere, vmem],
        out_shape=[
            jax.ShapeDtypeStruct((2, devices // 2 * shard, wide), BF16),
            jax.ShapeDtypeStruct((tokens, width), BF16),
            jax.ShapeDtypeStruct((2, devices // 2 * shard, ff_shard.shape[1]), BF16),
            jax.ShapeDtypeStruct((tokens, wide), BF16),
            jax.ShapeDtypeStruct((tokens, out_wide), BF16),
            jax.ShapeDtypeStruct((half, out_wide), BF16),
            jax.ShapeDtypeStruct((out_wide // LANES, 2, tokens), F32),
        ],
        scratch_shapes=[
            dma((62,)),
            dma((62,)),
            dma,
            dma((62,)),
            dma((62,)),
            dma,
            dma((2, ROW_PARTS)),
            dma((3, ROW_PARTS)),
            dma((2,)),
            dma((out_wide // LANES,)),
            dma((out_wide // LANES,)),
            dma((2,)),
            pltpu.VMEM((half, width), BF16),
            pltpu.VMEM((1, tokens), jnp.int32),
            pltpu.VMEM((1, tokens), jnp.int32),
            pltpu.VMEM((tokens, LANES), jnp.int32),
            pltpu.VMEM((width, wide), BF16),
            pltpu.VMEM((tokens, width), BF16),
            pltpu.VMEM((LANES, tokens), BF16),
            pltpu.VMEM((8, tokens), F32),
            pltpu.VMEM((LANES, tokens), F32),
        ],
        compiler_params=pltpu.CompilerParams(
            collective_id=collective_id, has_side_effects=True, vmem_limit_bytes=VMEM_BYTES
        ),
        cost_estimate=pl.CostEstimate(
            flops=2 * tokens * width * wide + 8 * tokens * tokens * out_wide,
            bytes_accessed=40 * half * width,
            transcendentals=2 * out_wide // LANES * tokens * tokens,
        ),
        name="front",
    )(attn_shard, rows, ff_shard, segments.reshape(1, tokens), cos, sin)


def enter(shard, rows, cross, mate):
    weights = lax.all_gather(shard, ("mp", "chip", "core"), axis=0, tiled=True)
    own = cross(rows)
    return weights.reshape(2, -1, shard.shape[1]), jnp.concatenate([own, mate(own)], axis=0)


class Reduce:
    SPACING = 4
    OFFSETS = (1, 5, 9, 13)
    STEPS = OFFSETS[-1] + SPACING * (LINE - 1) + 1

    def __init__(self, src, out, scratch):
        self.src, self.out = src, out
        (
            self.acc,
            self.mates,
            self.y_two,
            self.x_two,
            self.x_one,
            self.y_one,
            self.up,
            self.down,
            self.load_sem,
            self.mate_send,
            self.mate_recv,
            self.y_send,
            self.y_recv,
            self.x_send,
            self.x_recv,
            self.up_send,
            self.up_recv,
            self.down_send,
            self.down_recv,
        ) = scratch
        self.rows, self.width = self.acc.shape[3:]
        self.first = self.y_two.shape[3]
        self.a, self.b, self.core, self.y = place()

    @staticmethod
    def scratch(rows, width, first):
        dma = pltpu.SemaphoreType.DMA
        return [
            pltpu.VMEM((LINE, 2, 2, rows, width), BF16),
            pltpu.VMEM((LINE, 2, 2, rows, width), BF16),
            pltpu.VMEM((LINE, 2, rows, first), BF16),
            pltpu.VMEM((LINE, 2, rows, width - first), BF16),
            pltpu.VMEM((LINE, rows, first), BF16),
            pltpu.VMEM((LINE, rows, width - first), BF16),
            pltpu.VMEM((LINE, rows, width), BF16),
            pltpu.VMEM((LINE, rows, width), BF16),
            dma((LINE, 2, 2)),
            dma((LINE, 2, 2)),
            dma((LINE, 2, 2)),
            dma((LINE, 3)),
            dma((LINE, 3)),
            dma((LINE, 3)),
            dma((LINE, 3)),
            dma((LINE,)),
            dma((LINE,)),
            dma((LINE,)),
            dma((LINE,)),
        ]

    def owner(self, group):
        near = jnp.where(self.a < LINE // 2, LINE - 1 - group, group)
        inner = [[3, 0, 2, 1], [0, 3, 1, 2]]
        pick = lambda order: sum(jnp.where(group == g, order[g], 0) for g in range(LINE))
        return jnp.where(self.a == 1, pick(inner[0]), jnp.where(self.a == 2, pick(inner[1]), near))

    def remote(self, src, dst, send, recv, device):
        return pltpu.make_async_remote_copy(src, dst, send, recv, device_id=device, device_id_type=MESH_ID)

    def source(self, group, pb, py, core):
        row = pl.multiple_of(((self.owner(group) * 2 + pb) * 2 + core) * self.rows, self.rows)
        return self.src.at[py, pl.ds(row, self.rows), :]

    def load(self, group, pb, py):
        return pltpu.make_async_copy(
            self.source(group, pb, py, self.core), self.acc.at[group, pb, py], self.load_sem.at[group, pb, py]
        )

    def to_mate(self, group, pb, py):
        return self.remote(
            self.source(group, pb, py, 1 - self.core),
            self.mates.at[group, pb, py],
            self.mate_send.at[group, pb, py],
            self.mate_recv.at[group, pb, py],
            target(self.a, self.b, 1 - self.core, self.y),
        )

    def low(self):
        return pl.ds(0, self.first)

    def high(self):
        return pl.ds(self.first, self.width - self.first)

    def over_y(self, group, k):
        device = target(self.a, self.b, self.core, 1 - self.y)
        if k < 2:
            src, dst = self.acc.at[group, k, 1 - self.y, :, self.low()], self.y_two.at[group, k]
        else:
            src, dst = self.acc.at[group, self.b, 1 - self.y, :, self.high()], self.y_one.at[group]
        return self.remote(src, dst, self.y_send.at[group, k], self.y_recv.at[group, k], device)

    def over_x(self, group, k):
        device = target(self.a, 1 - self.b, self.core, self.y)
        if k < 2:
            src, dst = self.acc.at[group, 1 - self.b, k, :, self.high()], self.x_two.at[group, k]
        else:
            src, dst = self.acc.at[group, 1 - self.b, self.y, :, self.low()], self.x_one.at[group]
        return self.remote(src, dst, self.x_send.at[group, k], self.x_recv.at[group, k], device)

    def along(self, group, step):
        pa = self.owner(group)
        src = self.acc.at[group, self.b, self.y]
        device = target(self.a + step, self.b, self.core, self.y)
        buffer, send, recv = (
            (self.up, self.up_send, self.up_recv) if step > 0 else (self.down, self.down_send, self.down_recv)
        )
        return self.remote(src, buffer.at[pa], send.at[pa], recv.at[pa], device)

    def add(self, ref, other):
        tile = 16

        @pl.loop(0, self.rows // tile)
        def _(i):
            span = pl.ds(pl.multiple_of(i * tile, tile), tile)
            ref[span, :] += other[span, :]

    def begin(self):
        for group in range(LINE):
            for pb in range(2):
                for py in range(2):
                    self.to_mate(group, pb, py).start()
                    self.load(group, pb, py).start()

    def first_stage(self, group):
        for pb in range(2):
            for py in range(2):
                self.load(group, pb, py).wait()
                self.to_mate(group, pb, py).wait_recv()
                self.add(self.acc.at[group, pb, py], self.mates.at[group, pb, py])
        for k in range(2):
            self.over_y(group, k).start()
            self.over_x(group, k).start()

    def second_stage(self, group):
        for k in range(2):
            self.over_y(group, k).wait_recv()
            self.add(self.acc.at[group, k, self.y, :, self.low()], self.y_two.at[group, k])
            self.over_x(group, k).wait_recv()
            self.add(self.acc.at[group, self.b, k, :, self.high()], self.x_two.at[group, k])
        self.over_x(group, 2).start()
        self.over_y(group, 2).start()

    def third_stage(self, group):
        mine = self.acc.at[group, self.b, self.y]
        self.over_x(group, 2).wait_recv()
        self.add(mine.at[:, self.low()], self.x_one.at[group])
        self.over_y(group, 2).wait_recv()
        self.add(mine.at[:, self.high()], self.y_one.at[group])
        pa = self.owner(group)

        @pl.when((self.a == 0) & (pa > 0))
        def _():
            self.along(group, 1).start()

        @pl.when((self.a == LINE - 1) & (pa < LINE - 1))
        def _():
            self.along(group, -1).start()

    def line_stage(self, group):
        mine = self.acc.at[group, self.b, self.y]
        pa = self.owner(group)

        @pl.when((self.a > 0) & (pa > self.a))
        def _():
            self.along(group, 1).wait_recv()
            self.add(mine, self.up.at[pa])
            self.along(group, 1).start()

        @pl.when((self.a < LINE - 1) & (pa < self.a))
        def _():
            self.along(group, -1).wait_recv()
            self.add(mine, self.down.at[pa])
            self.along(group, -1).start()

    def step(self, t):
        stages = (self.first_stage, self.second_stage, self.third_stage, self.line_stage)
        for stage, start in zip(stages, self.OFFSETS):
            passed = t - start

            @pl.when((passed >= 0) & (passed < self.SPACING * LINE) & (lax.rem(passed, self.SPACING) == 0))
            def _():
                stage(passed // self.SPACING)

    def end(self):
        last = LINE - 1
        mine = self.acc.at[last, self.b, self.y]

        @pl.when(self.a > 0)
        def _():
            self.along(last, 1).wait_recv()
            self.add(mine, self.up.at[self.a])

        @pl.when(self.a < LINE - 1)
        def _():
            self.along(last, -1).wait_recv()
            self.add(mine, self.down.at[self.a])

        self.out[...] = mine[...].astype(F32)
        for group in range(LINE):
            self.mates_sent(group)
            for k in range(3):
                self.over_y(group, k).wait_send()
                self.over_x(group, k).wait_send()
            pa = self.owner(group)

            @pl.when(pa > self.a)
            def _():
                self.along(group, 1).wait_send()

            @pl.when(pa < self.a)
            def _():
                self.along(group, -1).wait_send()


    def mates_sent(self, group):
        for pb in range(2):
            for py in range(2):
                self.to_mate(group, pb, py).wait_send()


class Place(Reduce):
    SPACING = 1
    OFFSETS = (0, 1, 2, 3)
    STEPS = OFFSETS[-1] + SPACING * (LINE - 1) + 1

    def load(self, group, pb):
        return pltpu.make_async_copy(
            self.source(group, pb, self.core), self.acc.at[group, pb, self.core], self.load_sem.at[group, pb, 0]
        )

    def source(self, group, pb, core):
        row = pl.multiple_of(((self.owner(group) * 2 + pb) * 2 + core) * self.rows, self.rows)
        return self.src.at[pl.ds(row, self.rows), :]

    def to_mate(self, group, pb, py):
        return self.remote(
            self.source(group, pb, 1 - self.core),
            self.acc.at[group, pb, py],
            self.mate_send.at[group, pb, 0],
            self.mate_recv.at[group, pb, 0],
            target(self.a, self.b, 1 - self.core, self.y),
        )

    def begin(self):
        for group in range(LINE):
            for pb in range(2):
                self.to_mate(group, pb, self.core).start()
                self.load(group, pb).start()

    def first_stage(self, group):
        for pb in range(2):
            self.load(group, pb).wait()
            self.to_mate(group, pb, 1 - self.core).wait_recv()
        for k in range(2):
            self.over_y(group, k).start()
            self.over_x(group, k).start()

    def mates_sent(self, group):
        for pb in range(2):
            self.to_mate(group, pb, self.core).wait_send()


def leave_kernel(
    back_ref,
    done_hbm,
    o_hbm,
    low_hbm,
    low_in_hbm,
    weights_hbm,
    grad_hbm,
    sums_ref,
    grad_ref,
    o_ref,
    low_ref,
    weights_ref,
    total,
    grads,
    mate_out,
    mate_in,
    cross_out,
    cross_in,
    load_sem,
    mate_send,
    mate_recv,
    cross_send,
    cross_recv,
    *scratch,
):
    a, b, core, y = place()
    moves = core != y
    half = total.shape[0]
    wide = back_ref.shape[1]
    loads = [
        pltpu.make_async_copy(done_hbm, grads.at[:, pl.ds(0, wide)], load_sem.at[6]),
        pltpu.make_async_copy(low_hbm, low_ref.at[pl.ds(0, half)], load_sem.at[0]),
        pltpu.make_async_copy(low_in_hbm, low_ref.at[pl.ds(half, half)], load_sem.at[1]),
        pltpu.make_async_copy(o_hbm, o_ref, load_sem.at[2]),
        pltpu.make_async_copy(weights_hbm.at[core], weights_ref, load_sem.at[3]),
        pltpu.make_async_copy(grad_hbm, total, load_sem.at[4]),
    ]
    for load in loads:
        load.start()
    greet(moves)
    reduce = Place(grads, sums_ref, scratch)
    for load in loads[:4]:
        load.wait()
    grads[:, wide:] = dot(low_ref[...], o_ref[...], TN).astype(BF16)
    reduce.begin()
    loads[4].wait()
    mate_out[...] = dot(back_ref[half:, :], weights_ref[...], NT).astype(BF16)
    exchange = reduce.remote(mate_out, mate_in, mate_send, mate_recv, target(a, b, 1 - core, y))
    exchange.start()
    loads[5].wait()
    total[...] += dot(back_ref[:half, :], weights_ref[...], NT)
    exchange.wait()
    total[...] += mate_in[...].astype(F32)
    part = half // LINE

    def crossing(k):
        span = pl.ds(pl.multiple_of(k * part, part), part)
        return reduce.remote(
            cross_out.at[span], cross_in.at[span], cross_send.at[k], cross_recv.at[k], target(a, b, y, core)
        )

    @pl.when(moves)
    def _():
        cross_out[...] = total[...].astype(BF16)

    @pl.loop(0, reduce.STEPS)
    def _(t):
        reduce.step(t)

        @pl.when(moves & (t >= 1) & (t <= LINE))
        def _():
            crossing(t - 1).start()

    @pl.when(moves)
    def _():
        for k in range(LINE):
            crossing(k).wait()
        grad_ref[...] = cross_in[...].astype(F32)

    @pl.when(jnp.logical_not(moves))
    def _():
        grad_ref[...] = total[...]

    reduce.end()


def leave(back, done, o, low, low_in, weights, grad_one, collective_id):
    tokens, width = back.shape[0], grad_one.shape[1]
    half = tokens // 2
    wide, out_wide = back.shape[1], o.shape[1]
    rows = width // (4 * LINE)
    vmem, anywhere = pl.BlockSpec(memory_space=pltpu.VMEM), pl.BlockSpec(memory_space=pl.ANY)
    dma = pltpu.SemaphoreType.DMA
    return pl.pallas_call(
        leave_kernel,
        in_specs=[vmem] + [anywhere] * 6,
        out_specs=[vmem] * 2,
        out_shape=[
            jax.ShapeDtypeStruct((rows, wide + out_wide), F32),
            jax.ShapeDtypeStruct((half, width), F32),
        ],
        scratch_shapes=[
            pltpu.VMEM((tokens, out_wide), BF16),
            pltpu.VMEM((tokens, width), BF16),
            pltpu.VMEM((width, wide), BF16),
            pltpu.VMEM((half, width), F32),
            pltpu.VMEM((width, wide + out_wide), BF16),
            pltpu.VMEM((half, width), BF16),
            pltpu.VMEM((half, width), BF16),
            pltpu.VMEM((half, width), BF16),
            pltpu.VMEM((half, width), BF16),
            dma((7,)),
            dma,
            dma,
            dma((LINE,)),
            dma((LINE,)),
            *Reduce.scratch(rows, wide + out_wide, FIRST_TILES * LANES),
        ],
        compiler_params=pltpu.CompilerParams(
            collective_id=collective_id, has_side_effects=True, vmem_limit_bytes=VMEM_BYTES
        ),
        cost_estimate=pl.CostEstimate(
            flops=4 * tokens * width * (wide + out_wide), bytes_accessed=40 * half * width, transcendentals=0
        ),
        name="leave",
    )(back, done, o, low, low_in, weights, grad_one)


FF_ROWS = 256


def normalize(hidden):
    centered = hidden - jnp.mean(hidden, axis=-1, keepdims=True)
    inv_std = lax.rsqrt(jnp.mean(centered * centered, axis=-1, keepdims=True) + EPSILON)
    return centered * inv_std, inv_std


def normalize_back(grad_y, normed, inv_std, gain):
    scaled = grad_y * gain
    return inv_std * (
        scaled
        - jnp.mean(scaled, axis=-1, keepdims=True)
        - normed * jnp.mean(scaled * normed, axis=-1, keepdims=True)
    )


def feed_kernel(
    x_ref,
    o_ref,
    o_in_ref,
    out_ref,
    vectors_ref,
    d_ref,
    d_in_ref,
    weights_ref,
    y_ref,
    grad_ref,
    grad_low_ref,
    do_ref,
    do_mate_ref,
    sums_ref,
    weights,
    acts,
    turned,
    factor,
    silus,
    vectors,
    totals,
    sems,
    y_slots,
    y_send,
    y_recv,
    *,
    blocks,
    remote,
):
    step = pl.program_id(0)
    a, b, core, y = place()
    moves = core != y

    def at_home(k):
        span = pl.ds(pl.multiple_of(k * FF_ROWS, FF_ROWS), FF_ROWS)
        return pltpu.make_async_copy(y_slots.at[lax.rem(k, 2)], y_ref.at[span], y_send.at[lax.rem(k, 2)])

    def across(k):
        span = pl.ds(pl.multiple_of(k * FF_ROWS, FF_ROWS), FF_ROWS)
        return pltpu.make_async_remote_copy(
            y_slots.at[lax.rem(k, 2)],
            y_ref.at[span],
            y_send.at[lax.rem(k, 2)],
            y_recv.at[k],
            device_id=target(a, b, y, core),
            device_id_type=MESH_ID,
        )

    def each(k, move, stay):
        if remote:

            @pl.when(moves)
            def _():
                move(across(k))

            @pl.when(jnp.logical_not(moves))
            def _():
                stay(at_home(k))
        else:
            stay(at_home(k))

    if remote:

        @pl.when((step == 0) & moves)
        def _():
            barrier = pltpu.get_barrier_semaphore()
            pl.semaphore_signal(barrier, inc=1, device_id=target(a, b, y, core), device_id_type=MESH_ID)
            pl.semaphore_wait(barrier, 1)

    half_ff = weights.shape[2] // 3

    def fetch(half, kind):
        columns = pl.ds(kind * half_ff, half_ff)
        return pltpu.make_async_copy(
            weights_ref.at[half, :, columns], weights.at[half, :, columns], sems.at[half, kind]
        )

    @pl.when(step == 0)
    def _():
        for half in range(2):
            for kind in range(3):
                fetch(half, kind).start()
        vectors[...] = vectors_ref[0].astype(F32).T[:8]
        totals[...] = jnp.zeros_like(totals)

    @pl.when(step < blocks)
    def _():
        def weight(half, kind):
            return weights[half, :, kind * half_ff : (kind + 1) * half_ff]

        def ready(half, kinds):
            @pl.when(step == 0)
            def _():
                for kind in kinds:
                    fetch(half, kind).wait()

        rows = pl.ds(pl.multiple_of(step * FF_ROWS, FF_ROWS), FF_ROWS)
        gain_one, bias_one, gain_two, bias_two = (vectors[k : k + 1, :] for k in range(4))
        attn = dot(o_ref[...], out_ref[core], NT) + dot(o_in_ref[...], out_ref[1 - core], NT)
        first_hat, first_inv = normalize(x_ref[...].astype(F32) + attn)
        middle = first_hat * gain_one + bias_one
        middle_low = middle.astype(BF16)
        turned[0, :, rows] = middle_low.T
        mlp = middle
        for half in range(2):
            columns = slice(half * half_ff, (half + 1) * half_ff)
            ready(half, (0, 1))
            gate = dot(middle_low, weight(half, 0))
            up = dot(middle_low, weight(half, 1))
            sig = jax.nn.sigmoid(gate)
            silu = gate * sig
            hidden = (silu * up).astype(BF16)
            acts[2, rows, columns] = hidden
            silus[:, columns] = silu
            factor[:, columns] = up * sig * (1.0 + gate * (1.0 - sig))
            ready(half, (2,))
            mlp = mlp + dot(hidden, weight(half, 2), NT)
        second_hat, second_inv = normalize(mlp)

        @pl.when(step >= 2)
        def _():
            each(step - 2, lambda copy: copy.wait_send(), lambda copy: copy.wait())

        y_slots[lax.rem(step, 2)] = (second_hat * gain_two + bias_two).astype(BF16)
        each(step, lambda copy: copy.start(), lambda copy: copy.start())
        d = jnp.where(moves, d_in_ref[...], d_ref[...]).astype(F32)
        grad_two = normalize_back(d, second_hat, second_inv, gain_two)
        totals[2:3, :] += jnp.sum(d * second_hat, axis=0, keepdims=True)
        totals[3:4, :] += jnp.sum(d, axis=0, keepdims=True)
        grad_low = grad_two.astype(BF16)
        turned[1, :, rows] = grad_low.T
        grad_middle = grad_two
        for half in range(2):
            columns = slice(half * half_ff, (half + 1) * half_ff)
            grad_hidden = dot(grad_low, weight(half, 2))
            grad_gate = (grad_hidden * factor[:, columns]).astype(BF16)
            grad_up = (grad_hidden * silus[:, columns]).astype(BF16)
            acts[0, rows, columns] = grad_gate
            acts[1, rows, columns] = grad_up
            grad_middle = grad_middle + dot(grad_gate, weight(half, 0), NT) + dot(grad_up, weight(half, 1), NT)
        totals[0:1, :] += jnp.sum(grad_middle * first_hat, axis=0, keepdims=True)
        totals[1:2, :] += jnp.sum(grad_middle, axis=0, keepdims=True)
        grad_one = normalize_back(grad_middle, first_hat, first_inv, gain_one)
        grad_ref[...] = grad_one
        first_low = grad_one.astype(BF16)
        grad_low_ref[...] = first_low
        do_ref[...] = dot(first_low, out_ref[core]).astype(BF16)
        do_mate_ref[...] = dot(first_low, out_ref[1 - core]).astype(BF16)

    @pl.when(step == blocks + 13)
    def _():
        for k in (blocks - 2, blocks - 1):
            each(jnp.int32(k), lambda copy: copy.wait_send(), lambda copy: copy.wait())
        if remote:

            @pl.when(moves)
            def _():
                for k in range(blocks):
                    across(jnp.int32(k)).wait_recv()

    cut = half_ff // 2
    index = jnp.maximum(step - blocks, 0)
    half, place_in = index // 7, lax.rem(index, 7)

    @pl.when((step >= blocks) & (place_in < 6))
    def _():
        kind = place_in // 2
        start = pl.multiple_of(half * half_ff + lax.rem(place_in, 2) * cut, cut)
        sums_ref[0] = dot(turned[kind // 2], acts[kind, :, pl.ds(start, cut)]).astype(BF16)

    @pl.when((step >= blocks) & (place_in == 6))
    def _():
        sums_ref[0, :, :LANES] = totals[...].T.astype(BF16)


def feed(rows_all, o, o_in, ff_w, d_out, d_in, devices, collective_id):
    half_len, width = d_out.shape
    half_cols = o.shape[1]
    half_ff = 4 * half_cols
    blocks = half_len // FF_ROWS
    token = lambda columns: pl.BlockSpec((FF_ROWS, columns), lambda i: (jnp.minimum(i, blocks - 1), 0))

    params = dict(vmem_limit_bytes=FEED_VMEM)
    if devices == 8 * LINE:
        params.update(collective_id=collective_id, has_side_effects=True)

    def place_sums(i):
        k = jnp.maximum(i - blocks, 0)
        return (k // 7, 0, lax.rem(k, 7))

    return pl.pallas_call(
        functools.partial(feed_kernel, blocks=blocks, remote=devices == 8 * LINE),
        grid_spec=pltpu.PrefetchScalarGridSpec(
            num_scalar_prefetch=0,
            grid=(blocks + 14,),
            in_specs=[
                token(width),
                token(half_cols),
                token(half_cols),
                pl.BlockSpec((2, width, half_cols), lambda i: (0, 0, 12)),
                pl.BlockSpec((1, width, LANES), lambda i: (0, 0, 13 * half_cols // LANES)),
                token(width),
                token(width),
                pl.BlockSpec(memory_space=pl.ANY),
            ],
            out_specs=[
                pl.BlockSpec(memory_space=pl.ANY),
                token(width),
                token(width),
                token(half_cols),
                token(half_cols),
                pl.BlockSpec((1, width, half_ff // 2), place_sums),
            ],
            scratch_shapes=[
                pltpu.VMEM((2, width, 3 * half_ff), BF16),
                pltpu.VMEM((3, half_len, 2 * half_ff), BF16),
                pltpu.VMEM((2, width, half_len), BF16),
                pltpu.VMEM((FF_ROWS, 2 * half_ff), F32),
                pltpu.VMEM((FF_ROWS, 2 * half_ff), F32),
                pltpu.VMEM((8, width), F32),
                pltpu.VMEM((LANES, width), F32),
                pltpu.SemaphoreType.DMA((2, 3)),
                pltpu.VMEM((2, FF_ROWS, width), BF16),
                pltpu.SemaphoreType.DMA((2,)),
                pltpu.SemaphoreType.DMA((blocks,)),
            ],
        ),
        out_shape=[
            jax.ShapeDtypeStruct((half_len, width), BF16),
            jax.ShapeDtypeStruct((half_len, width), F32),
            jax.ShapeDtypeStruct((half_len, width), BF16),
            jax.ShapeDtypeStruct((half_len, half_cols), BF16),
            jax.ShapeDtypeStruct((half_len, half_cols), BF16),
            jax.ShapeDtypeStruct((2, width, 3 * half_ff + LANES), BF16),
        ],
        compiler_params=pltpu.CompilerParams(**params),
        cost_estimate=pl.CostEstimate(
            flops=half_len * width * (2 * 2 * width + 6 * 6 * half_ff),
            bytes_accessed=4 * ff_w.size + 20 * half_len * width,
            transcendentals=2 * half_len * half_ff,
        ),
        name="feed",
    )(rows_all, o, o_in, ff_w, ff_w, d_out, d_in, ff_w)


def on_device(
    mp,
    devices,
    inputs,
    segments,
    w_qkv,
    w_out,
    first_gain,
    first_bias,
    w_gate,
    w_up,
    w_down,
    second_gain,
    second_bias,
    d_out,
):
    group = ("chip", "mp")
    swaps = [(a * mp + b, b * mp + a) for a in range(2) for b in range(mp) if a != b]

    core, y = lax.axis_index("core"), lax.axis_index("mp")
    moves = core != y

    def cross_in(tensor):
        return lax.ppermute(tensor, ("core", "mp"), swaps)

    def cross(tensor):
        return jnp.where(moves, cross_in(tensor), tensor)

    def mate(tensor):
        return lax.ppermute(tensor, "core", [(0, 1), (1, 0)])

    shard, half_cols = w_qkv.shape[1], w_qkv.shape[2]
    pairs = half_cols // LANES
    half_ff = w_gate.shape[1]
    half_len, width = inputs.shape
    turn = core * half_len

    attn_shard = w_qkv.reshape(3, shard, pairs, LANES).transpose(1, 2, 0, 3).reshape(shard, 3 * half_cols)
    vectors = jnp.stack([first_gain, first_bias, second_gain, second_bias], axis=1)
    pad = jnp.zeros((shard, LANES - 4), BF16)
    ff_shard = jnp.concatenate([w_gate, w_up, w_down.T, w_out.T, vectors, pad], axis=1)
    labels = cross(segments)
    labels = jnp.where(core == 0, labels, jnp.roll(labels, half_len))
    d_in = cross_in(d_out)
    cos, sin = (jnp.asarray(t) for t in rope_tables())
    place_id = jnp.stack([core, moves.astype(jnp.int32)])
    if devices == 8 * LINE:
        attn_w, rows_all, ff_w, qkv, o, o_in, lse = front(
            attn_shard, inputs, ff_shard, segments, cos, sin, devices, 1
        )
    else:
        attn_w, rows_all = enter(attn_shard, inputs, cross, mate)
        ff_w = lax.all_gather(ff_shard, ("mp", "chip", "core"), axis=0, tiled=True).reshape(2, width, -1)
        qkv = project(place_id, rows_all, attn_w, cos, sin)
        o, lse = attend(qkv, labels, turn)
        o_in = mate(o[half_len:])
    outputs, grad_one, grad_one_low, do, do_mate, ff_sum = feed(rows_all, o, o_in, ff_w, d_out, d_in, devices, 4)
    do_in = mate(do_mate)
    grad_low_in = mate(grad_one_low)
    back, weight_grad, ff_grad = attend_back(
        qkv, o, do, do_in, lse, labels, cos, sin, rows_all, ff_sum, devices, 2
    )
    if devices == 8 * LINE:
        attn_grad, grad_inputs = leave(
            back, weight_grad, o, grad_one_low, grad_low_in, attn_w, grad_one, 3
        )
    else:
        grad_out_t = dot(jnp.concatenate([grad_one_low, grad_low_in]), o, TN).astype(BF16)
        attn_sum = jnp.concatenate([weight_grad, grad_out_t], axis=1)
        attn_sum = jnp.where(jnp.arange(2)[:, None, None] == core, attn_sum[None], 0)
        attn_grad = scatter_sum(attn_sum)
        grad_rows = dot(back, lax.dynamic_index_in_dim(attn_w, core, 0, False), NT)
        grad_rows = grad_rows[:half_len] + mate(grad_rows[half_len:].astype(BF16)).astype(F32)
        grad_inputs = grad_one + grad_rows
        grad_inputs = jnp.where(moves, cross_in(grad_inputs.astype(BF16)).astype(F32), grad_inputs)
        outputs = cross(outputs)

    grad_qkv = (
        attn_grad[:, : 3 * half_cols]
        .reshape(shard, pairs, 3, LANES)
        .transpose(2, 0, 1, 3)
        .reshape(3, shard, half_cols)
    )
    grad_out = attn_grad[:, 3 * half_cols :].T
    grad_gate, grad_up, grad_down_t = (ff_grad[:, k * half_ff : (k + 1) * half_ff] for k in range(3))
    grad_vectors = ff_grad[:, 3 * half_ff : 3 * half_ff + 4]
    return (
        outputs,
        grad_inputs,
        grad_qkv,
        grad_out,
        grad_vectors[:, 0],
        grad_vectors[:, 1],
        grad_gate,
        grad_up,
        grad_down_t.T,
        grad_vectors[:, 2],
        grad_vectors[:, 3],
    )


def solution(mesh):
    dp, mp = mesh.shape["dp"], mesh.shape["mp"]
    split = Mesh(mesh.devices.reshape(dp // 2, 2, mp), ("chip", "core", "mp"))
    rows = P(("chip", "core", "mp"), None)
    vector = P(("chip", "core"))
    columns = P(("chip", "core"), "mp")
    turned = P("mp", ("chip", "core"))
    stacked = P(None, ("chip", "core"), "mp")
    return jax.shard_map(
        functools.partial(on_device, mp, dp * mp),
        mesh=split,
        in_specs=(
            rows,
            vector,
            stacked,
            turned,
            vector,
            vector,
            columns,
            columns,
            turned,
            vector,
            vector,
            rows,
        ),
        out_specs=(
            rows,
            rows,
            stacked,
            turned,
            vector,
            vector,
            columns,
            columns,
            turned,
            vector,
            vector,
        ),
        check_vma=False,
    )
```

```python
import functools

import jax
import jax.numpy as jnp
import numpy as np
from jax import lax
from jax.experimental import pallas as pl
from jax.experimental.pallas import tpu as pltpu
from jax.sharding import Mesh
from jax.sharding import PartitionSpec as P

HEAD_DIM = 64
SEQ_LEN = 2048
LANES = 128
EPSILON = 1e-12
ROPE_BASE = 1000.0
MASKED = -10000.0
SCALE = HEAD_DIM**-0.5
F32 = jnp.float32
BF16 = jnp.bfloat16
NT = (((1,), (1,)), ((), ()))
NN = (((1,), (0,)), ((), ()))
TN = (((0,), (0,)), ((), ()))
VMEM_BYTES = 60 << 20
FEED_VMEM = 62 << 20
FWD_Q, FWD_K = 1024, 512
BWD_K = 512
ROW_BLOCK = 256
MESH_ID = pl.DeviceIdType.MESH
LINE = 4
FIRST_TILES = 2
ROW_PARTS = LINE


def dot(left, right, dims=NN):
    return lax.dot_general(left, right, dims, preferred_element_type=F32)


def rope_tables():
    half = HEAD_DIM // 2
    frequency = ROPE_BASE ** (-2.0 * np.arange(half) / HEAD_DIM)
    angles = np.arange(SEQ_LEN)[:, None] * frequency[None, :]
    cos, sin = np.cos(angles), np.sin(angles)
    heads = LANES // HEAD_DIM
    return (
        np.tile(np.concatenate([cos, cos], 1), (1, heads)).astype(np.float32),
        np.tile(np.concatenate([-sin, sin], 1), (1, heads)).astype(np.float32),
    )


def half_swap(tile):
    lane = lax.broadcasted_iota(jnp.int32, (1, LANES), 1)
    half = HEAD_DIM // 2
    return jnp.where(
        lane % HEAD_DIM < half,
        pltpu.roll(tile, LANES - half, 1),
        pltpu.roll(tile, half, 1),
    )


def project_kernel(core_ref, x_ref, w_ref, cos_ref, sin_ref, out_ref, *, pairs):
    x = x_ref[...]
    cos, sin = cos_ref[...], sin_ref[...]
    for pair in range(pairs):
        base = pair * 3 * LANES
        tile = dot(x, w_ref[0, :, base : base + 3 * LANES])
        for kind in range(2):
            part = tile[:, kind * LANES : (kind + 1) * LANES]
            out_ref[:, base + kind * LANES : base + (kind + 1) * LANES] = (
                part * cos + half_swap(part) * sin
            ).astype(BF16)
        out_ref[:, base + 2 * LANES : base + 3 * LANES] = tile[:, 2 * LANES :].astype(BF16)


def project(core, rows, weights, cos, sin):
    tokens, depth = rows.shape
    wide = weights.shape[2]
    steps = tokens // ROW_BLOCK

    def turned(step, core_ref):
        return (lax.rem(step + core_ref[0] * (steps // 2), steps), 0)

    return pl.pallas_call(
        functools.partial(project_kernel, pairs=wide // (3 * LANES)),
        grid_spec=pltpu.PrefetchScalarGridSpec(
            num_scalar_prefetch=1,
            grid=(steps,),
            in_specs=[
                pl.BlockSpec((ROW_BLOCK, depth), lambda i, c: (i, 0)),
                pl.BlockSpec((1, depth, wide), lambda i, c: (c[0], 0, 0)),
                pl.BlockSpec((ROW_BLOCK, LANES), turned),
                pl.BlockSpec((ROW_BLOCK, LANES), turned),
            ],
            out_specs=pl.BlockSpec((ROW_BLOCK, wide), lambda i, c: (i, 0)),
        ),
        out_shape=jax.ShapeDtypeStruct((tokens, wide), BF16),
        compiler_params=pltpu.CompilerParams(vmem_limit_bytes=VMEM_BYTES),
        cost_estimate=pl.CostEstimate(
            flops=2 * tokens * depth * wide,
            bytes_accessed=2 * tokens * (depth + wide) + 2 * depth * wide,
            transcendentals=0,
        ),
        name="project",
    )(core, rows, weights, cos, sin)


def block_range(labels, block, other, turn):
    blocks = labels.shape[0] // block
    valid = labels >= 0
    tiles = labels.reshape(blocks, block)
    first, last = tiles[:, 0], jnp.max(tiles, axis=1)
    low = jnp.sum((valid[None] & (labels[None] < first[:, None])).astype(jnp.int32), 1)
    high = jnp.sum((valid[None] & (labels[None] <= last[:, None])).astype(jnp.int32), 1)
    offset = (labels.shape[0] - turn) // other
    return low // other + offset, jnp.where(high > low, (high + other - 1) // other, low // other) + offset


def attend_kernel(low_ref, high_ref, q_ref, k_ref, v_ref, key_ref, query_ref, o_ref, lse_ref, v_turned):
    tokens = q_ref.shape[0]
    key_blocks = tokens // FWD_K
    lane = lax.broadcasted_iota(jnp.int32, (1, LANES), 1)
    zero = jnp.zeros((), BF16)
    v_turned[...] = v_ref[...].T

    @pl.loop(0, tokens // FWD_Q)
    def _(i):
        q0 = pl.multiple_of(i * FWD_Q, FWD_Q)
        scaled = q_ref[pl.ds(q0, FWD_Q), :] * jnp.asarray(SCALE, BF16)
        halves = (
            jnp.where(lane < HEAD_DIM, scaled, zero),
            jnp.where(lane >= HEAD_DIM, scaled, zero),
        )
        query_label = query_ref[:, pl.ds(q0, FWD_Q)]

        def body(j, carry):
            k0 = pl.multiple_of(lax.rem(j, key_blocks) * FWD_K, FWD_K)
            k = k_ref[pl.ds(k0, FWD_K), :]
            same = key_ref[pl.ds(k0, FWD_K), :] == query_label
            scores = [dot(k, half, NT) for half in halves]
            out = []
            for h in range(2):
                top, total, acc = carry[h]
                s = jnp.where(same, scores[h], -1e30)
                new_top = jnp.maximum(top, jnp.max(s, axis=0, keepdims=True))
                fade = jnp.exp(top - new_top)
                e = jnp.exp(s - new_top)
                total = fade * total + jnp.sum(e, axis=0, keepdims=True)
                part = dot(v_turned[h * HEAD_DIM : (h + 1) * HEAD_DIM, pl.ds(k0, FWD_K)], e.astype(BF16))
                out.append((new_top, total, acc * fade + part))
            return tuple(out)

        start = (
            jnp.full((1, FWD_Q), MASKED, F32),
            jnp.zeros((1, FWD_Q), F32),
            jnp.zeros((HEAD_DIM, FWD_Q), F32),
        )
        ended = lax.fori_loop(low_ref[i], high_ref[i], body, (start, start))
        out = []
        for h in range(2):
            top, total, acc = ended[h]
            norm = jnp.maximum(total, 1.0)
            out.append(acc / norm)
            lse_ref[0, pl.ds(h, 1), pl.ds(q0, FWD_Q)] = top + jnp.log(norm)
        o_ref[pl.ds(q0, FWD_Q), :] = jnp.concatenate(out, 0).T.astype(BF16)


def attend(qkv, labels, turn):
    tokens = qkv.shape[0]
    pairs = qkv.shape[1] // (3 * LANES)
    low, high = block_range(labels, FWD_Q, FWD_K, turn)
    queries = jnp.where(labels < 0, -2, labels)
    whole = lambda shape: pl.BlockSpec(shape, lambda p, *_: (0,) * len(shape))
    part = lambda kind: pl.BlockSpec((tokens, LANES), lambda p, *_: (0, 3 * p + kind))
    return pl.pallas_call(
        attend_kernel,
        grid_spec=pltpu.PrefetchScalarGridSpec(
            num_scalar_prefetch=2,
            grid=(pairs,),
            in_specs=[part(0), part(1), part(2), whole((tokens, 1)), whole((1, tokens))],
            out_specs=[
                pl.BlockSpec((tokens, LANES), lambda p, *_: (0, p)),
                pl.BlockSpec((1, 2, tokens), lambda p, *_: (p, 0, 0)),
            ],
            scratch_shapes=[pltpu.VMEM((LANES, tokens), BF16)],
        ),
        out_shape=[
            jax.ShapeDtypeStruct((tokens, pairs * LANES), BF16),
            jax.ShapeDtypeStruct((pairs, 2, tokens), F32),
        ],
        compiler_params=pltpu.CompilerParams(vmem_limit_bytes=VMEM_BYTES),
        cost_estimate=pl.CostEstimate(
            flops=pairs * 8 * tokens * tokens * LANES,
            bytes_accessed=pairs * 4 * tokens * LANES * 2,
            transcendentals=pairs * 2 * tokens * tokens,
        ),
        name="attend",
    )(low, high, qkv, qkv, qkv, labels[:, None], queries[None])


def attend_back_step(t, refs, scratch):
    o_all, do_all, lse_ref, key_ref, query_ref, cos_ref, sin_ref, rows_ref, q_all, grads_ref = refs
    dq_turned, inner, k_turned, held = scratch
    tokens = q_all.shape[0]
    steps = 2 * tokens // BWD_K
    pair, place_in = t // steps, lax.rem(t, steps)
    j, h = place_in // 2, lax.rem(place_in, 2)
    half = tokens // 2
    turn = lax.axis_index("core") * half
    lane = lax.broadcasted_iota(jnp.int32, (1, LANES), 1)
    zero = jnp.zeros((), BF16)
    mine = lane // HEAD_DIM == h

    def lanes(kind):
        return pl.ds(pl.multiple_of((pair * 3 + kind) * LANES, LANES), LANES)

    own = pl.ds(pl.multiple_of(pair * LANES, LANES), LANES)
    feats = pl.ds(pl.multiple_of(h * HEAD_DIM, HEAD_DIM), HEAD_DIM)

    def unrope(tile, start, rows):
        at = pl.ds(pl.multiple_of(lax.rem(start + turn, tokens), rows), rows)
        return (tile * cos_ref[at, :] - half_swap(tile) * sin_ref[at, :]).astype(BF16)

    @pl.when(place_in == 0)
    def _():
        k_turned[...] = q_all[:, lanes(1)].T
        product = (o_all[:, own].astype(F32) * do_all[:, own].astype(F32)).T
        inner[0:1, :] = jnp.sum(product[:HEAD_DIM], axis=0, keepdims=True)
        inner[1:2, :] = jnp.sum(product[HEAD_DIM:], axis=0, keepdims=True)
        dq_turned[...] = jnp.zeros_like(dq_turned)

    start = pl.multiple_of(j * BWD_K, BWD_K)
    key_rows = pl.ds(start, BWD_K)
    k = jnp.where(mine, q_all[key_rows, lanes(1)], zero)
    v = jnp.where(mine, q_all[key_rows, lanes(2)], zero)
    q, do = q_all[:, lanes(0)], do_all[:, own]
    s = dot(k, q, NT)
    p = jnp.exp(s * SCALE - lse_ref[pair, pl.ds(h, 1), :])
    p = jnp.where(key_ref[key_rows, :] == query_ref[...], p, 0.0)
    dp = dot(v, do, NT)
    ds = (p * (dp - inner[pl.ds(h, 1), :])).astype(BF16)
    dv = dot(p.astype(BF16), do)
    dk = dot(ds, q)
    dq_turned[feats, :] += dot(k_turned[feats, key_rows], ds)
    results = (unrope(dk * SCALE, start, BWD_K), dv.astype(BF16))

    @pl.when(h == 0)
    def _():
        for kind in range(2):
            held[kind] = results[kind]

    @pl.when(h == 1)
    def _():
        for kind in range(2):
            q_all[key_rows, lanes(1 + kind)] = jnp.where(lane < HEAD_DIM, held[kind], results[kind])

    @pl.when(place_in == steps - 1)
    def _():
        for at in (0, half):
            rows = pl.ds(at, half)
            q_all[rows, lanes(0)] = unrope(dq_turned[:, rows].T * SCALE, at, half)
        span = pl.ds(pl.multiple_of(pair * 3 * LANES, LANES), 3 * LANES)
        grads_ref[:, span] = dot(rows_ref[...], q_all[:, span], TN).astype(BF16)


def attend_back_kernel(*refs, remote):
    refs, steps = list(refs), 2 * refs[0].shape[0] // BWD_K * (refs[0].shape[1] // (3 * LANES))
    inputs, refs = refs[:10], refs[10:]
    do_all, do_sem, scratch = refs[-2], refs[-1], None
    refs = refs[:-2]
    half = inputs[2].shape[0]
    takes = [
        pltpu.make_async_copy(inputs[2 + k], do_all.at[pl.ds(k * half, half)], do_sem.at[k]) for k in range(2)
    ]
    takes.append(pltpu.make_async_copy(inputs[0], refs[1 if remote else 0], do_sem.at[2]))
    inputs = [inputs[1], do_all, *inputs[4:]]
    for take in takes:
        take.start()
    if not remote:
        out_ref, grads_ref, scratch = refs[0], refs[1], refs[2:]
        for take in takes:
            take.wait()

        @pl.loop(0, steps)
        def _(t):
            attend_back_step(t, (*inputs, out_ref, grads_ref), scratch)

        return
    grads, out_ref, grads_ref, sums, scratch = refs[0], refs[1], refs[2], refs[3], refs[4:]
    greet(False)
    reduce = Reduce(grads, sums, scratch[4:])
    reduce.begin()
    for take in takes:
        take.wait()

    @pl.loop(0, max(steps, reduce.STEPS))
    def _(t):
        reduce.step(t)

        @pl.when(t < steps)
        def _():
            attend_back_step(t, (*inputs, out_ref, grads_ref), scratch[:4])

    reduce.end()


def attend_back(qkv, o, do, do_in, lse, labels, cos, sin, rows_all, grads, devices, collective_id):
    tokens, wide = qkv.shape
    remote = devices == 8 * LINE
    queries = jnp.where(labels < 0, -2, labels)
    vmem = pl.BlockSpec(memory_space=pltpu.VMEM)
    operands = [qkv, o, do, do_in, lse, labels[:, None], queries[None], cos, sin, rows_all]
    out_shape = [
        jax.ShapeDtypeStruct((tokens, wide), BF16),
        jax.ShapeDtypeStruct((rows_all.shape[1], wide), BF16),
    ]
    scratch = [
        pltpu.VMEM((LANES, tokens), F32),
        pltpu.VMEM((8, tokens), F32),
        pltpu.VMEM((LANES, tokens), BF16),
        pltpu.VMEM((2, BWD_K, LANES), BF16),
    ]
    anywhere = pl.BlockSpec(memory_space=pl.ANY)
    in_specs = [anywhere, vmem, anywhere, anywhere] + [vmem] * 6
    params = dict(vmem_limit_bytes=VMEM_BYTES)
    if remote:
        rows, width = 2 * grads.shape[1] // devices, grads.shape[2]
        operands.append(grads)
        in_specs.append(pl.BlockSpec(memory_space=pl.ANY))
        out_shape.append(jax.ShapeDtypeStruct((rows, width), F32))
        scratch += Reduce.scratch(rows, width, (width // LANES + 1) // 2 * LANES)
        params.update(collective_id=collective_id, has_side_effects=True)
    scratch += [pltpu.VMEM((tokens, wide // 3), BF16), pltpu.SemaphoreType.DMA((3,))]
    out = pl.pallas_call(
        functools.partial(attend_back_kernel, remote=remote),
        in_specs=in_specs,
        out_specs=[vmem] * len(out_shape),
        out_shape=out_shape,
        scratch_shapes=scratch,
        compiler_params=pltpu.CompilerParams(**params),
        cost_estimate=pl.CostEstimate(
            flops=wide // (3 * LANES) * 20 * tokens * tokens * LANES,
            bytes_accessed=8 * tokens * wide,
            transcendentals=wide // (3 * LANES) * 2 * tokens * tokens,
        ),
        name="attend_back",
    )(*operands)
    return tuple(out) if remote else (*out, scatter_sum(grads))


def scatter_sum(grads):
    flat = grads.reshape(-1, grads.shape[2])
    return lax.psum_scatter(flat, ("mp", "chip", "core"), scatter_dimension=0, tiled=True).astype(F32)


def place():
    chip = lax.axis_index("chip")
    return chip // 2, lax.rem(chip, 2), lax.axis_index("core"), lax.axis_index("mp")


def target(a, b, core, y):
    return {"chip": a * 2 + b, "core": core, "mp": y}


def greet(moves):
    a, b, core, y = place()
    barrier = pltpu.get_barrier_semaphore()

    def signal(device):
        pl.semaphore_signal(barrier, inc=1, device_id=device, device_id_type=MESH_ID)

    signal(target(a, 1 - b, core, y))
    signal(target(a, b, core, 1 - y))
    signal(target(a, b, 1 - core, y))

    @pl.when(a > 0)
    def _():
        signal(target(a - 1, b, core, y))

    @pl.when(a < LINE - 1)
    def _():
        signal(target(a + 1, b, core, y))

    @pl.when(moves)
    def _():
        signal(target(a, b, y, core))

    edges = jnp.where(a > 0, 1, 0) + jnp.where(a < LINE - 1, 1, 0) + jnp.where(moves, 1, 0)
    pl.semaphore_wait(barrier, 3 + edges)


class Gather:
    def __init__(self, src, dst, send, recv, local, first_tiles):
        self.src, self.dst, self.send, self.recv, self.local = src, dst, send, recv, local
        self.rows, self.width = src.shape
        tiles = self.width // LANES
        first = (first_tiles or tiles // 2) * LANES
        self.columns = [(0, first), (first, self.width - first)]
        self.a, self.b, self.core, self.y = place()

    def span(self, half):
        start, size = (0, self.width) if half is None else self.columns[half]
        return pl.ds(start, size)

    def at(self, piece, core=None):
        pa, pb, py, half = piece
        core = self.core if core is None else core
        row = pl.multiple_of(((pa * 2 + pb) * 2 + core) * self.rows, self.rows)
        return self.dst.at[py, pl.ds(row, self.rows), self.span(half)]

    def own_copy(self):
        return pltpu.make_async_copy(self.src, self.at((self.a, self.b, self.y, None)), self.local)

    def start(self, piece, slot, device, mine=False):
        source = self.src.at[:, self.span(piece[3])] if mine else self.at(piece)
        pltpu.make_async_remote_copy(
            source, self.at(piece), self.send.at[slot], self.recv.at[slot], device_id=device, device_id_type=MESH_ID
        ).start()

    def handle(self, piece, slot, core=None):
        ref = self.at(piece, core)
        return pltpu.make_async_remote_copy(
            ref,
            ref,
            self.send.at[slot],
            self.recv.at[slot],
            device_id=target(self.a, self.b, 1 - self.core, self.y),
            device_id_type=MESH_ID,
        )

    def arrived(self, piece, slot, core=None):
        self.handle(piece, slot, core).wait_recv()

    def sent(self, piece, slot):
        self.handle(piece, slot).wait_send()

    def to_x(self, piece, slot, mine=False):
        self.start(piece, slot, target(self.a, 1 - self.b, self.core, self.y), mine)

    def to_y(self, piece, slot, mine=False):
        self.start(piece, slot, target(self.a, self.b, self.core, 1 - self.y), mine)

    def to_mate(self, piece, slot, mine=False):
        self.start(piece, slot, target(self.a, self.b, 1 - self.core, self.y), mine)

    def to_line(self, piece, slot, step, mine=False):
        self.start(piece, slot, target(self.a + step, self.b, self.core, self.y), mine)

    def spread(self, pa, rank, mine=False):
        b, y = self.b, self.y
        self.to_x((pa, b, y, 0), 6 + rank, mine)
        self.to_y((pa, b, y, 1), 18 + rank, mine)
        for half in range(2):
            self.to_mate((pa, b, y, half), 30 + 2 * rank + half, mine)
        self.to_y((pa, b, y, 0), 22 + rank, mine)
        self.to_x((pa, b, y, 1), 10 + rank, mine)

    def begin(self):
        a, b, y = self.a, self.b, self.y
        piece = (a, b, y, None)

        @pl.when(a < LINE - 1)
        def _():
            self.to_line(piece, 0, 1, True)

        @pl.when(a > 0)
        def _():
            self.to_line(piece, 3, -1, True)

        self.spread(a, 0, True)
        self.own_copy().start()

    def hop(self, h):
        a, b, y = self.a, self.b, self.y

        @pl.when(a - h >= 0)
        def _():
            self.arrived((a - h, b, y, None), h - 1)
            if h < LINE - 1:

                @pl.when(a < LINE - 1)
                def _():
                    self.to_line((a - h, b, y, None), h, 1)

            self.spread(a - h, LINE - h)

        @pl.when(a + h < LINE)
        def _():
            self.arrived((a + h, b, y, None), 2 + h)
            if h < LINE - 1:

                @pl.when(a > 0)
                def _():
                    self.to_line((a + h, b, y, None), 3 + h, -1)

            self.spread(a + h, h)

    def ranks(self):
        return [(rank, lax.rem(self.a + rank, LINE)) for rank in range(LINE)]

    def turn(self):
        b, y = self.b, self.y
        for rank, pa in self.ranks():
            self.arrived((pa, 1 - b, y, 0), 6 + rank)
            self.to_y((pa, 1 - b, y, 0), 26 + rank)
            self.to_mate((pa, 1 - b, y, 0), 38 + rank)
            self.arrived((pa, b, 1 - y, 1), 18 + rank)
            self.to_x((pa, b, 1 - y, 1), 14 + rank)
            self.to_mate((pa, b, 1 - y, 1), 42 + rank)

    def last(self):
        b, y = self.b, self.y
        for rank, pa in self.ranks():
            for far in range(2):
                pb, py = (b, 1 - b)[far], (y, 1 - y)[far]
                self.arrived((pa, pb, 1 - y, 0), 22 + 4 * far + rank)
                self.to_mate((pa, pb, 1 - y, 0), 46 + 4 * far + rank)
                self.arrived((pa, 1 - b, py, 1), 10 + 4 * far + rank)
                self.to_mate((pa, 1 - b, py, 1), 54 + 4 * far + rank)

    def end(self):
        a, b, y = self.a, self.b, self.y
        other = 1 - self.core
        for rank, pa in self.ranks():
            pieces = [((pa, b, y, 0), 30 + 2 * rank), ((pa, b, y, 1), 31 + 2 * rank)]
            pieces += [((pa, 1 - b, y, 0), 38 + rank), ((pa, b, 1 - y, 1), 42 + rank)]
            for far in range(2):
                pb, py = (b, 1 - b)[far], (y, 1 - y)[far]
                pieces += [((pa, pb, 1 - y, 0), 46 + 4 * far + rank), ((pa, 1 - b, py, 1), 54 + 4 * far + rank)]
            for piece, slot in pieces:
                self.arrived(piece, slot, other)
                self.sent(piece, slot)
            self.sent((pa, b, y, 0), 6 + rank)
            self.sent((pa, b, y, 1), 18 + rank)
            self.sent((pa, b, y, 1), 10 + rank)
            self.sent((pa, b, 1 - y, 1), 14 + rank)
            self.sent((pa, b, y, 0), 22 + rank)
            self.sent((pa, 1 - b, y, 0), 26 + rank)

        @pl.when(a < LINE - 1)
        def _():
            self.sent((a, b, y, None), 0)

        @pl.when(a > 0)
        def _():
            self.sent((a, b, y, None), 3)

        for h in range(1, LINE - 1):

            @pl.when((a - h >= 0) & (a < LINE - 1))
            def _():
                self.sent((a - h, b, y, None), h)

            @pl.when((a + h < LINE) & (a > 0))
            def _():
                self.sent((a + h, b, y, None), 3 + h)

        self.own_copy().wait()


def front_kernel(
    attn_src,
    rows,
    ff_src,
    labels_ref,
    cos_ref,
    sin_ref,
    attn_w,
    rows_all,
    ff_w,
    qkv_ref,
    o_ref,
    o_in,
    lse_ref,
    attn_send,
    attn_recv,
    attn_local,
    ff_send,
    ff_recv,
    ff_local,
    row_send,
    row_recv,
    label_sems,
    o_send,
    o_recv,
    load_sems,
    held,
    labels_in,
    query_labels,
    key_labels,
    weights,
    x_ref,
    v_turned,
    state,
    acc,
):
    a, b, core, y = place()
    half = rows.shape[0]
    tokens = 2 * half
    part = half // ROW_PARTS
    moves = core != y
    turn = core * half
    greet(moves)
    labels_across = pltpu.make_async_remote_copy(
        labels_ref,
        labels_in,
        label_sems.at[0],
        label_sems.at[1],
        device_id=target(a, b, y, core),
        device_id_type=MESH_ID,
    )

    def crossing(k):
        span = pl.ds(k * part, part)
        return pltpu.make_async_remote_copy(
            rows.at[span],
            rows_all.at[span],
            row_send.at[0, k],
            row_recv.at[0, k],
            device_id=target(a, b, y, core),
            device_id_type=MESH_ID,
        )

    def to_mate(source, k):
        return pltpu.make_async_remote_copy(
            source.at[pl.ds(k * part, part)],
            rows_all.at[pl.ds(half + k * part, part)],
            row_send.at[1, k],
            row_recv.at[1, k],
            device_id=target(a, b, 1 - core, y),
            device_id_type=MESH_ID,
        )

    take = pltpu.make_async_copy(rows, held, row_recv.at[2, 0])
    stay = pltpu.make_async_copy(held, rows_all.at[pl.ds(0, half)], row_recv.at[2, 1])

    def send(k):
        @pl.when(moves)
        def _():
            crossing(k).start()

        @pl.when(jnp.logical_not(moves))
        def _():
            to_mate(rows, k).start()

    def hand_on(k):
        @pl.when(moves)
        def _():
            crossing(k).wait()
            to_mate(rows_all, k).start()

    @pl.when(moves)
    def _():
        labels_across.start()

    @pl.when(jnp.logical_not(moves))
    def _():
        take.start()

    gather = Gather(attn_src, attn_w, attn_send, attn_recv, attn_local, FIRST_TILES)
    later = Gather(ff_src, ff_w, ff_send, ff_recv, ff_local, None)
    gather.begin()
    send(0)

    @pl.when(jnp.logical_not(moves))
    def _():
        take.wait()
        stay.start()

    for h in range(1, LINE):
        gather.hop(h)
        send(h)
    later.begin()
    hand_on(0)
    hand_on(1)
    gather.turn()
    hand_on(2)
    hand_on(3)
    gather.last()

    @pl.when(jnp.logical_not(moves))
    def _():
        stay.wait()

    for k in range(ROW_PARTS):
        to_mate(rows_all, k).wait()
    gather.end()
    later.hop(1)
    load_w = pltpu.make_async_copy(attn_w.at[core], weights, load_sems.at[0])
    load_x = pltpu.make_async_copy(rows_all, x_ref, load_sems.at[1])
    load_w.start()
    load_x.start()

    @pl.when(moves)
    def _():
        labels_across.wait()

    labels = jnp.where(moves, labels_in[...], labels_ref[...])
    labels = jnp.where(core == 1, jnp.concatenate([labels[:, half:], labels[:, :half]], axis=1), labels)
    query_labels[...] = jnp.where(labels < 0, -2, labels)
    key_labels[...] = jnp.broadcast_to(labels, (LANES, tokens)).T
    load_w.wait()
    load_x.wait()
    pairs = weights.shape[1] // (3 * LANES)

    @pl.loop(0, tokens // ROW_BLOCK)
    def _(i):
        at = pl.ds(pl.multiple_of(i * ROW_BLOCK, ROW_BLOCK), ROW_BLOCK)
        table = pl.ds(pl.multiple_of(lax.rem(i * ROW_BLOCK + turn, tokens), ROW_BLOCK), ROW_BLOCK)
        x = x_ref[at, :]
        cos, sin = cos_ref[table, :], sin_ref[table, :]
        for pair in range(pairs):
            base = pair * 3 * LANES
            tile = dot(x, weights[:, base : base + 3 * LANES])
            for kind in range(2):
                span = slice(base + kind * LANES, base + (kind + 1) * LANES)
                flat = tile[:, kind * LANES : (kind + 1) * LANES]
                qkv_ref[at, span] = (flat * cos + half_swap(flat) * sin).astype(BF16)
            qkv_ref[at, base + 2 * LANES : base + 3 * LANES] = tile[:, 2 * LANES :].astype(BF16)

    later.hop(2)
    lane = lax.broadcasted_iota(jnp.int32, (1, LANES), 1)
    zero = jnp.zeros((), BF16)
    blocks = tokens // FWD_K

    def o_to_mate(pair):
        span = pl.ds(pl.multiple_of(pair * LANES, LANES), LANES)
        return pltpu.make_async_remote_copy(
            o_ref.at[pl.ds(half, half), span],
            o_in.at[:, span],
            o_send.at[pair],
            o_recv.at[pair],
            device_id=target(a, b, 1 - core, y),
            device_id_type=MESH_ID,
        )

    @pl.loop(0, pairs * blocks)
    def _(t):
        pair, j = t // blocks, lax.rem(t, blocks)

        def lanes(kind):
            return pl.ds(pl.multiple_of((pair * 3 + kind) * LANES, LANES), LANES)

        @pl.when(t == blocks)
        def _():
            later.hop(3)

        @pl.when(t == 2 * blocks)
        def _():
            later.turn()

        @pl.when(j == 0)
        def _():
            v_turned[...] = qkv_ref[:, lanes(2)].T
            for h in range(2):
                state[2 * h : 2 * h + 1, :] = jnp.full((1, tokens), MASKED, F32)
                state[2 * h + 1 : 2 * h + 2, :] = jnp.zeros((1, tokens), F32)
            acc[...] = jnp.zeros_like(acc)

        keys = pl.ds(pl.multiple_of(j * FWD_K, FWD_K), FWD_K)
        k = qkv_ref[keys, lanes(1)]
        q = qkv_ref[:, lanes(0)] * jnp.asarray(SCALE, BF16)
        same = key_labels[keys, :1] == query_labels[...]
        for h in range(2):
            feats = slice(h * HEAD_DIM, (h + 1) * HEAD_DIM)
            s = dot(k, jnp.where(lane // HEAD_DIM == h, q, zero), NT)
            s = jnp.where(same, s, -1e30)
            top, total = state[2 * h : 2 * h + 1, :], state[2 * h + 1 : 2 * h + 2, :]
            new_top = jnp.maximum(top, jnp.max(s, axis=0, keepdims=True))
            fade = jnp.exp(top - new_top)
            e = jnp.exp(s - new_top)
            state[2 * h : 2 * h + 1, :] = new_top
            state[2 * h + 1 : 2 * h + 2, :] = fade * total + jnp.sum(e, axis=0, keepdims=True)
            acc[feats, :] = acc[feats, :] * fade + dot(v_turned[feats, keys], e.astype(BF16))

        @pl.when(j == blocks - 1)
        def _():
            for h in range(2):
                feats = slice(h * HEAD_DIM, (h + 1) * HEAD_DIM)
                norm = jnp.maximum(state[2 * h + 1 : 2 * h + 2, :], 1.0)
                acc[feats, :] = acc[feats, :] / norm
                lse_ref[pair, pl.ds(h, 1), :] = state[2 * h : 2 * h + 1, :] + jnp.log(norm)
            o_ref[:, pl.ds(pl.multiple_of(pair * LANES, LANES), LANES)] = acc[...].T.astype(BF16)
            o_to_mate(pair).start()

    later.last()
    later.end()
    for pair in range(pairs):
        o_to_mate(pair).wait()


def front(attn_shard, rows, ff_shard, segments, cos, sin, devices, collective_id):
    shard, wide = attn_shard.shape
    half, width = rows.shape
    tokens, out_wide = 2 * half, wide // 3
    vmem, anywhere = pl.BlockSpec(memory_space=pltpu.VMEM), pl.BlockSpec(memory_space=pl.ANY)
    dma = pltpu.SemaphoreType.DMA
    return pl.pallas_call(
        front_kernel,
        in_specs=[anywhere, anywhere, anywhere, vmem, vmem, vmem],
        out_specs=[anywhere, anywhere, anywhere, vmem, vmem, anywhere, vmem],
        out_shape=[
            jax.ShapeDtypeStruct((2, devices // 2 * shard, wide), BF16),
            jax.ShapeDtypeStruct((tokens, width), BF16),
            jax.ShapeDtypeStruct((2, devices // 2 * shard, ff_shard.shape[1]), BF16),
            jax.ShapeDtypeStruct((tokens, wide), BF16),
            jax.ShapeDtypeStruct((tokens, out_wide), BF16),
            jax.ShapeDtypeStruct((half, out_wide), BF16),
            jax.ShapeDtypeStruct((out_wide // LANES, 2, tokens), F32),
        ],
        scratch_shapes=[
            dma((62,)),
            dma((62,)),
            dma,
            dma((62,)),
            dma((62,)),
            dma,
            dma((2, ROW_PARTS)),
            dma((3, ROW_PARTS)),
            dma((2,)),
            dma((out_wide // LANES,)),
            dma((out_wide // LANES,)),
            dma((2,)),
            pltpu.VMEM((half, width), BF16),
            pltpu.VMEM((1, tokens), jnp.int32),
            pltpu.VMEM((1, tokens), jnp.int32),
            pltpu.VMEM((tokens, LANES), jnp.int32),
            pltpu.VMEM((width, wide), BF16),
            pltpu.VMEM((tokens, width), BF16),
            pltpu.VMEM((LANES, tokens), BF16),
            pltpu.VMEM((8, tokens), F32),
            pltpu.VMEM((LANES, tokens), F32),
        ],
        compiler_params=pltpu.CompilerParams(
            collective_id=collective_id, has_side_effects=True, vmem_limit_bytes=VMEM_BYTES
        ),
        cost_estimate=pl.CostEstimate(
            flops=2 * tokens * width * wide + 8 * tokens * tokens * out_wide,
            bytes_accessed=40 * half * width,
            transcendentals=2 * out_wide // LANES * tokens * tokens,
        ),
        name="front",
    )(attn_shard, rows, ff_shard, segments.reshape(1, tokens), cos, sin)


def enter(shard, rows, cross, mate):
    weights = lax.all_gather(shard, ("mp", "chip", "core"), axis=0, tiled=True)
    own = cross(rows)
    return weights.reshape(2, -1, shard.shape[1]), jnp.concatenate([own, mate(own)], axis=0)


class Reduce:
    SPACING = 4
    OFFSETS = (1, 5, 9, 13)
    STEPS = OFFSETS[-1] + SPACING * (LINE - 1) + 1

    def __init__(self, src, out, scratch):
        self.src, self.out = src, out
        (
            self.acc,
            self.mates,
            self.y_two,
            self.x_two,
            self.x_one,
            self.y_one,
            self.up,
            self.down,
            self.load_sem,
            self.mate_send,
            self.mate_recv,
            self.y_send,
            self.y_recv,
            self.x_send,
            self.x_recv,
            self.up_send,
            self.up_recv,
            self.down_send,
            self.down_recv,
        ) = scratch
        self.rows, self.width = self.acc.shape[3:]
        self.first = self.y_two.shape[3]
        self.a, self.b, self.core, self.y = place()

    @staticmethod
    def scratch(rows, width, first):
        dma = pltpu.SemaphoreType.DMA
        return [
            pltpu.VMEM((LINE, 2, 2, rows, width), BF16),
            pltpu.VMEM((LINE, 2, 2, rows, width), BF16),
            pltpu.VMEM((LINE, 2, rows, first), BF16),
            pltpu.VMEM((LINE, 2, rows, width - first), BF16),
            pltpu.VMEM((LINE, rows, first), BF16),
            pltpu.VMEM((LINE, rows, width - first), BF16),
            pltpu.VMEM((LINE, rows, width), BF16),
            pltpu.VMEM((LINE, rows, width), BF16),
            dma((LINE, 2, 2)),
            dma((LINE, 2, 2)),
            dma((LINE, 2, 2)),
            dma((LINE, 3)),
            dma((LINE, 3)),
            dma((LINE, 3)),
            dma((LINE, 3)),
            dma((LINE,)),
            dma((LINE,)),
            dma((LINE,)),
            dma((LINE,)),
        ]

    def owner(self, group):
        near = jnp.where(self.a < LINE // 2, LINE - 1 - group, group)
        inner = [[3, 0, 2, 1], [0, 3, 1, 2]]
        pick = lambda order: sum(jnp.where(group == g, order[g], 0) for g in range(LINE))
        return jnp.where(self.a == 1, pick(inner[0]), jnp.where(self.a == 2, pick(inner[1]), near))

    def remote(self, src, dst, send, recv, device):
        return pltpu.make_async_remote_copy(src, dst, send, recv, device_id=device, device_id_type=MESH_ID)

    def source(self, group, pb, py, core):
        row = pl.multiple_of(((self.owner(group) * 2 + pb) * 2 + core) * self.rows, self.rows)
        return self.src.at[py, pl.ds(row, self.rows), :]

    def load(self, group, pb, py):
        return pltpu.make_async_copy(
            self.source(group, pb, py, self.core), self.acc.at[group, pb, py], self.load_sem.at[group, pb, py]
        )

    def to_mate(self, group, pb, py):
        return self.remote(
            self.source(group, pb, py, 1 - self.core),
            self.mates.at[group, pb, py],
            self.mate_send.at[group, pb, py],
            self.mate_recv.at[group, pb, py],
            target(self.a, self.b, 1 - self.core, self.y),
        )

    def low(self):
        return pl.ds(0, self.first)

    def high(self):
        return pl.ds(self.first, self.width - self.first)

    def over_y(self, group, k):
        device = target(self.a, self.b, self.core, 1 - self.y)
        if k < 2:
            src, dst = self.acc.at[group, k, 1 - self.y, :, self.low()], self.y_two.at[group, k]
        else:
            src, dst = self.acc.at[group, self.b, 1 - self.y, :, self.high()], self.y_one.at[group]
        return self.remote(src, dst, self.y_send.at[group, k], self.y_recv.at[group, k], device)

    def over_x(self, group, k):
        device = target(self.a, 1 - self.b, self.core, self.y)
        if k < 2:
            src, dst = self.acc.at[group, 1 - self.b, k, :, self.high()], self.x_two.at[group, k]
        else:
            src, dst = self.acc.at[group, 1 - self.b, self.y, :, self.low()], self.x_one.at[group]
        return self.remote(src, dst, self.x_send.at[group, k], self.x_recv.at[group, k], device)

    def along(self, group, step):
        pa = self.owner(group)
        src = self.acc.at[group, self.b, self.y]
        device = target(self.a + step, self.b, self.core, self.y)
        buffer, send, recv = (
            (self.up, self.up_send, self.up_recv) if step > 0 else (self.down, self.down_send, self.down_recv)
        )
        return self.remote(src, buffer.at[pa], send.at[pa], recv.at[pa], device)

    def add(self, ref, other):
        tile = 16

        @pl.loop(0, self.rows // tile)
        def _(i):
            span = pl.ds(pl.multiple_of(i * tile, tile), tile)
            ref[span, :] += other[span, :]

    def begin(self):
        for group in range(LINE):
            for pb in range(2):
                for py in range(2):
                    self.to_mate(group, pb, py).start()
                    self.load(group, pb, py).start()

    def first_stage(self, group):
        for pb in range(2):
            for py in range(2):
                self.load(group, pb, py).wait()
                self.to_mate(group, pb, py).wait_recv()
                self.add(self.acc.at[group, pb, py], self.mates.at[group, pb, py])
        for k in range(2):
            self.over_y(group, k).start()
            self.over_x(group, k).start()

    def second_stage(self, group):
        for k in range(2):
            self.over_y(group, k).wait_recv()
            self.add(self.acc.at[group, k, self.y, :, self.low()], self.y_two.at[group, k])
            self.over_x(group, k).wait_recv()
            self.add(self.acc.at[group, self.b, k, :, self.high()], self.x_two.at[group, k])
        self.over_x(group, 2).start()
        self.over_y(group, 2).start()

    def third_stage(self, group):
        mine = self.acc.at[group, self.b, self.y]
        self.over_x(group, 2).wait_recv()
        self.add(mine.at[:, self.low()], self.x_one.at[group])
        self.over_y(group, 2).wait_recv()
        self.add(mine.at[:, self.high()], self.y_one.at[group])
        pa = self.owner(group)

        @pl.when((self.a == 0) & (pa > 0))
        def _():
            self.along(group, 1).start()

        @pl.when((self.a == LINE - 1) & (pa < LINE - 1))
        def _():
            self.along(group, -1).start()

    def line_stage(self, group):
        mine = self.acc.at[group, self.b, self.y]
        pa = self.owner(group)

        @pl.when((self.a > 0) & (pa > self.a))
        def _():
            self.along(group, 1).wait_recv()
            self.add(mine, self.up.at[pa])
            self.along(group, 1).start()

        @pl.when((self.a < LINE - 1) & (pa < self.a))
        def _():
            self.along(group, -1).wait_recv()
            self.add(mine, self.down.at[pa])
            self.along(group, -1).start()

    def step(self, t):
        stages = (self.first_stage, self.second_stage, self.third_stage, self.line_stage)
        for stage, start in zip(stages, self.OFFSETS):
            passed = t - start

            @pl.when((passed >= 0) & (passed < self.SPACING * LINE) & (lax.rem(passed, self.SPACING) == 0))
            def _():
                stage(passed // self.SPACING)

    def end(self):
        last = LINE - 1
        mine = self.acc.at[last, self.b, self.y]

        @pl.when(self.a > 0)
        def _():
            self.along(last, 1).wait_recv()
            self.add(mine, self.up.at[self.a])

        @pl.when(self.a < LINE - 1)
        def _():
            self.along(last, -1).wait_recv()
            self.add(mine, self.down.at[self.a])

        self.out[...] = mine[...].astype(F32)
        for group in range(LINE):
            self.mates_sent(group)
            for k in range(3):
                self.over_y(group, k).wait_send()
                self.over_x(group, k).wait_send()
            pa = self.owner(group)

            @pl.when(pa > self.a)
            def _():
                self.along(group, 1).wait_send()

            @pl.when(pa < self.a)
            def _():
                self.along(group, -1).wait_send()


    def mates_sent(self, group):
        for pb in range(2):
            for py in range(2):
                self.to_mate(group, pb, py).wait_send()


class Place(Reduce):
    SPACING = 1
    OFFSETS = (0, 1, 2, 3)
    STEPS = OFFSETS[-1] + SPACING * (LINE - 1) + 1

    def load(self, group, pb):
        return pltpu.make_async_copy(
            self.source(group, pb, self.core), self.acc.at[group, pb, self.core], self.load_sem.at[group, pb, 0]
        )

    def source(self, group, pb, core):
        row = pl.multiple_of(((self.owner(group) * 2 + pb) * 2 + core) * self.rows, self.rows)
        return self.src.at[pl.ds(row, self.rows), :]

    def to_mate(self, group, pb, py):
        return self.remote(
            self.source(group, pb, 1 - self.core),
            self.acc.at[group, pb, py],
            self.mate_send.at[group, pb, 0],
            self.mate_recv.at[group, pb, 0],
            target(self.a, self.b, 1 - self.core, self.y),
        )

    def begin(self):
        for group in range(LINE):
            for pb in range(2):
                self.to_mate(group, pb, self.core).start()
                self.load(group, pb).start()

    def first_stage(self, group):
        for pb in range(2):
            self.load(group, pb).wait()
            self.to_mate(group, pb, 1 - self.core).wait_recv()
        for k in range(2):
            self.over_y(group, k).start()
            self.over_x(group, k).start()

    def mates_sent(self, group):
        for pb in range(2):
            self.to_mate(group, pb, self.core).wait_send()


def leave_kernel(
    back_ref,
    done_hbm,
    o_hbm,
    low_hbm,
    low_in_hbm,
    weights_hbm,
    grad_hbm,
    qkv_grad_ref,
    out_grad_ref,
    grad_ref,
    o_ref,
    low_ref,
    weights_ref,
    total,
    grads,
    mate_out,
    mate_in,
    cross_out,
    cross_in,
    load_sem,
    mate_send,
    mate_recv,
    cross_send,
    cross_recv,
    sums_ref,
    *scratch,
):
    a, b, core, y = place()
    moves = core != y
    half = total.shape[0]
    wide = back_ref.shape[1]
    loads = [
        pltpu.make_async_copy(done_hbm, grads.at[:, pl.ds(0, wide)], load_sem.at[6]),
        pltpu.make_async_copy(low_hbm, low_ref.at[pl.ds(0, half)], load_sem.at[0]),
        pltpu.make_async_copy(low_in_hbm, low_ref.at[pl.ds(half, half)], load_sem.at[1]),
        pltpu.make_async_copy(o_hbm, o_ref, load_sem.at[2]),
        pltpu.make_async_copy(weights_hbm.at[core], weights_ref, load_sem.at[3]),
        pltpu.make_async_copy(grad_hbm, total, load_sem.at[4]),
    ]
    for load in loads:
        load.start()
    greet(moves)
    reduce = Place(grads, sums_ref, scratch)
    for load in loads[:4]:
        load.wait()
    grads[:, wide:] = dot(low_ref[...], o_ref[...], TN).astype(BF16)
    reduce.begin()
    loads[4].wait()
    mate_out[...] = dot(back_ref[half:, :], weights_ref[...], NT).astype(BF16)
    exchange = reduce.remote(mate_out, mate_in, mate_send, mate_recv, target(a, b, 1 - core, y))
    exchange.start()
    loads[5].wait()
    total[...] += dot(back_ref[:half, :], weights_ref[...], NT)
    exchange.wait()
    total[...] += mate_in[...].astype(F32)
    part = half // LINE

    def crossing(k):
        span = pl.ds(pl.multiple_of(k * part, part), part)
        return reduce.remote(
            cross_out.at[span], cross_in.at[span], cross_send.at[k], cross_recv.at[k], target(a, b, y, core)
        )

    @pl.when(moves)
    def _():
        cross_out[...] = total[...].astype(BF16)

    @pl.loop(0, reduce.STEPS)
    def _(t):
        reduce.step(t)

        @pl.when(moves & (t >= 1) & (t <= LINE))
        def _():
            crossing(t - 1).start()

    @pl.when(moves)
    def _():
        for k in range(LINE):
            crossing(k).wait()
        grad_ref[...] = cross_in[...].astype(F32)

    @pl.when(jnp.logical_not(moves))
    def _():
        grad_ref[...] = total[...]

    reduce.end()
    for pair in range(wide // (3 * LANES)):
        for kind in range(3):
            start = (pair * 3 + kind) * LANES
            qkv_grad_ref[kind, :, pair * LANES : (pair + 1) * LANES] = sums_ref[:, start : start + LANES]
    out_grad_ref[...] = sums_ref[:, wide:]


def leave(back, done, o, low, low_in, weights, grad_one, collective_id):
    tokens, width = back.shape[0], grad_one.shape[1]
    half = tokens // 2
    wide, out_wide = back.shape[1], o.shape[1]
    rows = width // (4 * LINE)
    vmem, anywhere = pl.BlockSpec(memory_space=pltpu.VMEM), pl.BlockSpec(memory_space=pl.ANY)
    dma = pltpu.SemaphoreType.DMA
    return pl.pallas_call(
        leave_kernel,
        in_specs=[vmem] + [anywhere] * 6,
        out_specs=[vmem] * 3,
        out_shape=[
            jax.ShapeDtypeStruct((3, rows, wide // 3), F32),
            jax.ShapeDtypeStruct((rows, out_wide), F32),
            jax.ShapeDtypeStruct((half, width), F32),
        ],
        scratch_shapes=[
            pltpu.VMEM((tokens, out_wide), BF16),
            pltpu.VMEM((tokens, width), BF16),
            pltpu.VMEM((width, wide), BF16),
            pltpu.VMEM((half, width), F32),
            pltpu.VMEM((width, wide + out_wide), BF16),
            pltpu.VMEM((half, width), BF16),
            pltpu.VMEM((half, width), BF16),
            pltpu.VMEM((half, width), BF16),
            pltpu.VMEM((half, width), BF16),
            dma((7,)),
            dma,
            dma,
            dma((LINE,)),
            dma((LINE,)),
            pltpu.VMEM((rows, wide + out_wide), F32),
            *Reduce.scratch(rows, wide + out_wide, FIRST_TILES * LANES),
        ],
        compiler_params=pltpu.CompilerParams(
            collective_id=collective_id, has_side_effects=True, vmem_limit_bytes=VMEM_BYTES
        ),
        cost_estimate=pl.CostEstimate(
            flops=4 * tokens * width * (wide + out_wide), bytes_accessed=40 * half * width, transcendentals=0
        ),
        name="leave",
    )(back, done, o, low, low_in, weights, grad_one)


FF_ROWS = 256


def normalize(hidden):
    centered = hidden - jnp.mean(hidden, axis=-1, keepdims=True)
    inv_std = lax.rsqrt(jnp.mean(centered * centered, axis=-1, keepdims=True) + EPSILON)
    return centered * inv_std, inv_std


def normalize_back(grad_y, normed, inv_std, gain):
    scaled = grad_y * gain
    return inv_std * (
        scaled
        - jnp.mean(scaled, axis=-1, keepdims=True)
        - normed * jnp.mean(scaled * normed, axis=-1, keepdims=True)
    )


def feed_kernel(
    x_ref,
    o_ref,
    o_in_ref,
    out_ref,
    vectors_ref,
    d_ref,
    d_in_ref,
    weights_ref,
    y_ref,
    grad_ref,
    grad_low_ref,
    do_ref,
    do_mate_ref,
    sums_ref,
    weights,
    acts,
    turned,
    factor,
    silus,
    vectors,
    totals,
    sems,
    y_slots,
    y_send,
    y_recv,
    *,
    blocks,
    remote,
):
    step = pl.program_id(0)
    a, b, core, y = place()
    moves = core != y

    def at_home(k):
        span = pl.ds(pl.multiple_of(k * FF_ROWS, FF_ROWS), FF_ROWS)
        return pltpu.make_async_copy(y_slots.at[lax.rem(k, 2)], y_ref.at[span], y_send.at[lax.rem(k, 2)])

    def across(k):
        span = pl.ds(pl.multiple_of(k * FF_ROWS, FF_ROWS), FF_ROWS)
        return pltpu.make_async_remote_copy(
            y_slots.at[lax.rem(k, 2)],
            y_ref.at[span],
            y_send.at[lax.rem(k, 2)],
            y_recv.at[k],
            device_id=target(a, b, y, core),
            device_id_type=MESH_ID,
        )

    def each(k, move, stay):
        if remote:

            @pl.when(moves)
            def _():
                move(across(k))

            @pl.when(jnp.logical_not(moves))
            def _():
                stay(at_home(k))
        else:
            stay(at_home(k))

    if remote:

        @pl.when((step == 0) & moves)
        def _():
            barrier = pltpu.get_barrier_semaphore()
            pl.semaphore_signal(barrier, inc=1, device_id=target(a, b, y, core), device_id_type=MESH_ID)
            pl.semaphore_wait(barrier, 1)

    half_ff = weights.shape[2] // 3

    def fetch(half, kind):
        columns = pl.ds(kind * half_ff, half_ff)
        return pltpu.make_async_copy(
            weights_ref.at[half, :, columns], weights.at[half, :, columns], sems.at[half, kind]
        )

    @pl.when(step == 0)
    def _():
        for half in range(2):
            for kind in range(3):
                fetch(half, kind).start()
        vectors[...] = vectors_ref[0].astype(F32).T[:8]
        totals[...] = jnp.zeros_like(totals)

    @pl.when(step < blocks)
    def _():
        def weight(half, kind):
            return weights[half, :, kind * half_ff : (kind + 1) * half_ff]

        def ready(half, kinds):
            @pl.when(step == 0)
            def _():
                for kind in kinds:
                    fetch(half, kind).wait()

        rows = pl.ds(pl.multiple_of(step * FF_ROWS, FF_ROWS), FF_ROWS)
        gain_one, bias_one, gain_two, bias_two = (vectors[k : k + 1, :] for k in range(4))
        attn = dot(o_ref[...], out_ref[core], NT) + dot(o_in_ref[...], out_ref[1 - core], NT)
        first_hat, first_inv = normalize(x_ref[...].astype(F32) + attn)
        middle = first_hat * gain_one + bias_one
        middle_low = middle.astype(BF16)
        turned[0, :, rows] = middle_low.T
        mlp = middle
        for half in range(2):
            columns = slice(half * half_ff, (half + 1) * half_ff)
            ready(half, (0, 1))
            gate = dot(middle_low, weight(half, 0))
            up = dot(middle_low, weight(half, 1))
            sig = jax.nn.sigmoid(gate)
            silu = gate * sig
            hidden = (silu * up).astype(BF16)
            acts[2, rows, columns] = hidden
            silus[:, columns] = silu
            factor[:, columns] = up * sig * (1.0 + gate * (1.0 - sig))
            ready(half, (2,))
            mlp = mlp + dot(hidden, weight(half, 2), NT)
        second_hat, second_inv = normalize(mlp)

        @pl.when(step >= 2)
        def _():
            each(step - 2, lambda copy: copy.wait_send(), lambda copy: copy.wait())

        y_slots[lax.rem(step, 2)] = (second_hat * gain_two + bias_two).astype(BF16)
        each(step, lambda copy: copy.start(), lambda copy: copy.start())
        d = jnp.where(moves, d_in_ref[...], d_ref[...]).astype(F32)
        grad_two = normalize_back(d, second_hat, second_inv, gain_two)
        totals[2:3, :] += jnp.sum(d * second_hat, axis=0, keepdims=True)
        totals[3:4, :] += jnp.sum(d, axis=0, keepdims=True)
        grad_low = grad_two.astype(BF16)
        turned[1, :, rows] = grad_low.T
        grad_middle = grad_two
        for half in range(2):
            columns = slice(half * half_ff, (half + 1) * half_ff)
            grad_hidden = dot(grad_low, weight(half, 2))
            grad_gate = (grad_hidden * factor[:, columns]).astype(BF16)
            grad_up = (grad_hidden * silus[:, columns]).astype(BF16)
            acts[0, rows, columns] = grad_gate
            acts[1, rows, columns] = grad_up
            grad_middle = grad_middle + dot(grad_gate, weight(half, 0), NT) + dot(grad_up, weight(half, 1), NT)
        totals[0:1, :] += jnp.sum(grad_middle * first_hat, axis=0, keepdims=True)
        totals[1:2, :] += jnp.sum(grad_middle, axis=0, keepdims=True)
        grad_one = normalize_back(grad_middle, first_hat, first_inv, gain_one)
        grad_ref[...] = grad_one
        first_low = grad_one.astype(BF16)
        grad_low_ref[...] = first_low
        do_ref[...] = dot(first_low, out_ref[core]).astype(BF16)
        do_mate_ref[...] = dot(first_low, out_ref[1 - core]).astype(BF16)

    @pl.when(step == blocks + 13)
    def _():
        for k in (blocks - 2, blocks - 1):
            each(jnp.int32(k), lambda copy: copy.wait_send(), lambda copy: copy.wait())
        if remote:

            @pl.when(moves)
            def _():
                for k in range(blocks):
                    across(jnp.int32(k)).wait_recv()

    cut = half_ff // 2
    index = jnp.maximum(step - blocks, 0)
    half, place_in = index // 7, lax.rem(index, 7)

    @pl.when((step >= blocks) & (place_in < 6))
    def _():
        kind = place_in // 2
        start = pl.multiple_of(half * half_ff + lax.rem(place_in, 2) * cut, cut)
        sums_ref[0] = dot(turned[kind // 2], acts[kind, :, pl.ds(start, cut)]).astype(BF16)

    @pl.when((step >= blocks) & (place_in == 6))
    def _():
        sums_ref[0, :, :LANES] = totals[...].T.astype(BF16)


def feed(rows_all, o, o_in, ff_w, d_out, d_in, devices, collective_id):
    half_len, width = d_out.shape
    half_cols = o.shape[1]
    half_ff = 4 * half_cols
    blocks = half_len // FF_ROWS
    token = lambda columns: pl.BlockSpec((FF_ROWS, columns), lambda i: (jnp.minimum(i, blocks - 1), 0))

    params = dict(vmem_limit_bytes=FEED_VMEM)
    if devices == 8 * LINE:
        params.update(collective_id=collective_id, has_side_effects=True)

    def place_sums(i):
        k = jnp.maximum(i - blocks, 0)
        return (k // 7, 0, lax.rem(k, 7))

    return pl.pallas_call(
        functools.partial(feed_kernel, blocks=blocks, remote=devices == 8 * LINE),
        grid_spec=pltpu.PrefetchScalarGridSpec(
            num_scalar_prefetch=0,
            grid=(blocks + 14,),
            in_specs=[
                token(width),
                token(half_cols),
                token(half_cols),
                pl.BlockSpec((2, width, half_cols), lambda i: (0, 0, 12)),
                pl.BlockSpec((1, width, LANES), lambda i: (0, 0, 13 * half_cols // LANES)),
                token(width),
                token(width),
                pl.BlockSpec(memory_space=pl.ANY),
            ],
            out_specs=[
                pl.BlockSpec(memory_space=pl.ANY),
                token(width),
                token(width),
                token(half_cols),
                token(half_cols),
                pl.BlockSpec((1, width, half_ff // 2), place_sums),
            ],
            scratch_shapes=[
                pltpu.VMEM((2, width, 3 * half_ff), BF16),
                pltpu.VMEM((3, half_len, 2 * half_ff), BF16),
                pltpu.VMEM((2, width, half_len), BF16),
                pltpu.VMEM((FF_ROWS, 2 * half_ff), F32),
                pltpu.VMEM((FF_ROWS, 2 * half_ff), F32),
                pltpu.VMEM((8, width), F32),
                pltpu.VMEM((LANES, width), F32),
                pltpu.SemaphoreType.DMA((2, 3)),
                pltpu.VMEM((2, FF_ROWS, width), BF16),
                pltpu.SemaphoreType.DMA((2,)),
                pltpu.SemaphoreType.DMA((blocks,)),
            ],
        ),
        out_shape=[
            jax.ShapeDtypeStruct((half_len, width), BF16),
            jax.ShapeDtypeStruct((half_len, width), F32),
            jax.ShapeDtypeStruct((half_len, width), BF16),
            jax.ShapeDtypeStruct((half_len, half_cols), BF16),
            jax.ShapeDtypeStruct((half_len, half_cols), BF16),
            jax.ShapeDtypeStruct((2, width, 3 * half_ff + LANES), BF16),
        ],
        compiler_params=pltpu.CompilerParams(**params),
        cost_estimate=pl.CostEstimate(
            flops=half_len * width * (2 * 2 * width + 6 * 6 * half_ff),
            bytes_accessed=4 * ff_w.size + 20 * half_len * width,
            transcendentals=2 * half_len * half_ff,
        ),
        name="feed",
    )(rows_all, o, o_in, ff_w, ff_w, d_out, d_in, ff_w)


def on_device(
    mp,
    devices,
    inputs,
    segments,
    w_qkv,
    w_out,
    first_gain,
    first_bias,
    w_gate,
    w_up,
    w_down,
    second_gain,
    second_bias,
    d_out,
):
    group = ("chip", "mp")
    swaps = [(a * mp + b, b * mp + a) for a in range(2) for b in range(mp) if a != b]

    core, y = lax.axis_index("core"), lax.axis_index("mp")
    moves = core != y

    def cross_in(tensor):
        return lax.ppermute(tensor, ("core", "mp"), swaps)

    def cross(tensor):
        return jnp.where(moves, cross_in(tensor), tensor)

    def mate(tensor):
        return lax.ppermute(tensor, "core", [(0, 1), (1, 0)])

    shard, half_cols = w_qkv.shape[1], w_qkv.shape[2]
    pairs = half_cols // LANES
    half_ff = w_gate.shape[1]
    half_len, width = inputs.shape
    turn = core * half_len

    attn_shard = w_qkv.reshape(3, shard, pairs, LANES).transpose(1, 2, 0, 3).reshape(shard, 3 * half_cols)
    vectors = jnp.stack([first_gain, first_bias, second_gain, second_bias]).T
    pad = jnp.zeros((shard, LANES - 4), BF16)
    ff_shard = jnp.concatenate([w_gate, w_up, w_down.T, w_out.T, vectors, pad], axis=1)
    labels = cross(segments)
    labels = jnp.where(core == 0, labels, jnp.roll(labels, half_len))
    d_in = cross_in(d_out)
    cos, sin = (jnp.asarray(t) for t in rope_tables())
    place_id = jnp.stack([core, moves.astype(jnp.int32)])
    if devices == 8 * LINE:
        attn_w, rows_all, ff_w, qkv, o, o_in, lse = front(
            attn_shard, inputs, ff_shard, segments, cos, sin, devices, 1
        )
    else:
        attn_w, rows_all = enter(attn_shard, inputs, cross, mate)
        ff_w = lax.all_gather(ff_shard, ("mp", "chip", "core"), axis=0, tiled=True).reshape(2, width, -1)
        qkv = project(place_id, rows_all, attn_w, cos, sin)
        o, lse = attend(qkv, labels, turn)
        o_in = mate(o[half_len:])
    outputs, grad_one, grad_one_low, do, do_mate, ff_sum = feed(rows_all, o, o_in, ff_w, d_out, d_in, devices, 4)
    do_in = mate(do_mate)
    grad_low_in = mate(grad_one_low)
    back, weight_grad, ff_grad = attend_back(
        qkv, o, do, do_in, lse, labels, cos, sin, rows_all, ff_sum, devices, 2
    )
    if devices == 8 * LINE:
        grad_qkv, grad_out, grad_inputs = leave(
            back, weight_grad, o, grad_one_low, grad_low_in, attn_w, grad_one, 3
        )
    else:
        grad_out_t = dot(jnp.concatenate([grad_one_low, grad_low_in]), o, TN).astype(BF16)
        attn_sum = jnp.concatenate([weight_grad, grad_out_t], axis=1)
        attn_sum = jnp.where(jnp.arange(2)[:, None, None] == core, attn_sum[None], 0)
        attn_grad = scatter_sum(attn_sum)
        grad_qkv = (
            attn_grad[:, : 3 * half_cols]
            .reshape(shard, pairs, 3, LANES)
            .transpose(2, 0, 1, 3)
            .reshape(3, shard, half_cols)
        )
        grad_out = attn_grad[:, 3 * half_cols :]
        grad_rows = dot(back, lax.dynamic_index_in_dim(attn_w, core, 0, False), NT)
        grad_rows = grad_rows[:half_len] + mate(grad_rows[half_len:].astype(BF16)).astype(F32)
        grad_inputs = grad_one + grad_rows
        grad_inputs = jnp.where(moves, cross_in(grad_inputs.astype(BF16)).astype(F32), grad_inputs)
        outputs = cross(outputs)

    grad_gate, grad_up, grad_down_t = (ff_grad[:, k * half_ff : (k + 1) * half_ff] for k in range(3))
    grad_vectors = ff_grad[:, 3 * half_ff : 3 * half_ff + 4]
    return (
        outputs,
        grad_inputs,
        grad_qkv,
        grad_out.T,
        grad_vectors[:, 0],
        grad_vectors[:, 1],
        grad_gate,
        grad_up,
        grad_down_t.T,
        grad_vectors[:, 2],
        grad_vectors[:, 3],
    )


def solution(mesh):
    dp, mp = mesh.shape["dp"], mesh.shape["mp"]
    split = Mesh(mesh.devices.reshape(dp // 2, 2, mp), ("chip", "core", "mp"))
    rows = P(("chip", "core", "mp"), None)
    vector = P(("chip", "core"))
    columns = P(("chip", "core"), "mp")
    turned = P("mp", ("chip", "core"))
    stacked = P(None, ("chip", "core"), "mp")
    return jax.shard_map(
        functools.partial(on_device, mp, dp * mp),
        mesh=split,
        in_specs=(
            rows,
            vector,
            stacked,
            turned,
            vector,
            vector,
            columns,
            columns,
            turned,
            vector,
            vector,
            rows,
        ),
        out_specs=(
            rows,
            rows,
            stacked,
            turned,
            vector,
            vector,
            columns,
            columns,
            turned,
            vector,
            vector,
        ),
        check_vma=False,
    )
```
